128 devices in a mesh: dp: 2 (over x_lo), tile: 64 (over y, x_hi, z, core).
Axes of the slice: x: 4 (x_hi: 2, x_lo: 2; x = x_hi * 2 + x_lo), y: 4, z: 4, core: 2. Of those that a mesh axis runs over, the one named last changes fastest.
Arguments:
- grad_out: bfloat16 [2, 256, 640, 512], P('dp', 'tile'), may hold values from -6 to 6
- bev_act: bfloat16 [2, 256, 640, 512], P('dp', 'tile'), may hold values from -16 to 16
- conv_weight: bfloat16 [512, 3, 3, 512], replicated, may hold values from -0.09375 to 0.09375
- img_in: bfloat16 [2, 32768, 512], P('dp', 'tile'), may hold values from -16 to 16
- backbone_weight: bfloat16 [512, 512], replicated, may hold values from -0.25 to 0.25
- route: int32 [2, 2560], P('dp'), may hold values from 0 to 255, as said below
- offsets: int32 [2, 163840], P('dp', 'tile'), may hold values from 0 to 62
- frac_x: int32 [2, 163840], P('dp', 'tile'), may hold values from 0 to 255
- frac_y: int32 [2, 163840], P('dp', 'tile'), may hold values from 0 to 255
Outputs:
- image_grad: bfloat16 [2, 32768, 512], P('dp', 'tile')
- conv_grad: bfloat16 [512, 3, 3, 512], replicated
- backbone_grad: bfloat16 [512, 512], replicated
The draws below stay inside these ranges and needn't reach their ends.
Inputs may be any that keep to these rules, and one draw needn't show every extreme that they name: `route`: owner of image block id is id // 4. Among the 40 ground blocks k * 40 to k * 40 + 39 of one sample, at most 2 have sources with one owner; in every sample some owner has exactly 2 such blocks from every device.
All inputs are finite; a program needn't handle non-finite values.
Results may differ from the reference program's by a relative error of at most 0.0073.
Values may be sent and summed in bfloat16 or wider, within the bound.
A program may use at most 192 MiB of HBM per device.

```python
import math
import jax
import jax.numpy as jnp
from jax import lax

C = 512
BW = 640
IB = 4
BLK = 64
IMGW = 64
BATCH = 2
NBR = 256
NB = 40
TOTB = 2560
CAP = 2
IMGB = 256
PIX = 32768
CELLS = 327680
PIXELS = 65536
N_TILE = 64


def draw_route(key, part):
    slot_total = N_TILE * CAP

    def one_sample(sample_key):
        favored = jax.random.randint(jax.random.fold_in(sample_key, 7), (), 0, N_TILE)

        def one_device(device_key):
            perm = jax.random.permutation(jax.random.fold_in(device_key, 1), slot_total)
            owner = perm // CAP
            edge = (perm == 0) | (perm == (N_TILE - 1) * CAP)
            score = jnp.where(owner == favored, 0, jnp.where(edge, 1, 2)).astype(jnp.int32)
            order = jnp.argsort(score, stable=True)
            chosen = perm[order][:NB]
            local = jax.random.randint(jax.random.fold_in(device_key, 3), (NB,), 0, IB)
            local = jnp.where(chosen == 0, 0, jnp.where(chosen == (N_TILE - 1) * CAP, IB - 1, local))
            ids = (chosen // CAP * IB + local).astype(jnp.int32)
            return jax.random.permutation(jax.random.fold_in(device_key, 5), ids)
        device_keys = jax.random.split(jax.random.fold_in(sample_key, 11), N_TILE)
        return jax.vmap(one_device)(device_keys).reshape(-1)
    sample_keys = jax.random.split(jax.random.fold_in(key, 13), BATCH)
    return jax.vmap(one_sample)(sample_keys).astype(jnp.int32)


def place_ends(drawn, own_key, least, largest):
    longest = drawn.shape.index(max(drawn.shape))
    spots = []
    for shift in (0, 1):
        where = [jax.random.randint(jax.random.fold_in(own_key, axis), (), 0, length) for axis, length in enumerate(drawn.shape)]
        where[longest] = (where[longest] + shift) % drawn.shape[longest]
        spots.append(tuple(where))
    return drawn.at[spots[0]].set(least).at[spots[1]].set(largest)


def with_spikes(values, rng, source, target, parts, factor):
    def block_of(axis_at):
        return (jnp.arange(values.shape[axis_at]) // (values.shape[axis_at] // parts)).reshape((-1,) + (1,) * (values.ndim - 1 - axis_at))

    first = jax.random.permutation(rng, parts)[block_of(target)]
    far = (block_of(target) + parts // 2) % parts
    return jnp.where((block_of(source) == first) | (block_of(source) == far), factor * values, values)


def shard_levels(stream_key, extent, shards, least, largest):
    def one(dim, shards_of):
        steps = jax.random.uniform(jax.random.fold_in(jax.random.fold_in(stream_key, 6), dim), (shards_of,), jnp.float32, least / len(shards), largest / len(shards))
        return jnp.repeat(jnp.exp(steps), extent[dim] // shards_of).reshape((-1,) + (1,) * (len(extent) - dim - 1))

    gain = one(*shards[0])
    for cut in shards[1:]:
        gain = gain * one(*cut)
    return gain


def normal_values(stream_key, shape, scale, reach, shards=(), kind=jnp.bfloat16):
    entries = jax.random.normal(stream_key, shape, jnp.float32) * scale
    if len(shards) > 0:
        entries = shard_levels(stream_key, shape, shards, -0.22, 0.18) * entries
    return jnp.clip(entries, min=-reach, max=reach).astype(kind)


def noise_with(stream_key, dims, deviation, reach, cuts, heavy, kind=jnp.bfloat16):
    drawn = deviation * jax.random.normal(stream_key, dims, jnp.float32)
    if cuts:
        drawn = drawn * shard_levels(stream_key, dims, cuts, -0.22, 0.18)
    return jnp.clip(with_spikes(drawn, jax.random.fold_in(stream_key, 3), *heavy), -reach, reach).astype(kind)


def setup_inputs(seed: int = 0) -> dict:
    key_list = jax.random.split(jax.random.key(seed), 10)
    return {
        "grad_out": normal_values(key_list[0], (BATCH, NBR, BW, C), 1.0, 6.0, ((0, 2), (1, 64))),
        "bev_act": noise_with(key_list[1], (BATCH, NBR, BW, C), 1.0, 16.0, ((0, 2), (1, 64)), (1, 3, 64, 4.0)),
        "conv_weight": normal_values(key_list[2], (C, 3, 3, C), (9 * C) ** -0.5, 0.09375),
        "img_in": noise_with(key_list[3], (BATCH, PIX, C), 1.0, 16.0, ((0, 2), (1, 64)), (1, 2, 64, 4.0)),
        "backbone_weight": normal_values(key_list[4], (C, C), C ** -0.5, 0.25),
        "route": draw_route(jax.random.fold_in(key_list[9], 71), 0),
        "offsets": place_ends(jax.random.randint(key_list[6], (BATCH, NBR * BW), 0, IMGW - 1), jax.random.fold_in(key_list[6], 1), 0, (IMGW - 1) - 1).astype(jnp.int32),
        "frac_x": place_ends(jax.random.randint(key_list[7], (BATCH, NBR * BW), 0, 256), jax.random.fold_in(key_list[7], 1), 0, 255).astype(jnp.int32),
        "frac_y": place_ends(jax.random.randint(key_list[8], (BATCH, NBR * BW), 0, 256), jax.random.fold_in(key_list[8], 1), 0, 255).astype(jnp.int32),
    }


def make_band(offsets, frac_x, frac_y, blocks, width):
    columns = lax.broadcasted_iota(jnp.int32, (1, 1, width), 2)
    shaped = offsets.reshape(blocks, -1, 1)
    right_w = frac_x.reshape(blocks, -1, 1).astype(jnp.float32) / 256.0
    lower_w = frac_y.reshape(blocks, -1, 1).astype(jnp.float32) / 256.0
    across = jnp.where(columns == shaped, 1.0 - right_w, 0.0) + jnp.where(columns == shaped + 1, right_w, 0.0)
    return jnp.concatenate([(1.0 - lower_w) * across, lower_w * across], axis=2).astype(jnp.bfloat16)

def silu_slope(value):
    sigma = jax.nn.sigmoid(value)
    return sigma * (1.0 + value * (1.0 - sigma))

def reference(grad_out, bev_act, conv_weight, img_in, backbone_weight, route, offsets, frac_x, frac_y):
    conv_total = jnp.zeros((C, 3, 3, C), jnp.float32)
    backbone_total = jnp.zeros((C, C), jnp.float32)
    images = []
    for sample in range(BATCH):
        pad_spec = ((1, 1), (1, 1), (0, 0))
        out_frame = jnp.pad(grad_out[sample], pad_spec)
        act_frame = jnp.pad(bev_act[sample], pad_spec)
        center = grad_out[sample].reshape(-1, C)
        bev_sum = jnp.zeros((NBR * BW, C), jnp.float32)
        for row_tap in range(3):
            for col_tap in range(3):
                shifted = out_frame[2 - row_tap:2 - row_tap + NBR, 2 - col_tap:2 - col_tap + BW].reshape(-1, C)
                bev_sum = bev_sum + jnp.dot(shifted, conv_weight[:, row_tap, col_tap, :].T, preferred_element_type=jnp.float32)
                moved = act_frame[row_tap:row_tap + NBR, col_tap:col_tap + BW].reshape(-1, C)
                term = jnp.dot(moved.T, center, preferred_element_type=jnp.float32)
                conv_total = conv_total.at[:, row_tap, col_tap, :].add(term)
        bev_grad = bev_sum.astype(jnp.bfloat16)
        blocks = bev_grad.reshape(TOTB, BLK, C)
        band = make_band(offsets[sample], frac_x[sample], frac_y[sample], TOTB, IMGW)
        pieces = jnp.einsum('kmp,kmc->kpc', band.astype(jnp.float32), blocks.astype(jnp.float32)).astype(jnp.bfloat16)
        feature_grad = jax.ops.segment_sum(pieces.astype(jnp.float32), route[sample], num_segments=IMGB).reshape(PIX, C)
        image = img_in[sample]
        pre = jnp.dot(image, backbone_weight, preferred_element_type=jnp.float32)
        scaled = (feature_grad * silu_slope(pre)).astype(jnp.bfloat16)
        images.append(jnp.dot(scaled, backbone_weight.T, preferred_element_type=jnp.float32).astype(jnp.bfloat16))
        backbone_total = backbone_total + jnp.dot(image.T, scaled, preferred_element_type=jnp.float32)
    conv_grad = (conv_total * (1.0 / math.sqrt(CELLS))).astype(jnp.bfloat16)
    backbone_grad = (backbone_total * (1.0 / math.sqrt(PIXELS))).astype(jnp.bfloat16)
    return (jnp.stack(images), conv_grad, backbone_grad)
```

```python
import functools
import math

import jax
import jax.numpy as jnp
from jax import lax
from jax.experimental import pallas as pl
from jax.experimental.pallas import tpu as pltpu
from jax.sharding import PartitionSpec as P

BLK = 64
IMGW = 64
PIXB = 2 * IMGW
TILES = 64
CAP = 2
MESH = pl.DeviceIdType.MESH
ANY = pl.BlockSpec(memory_space=pl.ANY)
VMEM = pl.BlockSpec(memory_space=pltpu.VMEM)
SMEM = pl.BlockSpec(memory_space=pltpu.SMEM)
BF = jnp.bfloat16
F32 = jnp.float32


def coords():
    t = lax.axis_index("tile")
    return t // 16, (t // 8) % 2 * 2 + lax.axis_index("dp"), (t // 2) % 4, t % 2


def device(y, x, z, core):
    return (x % 2, ((y * 2 + x // 2) * 4 + z) * 2 + core)


def along(axis, step):
    y, x, z, core = coords()
    if axis == "y":
        y = (y + step) % 4
    elif axis == "x":
        x = (x + step) % 4
    elif axis == "z":
        z = (z + step) % 4
    else:
        core = 1 - core
    return device(y, x, z, core)


def bev_kernel(idx_ref, g_ref, lo_ref, hi_ref, w_ref, s_ref, frame, w, acc, bev, sems, out_sem):
    rows, cols = g_ref.shape[0], g_ref.shape[1]
    copies = [
        pltpu.make_async_copy(w_ref, w, sems.at[0]),
        pltpu.make_async_copy(g_ref, frame.at[pl.ds(1, rows)], sems.at[1]),
        pltpu.make_async_copy(lo_ref, frame.at[0], sems.at[2]),
        pltpu.make_async_copy(hi_ref, frame.at[rows + 1], sems.at[3]),
    ]
    for copy in copies:
        copy.start()
    for copy in copies:
        copy.wait()
    half = 256

    def step(s, carry):
        r, n = s // 2, s % 2
        lanes = pl.ds(pl.multiple_of(n * half, half), half)

        def tap(j):
            total = None
            for i in range(3):
                term = lax.dot_general(
                    frame[r + 2 - i],
                    w[i * 3 + j, lanes, :],
                    (((1,), (1,)), ((), ())),
                    preferred_element_type=F32,
                )
                total = term if total is None else total + term
            return total

        acc[pl.ds(8, cols), :] = tap(1)
        acc[pl.ds(7, cols), :] += tap(0)
        acc[pl.ds(9, cols), :] += tap(2)
        bev[pl.ds(pl.multiple_of(r * cols, cols), cols), lanes] = acc[pl.ds(8, cols), :].astype(BF)
        return carry

    lax.fori_loop(0, 2 * rows, step, 0)

    def send(s, carry):
        start = pl.multiple_of(idx_ref[s] * BLK, BLK)
        pltpu.make_async_copy(bev.at[pl.ds(start, BLK)], s_ref.at[s], out_sem).start()
        return carry

    lax.fori_loop(0, TILES * CAP, send, 0)
    pltpu.make_async_copy(s_ref, s_ref, out_sem).wait()


def bev_slots(idx, g, lo, hi, w):
    rows, cols, chans = g.shape
    return pl.pallas_call(
        bev_kernel,
        out_shape=jax.ShapeDtypeStruct((TILES * CAP, BLK, chans), BF),
        in_specs=[SMEM, ANY, ANY, ANY, ANY],
        out_specs=ANY,
        scratch_shapes=[
            pltpu.VMEM((rows + 2, cols, chans), BF),
            pltpu.VMEM(w.shape, BF),
            pltpu.VMEM((cols + 16, 256), F32),
            pltpu.VMEM((rows * cols, chans), BF),
            pltpu.SemaphoreType.DMA((4,)),
            pltpu.SemaphoreType.DMA,
        ],
        compiler_params=pltpu.CompilerParams(vmem_limit_bytes=40 << 20),
        cost_estimate=pl.CostEstimate(
            flops=2 * 9 * rows * cols * chans * chans, bytes_accessed=24 << 20, transcendentals=0
        ),
        name="bev_slots",
    )(idx, g, lo, hi, w)


ORDERS = (("y", "z", "x"), ("z", "x", "y"), ("x", "y", "z"))
BATCHES = 8


def exchange_kernel(
    scale, s_ref, m_ref, w_ref, r_ref, rm_ref, o_ref,
    recv0, acc0, recv1, acc1, recv2, acc2, recv3,
    slot_send, slot_recv, meta_send, meta_recv, own_sem, pair_send, pair_recv, st_send, st_recv,
):
    y, x, z, core = coords()
    dp = lax.axis_index("dp")
    tile = lax.axis_index("tile")
    place = {"y": y, "x": x, "z": z}

    barrier = pltpu.get_barrier_semaphore()

    def greet(n, carry):
        pl.semaphore_signal(
            barrier, inc=1, device_id=(dp, (tile + n) % TILES), device_id_type=MESH
        )
        return carry

    lax.fori_loop(1, TILES, greet, 0)
    for step in (1, 3):
        pl.semaphore_signal(barrier, inc=1, device_id=along("x", step), device_id_type=MESH)
    pl.semaphore_wait(barrier, TILES + 1)

    def shifted(b, e, sign):
        dc, h, g = b // 4, (b // 2) % 2, b % 2
        dy = e % 4
        dz = (dy + 2 * (e // 4) + h) % 4
        dx = (g + e) % 2
        x_hi = x // 2
        return (
            (((y + 4 + sign * dy) % 4 * 2 + (x_hi + dx) % 2) * 4 + (z + 4 + sign * dz) % 4) * 2
            + (core + dc) % 2
        )

    def slot_copy(b, e):
        peer = shifted(b, e, 1)
        n = b * 8 + e
        return pltpu.make_async_remote_copy(
            src_ref=s_ref.at[peer], dst_ref=r_ref.at[tile],
            send_sem=slot_send.at[n], recv_sem=slot_recv.at[n],
            device_id=(dp, peer), device_id_type=MESH,
        )

    def meta_copy(b, e):
        peer = shifted(b, e, 1)
        n = b * 8 + e
        return pltpu.make_async_remote_copy(
            src_ref=m_ref.at[peer], dst_ref=rm_ref.at[tile],
            send_sem=meta_send.at[n], recv_sem=meta_recv.at[n],
            device_id=(dp, peer), device_id_type=MESH,
        )

    def issue(b):
        def one(e, carry):
            slot_copy(b, e).start()
            meta_copy(b, e).start()
            return carry

        lax.fori_loop(1 if b == 0 else 0, 8, one, 0)

    own = [
        pltpu.make_async_copy(s_ref.at[tile], r_ref.at[tile], own_sem.at[0]),
        pltpu.make_async_copy(m_ref.at[tile], rm_ref.at[tile], own_sem.at[1]),
    ]
    for copy in own:
        copy.start()

    half = w_ref.shape[1] // 2
    mine = pl.ds(pl.multiple_of(core * half, half), half)
    other = pl.ds(pl.multiple_of((1 - core) * half, half), half)
    pair = pltpu.make_async_remote_copy(
        src_ref=w_ref.at[:, other], dst_ref=recv0,
        send_sem=pair_send.at[0], recv_sem=pair_recv.at[0],
        device_id=along("core", 1), device_id_type=MESH,
    )
    pair.start()
    issue(0)
    pair.wait()

    def add0(k, carry):
        acc0[k] = (w_ref[k, mine, :].astype(F32) + recv0[k].astype(F32)).astype(BF)
        return carry

    lax.fori_loop(0, w_ref.shape[0], add0, 0)

    def taps(i):
        return pl.ds(3 * i, 3)

    def exchange(stage, source, landing):
        copies = []
        for i, order in enumerate(ORDERS):
            axis = order[stage if stage < 3 else 5 - stage]
            for d in (1, 2, 3):
                src, dst = source(i, (place[axis] + d) % 4), landing(i, d - 1)
                copies.append(
                    pltpu.make_async_remote_copy(
                        src_ref=src, dst_ref=dst,
                        send_sem=st_send.at[stage, i, d - 1], recv_sem=st_recv.at[stage, i, d - 1],
                        device_id=along(axis, d), device_id_type=MESH,
                    )
                )
        for copy in copies:
            copy.start()
        return copies

    def sixteenth(i, q):
        return pl.ds(pl.multiple_of(q * 16, 16), 16)

    def quarter(i, q):
        return pl.ds(pl.multiple_of(q * 64, 64), 64)

    def lane_part(q):
        return pl.ds(pl.multiple_of(q * 128, 128), 128)

    copies = exchange(
        0, lambda i, q: acc0.at[taps(i), quarter(i, q)], lambda i, k: recv1.at[i, k]
    )
    issue(1)
    for copy in copies:
        copy.wait()
    for i, order in enumerate(ORDERS):
        q = place[order[0]]
        for j in range(3):
            total = acc0[3 * i + j, quarter(i, q), :].astype(F32)
            for k in range(3):
                total = total + recv1[i, k, j].astype(F32)
            acc1[i, j] = total.astype(BF)
    copies = exchange(1, lambda i, q: acc1.at[i, :, sixteenth(i, q)], lambda i, k: recv2.at[i, k])
    issue(2)
    for copy in copies:
        copy.wait()
    for i, order in enumerate(ORDERS):
        q = place[order[1]]
        for j in range(3):
            total = acc1[i, j, sixteenth(i, q), :].astype(F32)
            for k in range(3):
                total = total + recv2[i, k, j].astype(F32)
            acc2[i, j] = total.astype(BF)
    copies = exchange(2, lambda i, q: acc2.at[i, :, :, lane_part(q)], lambda i, k: recv3.at[i, k])
    issue(3)
    for copy in copies:
        copy.wait()

    def rows64(i):
        return pl.ds(pl.multiple_of(core * half + place[ORDERS[i][0]] * 64, 64), 64)

    def rows16(i):
        return pl.ds(
            pl.multiple_of(
                core * half + place[ORDERS[i][0]] * 64 + place[ORDERS[i][1]] * 16, 16
            ),
            16,
        )

    for i, order in enumerate(ORDERS):
        q = place[order[2]]
        for j in range(3):
            total = acc2[i, j, :, lane_part(q)].astype(F32)
            for k in range(3):
                total = total + recv3[i, k, j].astype(F32)
            o_ref[3 * i + j, rows16(i), lane_part(q)] = (total * scale).astype(BF)

    def finish(copies, stage, landed):
        for copy in copies:
            copy.wait_send()
        for i, order in enumerate(ORDERS):
            axis = order[5 - stage]
            for d in (1, 2, 3):
                part = landed(i, (place[axis] + 4 - d) % 4)
                pltpu.make_async_remote_copy(
                    src_ref=part, dst_ref=part,
                    send_sem=st_send.at[stage, i, d - 1], recv_sem=st_recv.at[stage, i, d - 1],
                    device_id=along(axis, d), device_id_type=MESH,
                ).wait_recv()

    def gather(stage, part, landed, batch):
        copies = []
        for i, order in enumerate(ORDERS):
            axis = order[5 - stage]
            for d in (1, 2, 3):
                copies.append(
                    pltpu.make_async_remote_copy(
                        src_ref=part(i), dst_ref=part(i),
                        send_sem=st_send.at[stage, i, d - 1], recv_sem=st_recv.at[stage, i, d - 1],
                        device_id=along(axis, d), device_id_type=MESH,
                    )
                )
        for copy in copies:
            copy.start()
        issue(batch)
        finish(copies, stage, landed)

    gather(
        3,
        lambda i: o_ref.at[taps(i), rows16(i), lane_part(place[ORDERS[i][2]])],
        lambda i, q: o_ref.at[taps(i), rows16(i), lane_part(q)],
        4,
    )
    gather(
        4,
        lambda i: o_ref.at[taps(i), rows16(i)],
        lambda i, q: o_ref.at[
            taps(i),
            pl.ds(pl.multiple_of(core * half + place[ORDERS[i][0]] * 64 + q * 16, 16), 16),
        ],
        5,
    )
    gather(
        5,
        lambda i: o_ref.at[taps(i), rows64(i)],
        lambda i, q: o_ref.at[taps(i), pl.ds(pl.multiple_of(core * half + q * 64, 64), 64)],
        6,
    )
    back = pltpu.make_async_remote_copy(
        src_ref=o_ref.at[:, mine], dst_ref=o_ref.at[:, mine],
        send_sem=pair_send.at[1], recv_sem=pair_recv.at[1],
        device_id=along("core", 1), device_id_type=MESH,
    )
    back.start()
    issue(7)
    back.wait_send()
    pltpu.make_async_remote_copy(
        src_ref=o_ref.at[:, other], dst_ref=o_ref.at[:, other],
        send_sem=pair_send.at[1], recv_sem=pair_recv.at[1],
        device_id=along("core", 1), device_id_type=MESH,
    ).wait_recv()

    for copy in own:
        copy.wait()

    def drain(n, carry):
        b, e = n // 8, n % 8
        slot_copy(b, e).wait_send()
        meta_copy(b, e).wait_send()
        source = shifted(b, e, -1)
        pltpu.make_async_remote_copy(
            src_ref=s_ref.at[source], dst_ref=r_ref.at[source],
            send_sem=slot_send.at[n], recv_sem=slot_recv.at[n],
            device_id=(dp, source), device_id_type=MESH,
        ).wait_recv()
        pltpu.make_async_remote_copy(
            src_ref=m_ref.at[source], dst_ref=rm_ref.at[source],
            send_sem=meta_send.at[n], recv_sem=meta_recv.at[n],
            device_id=(dp, source), device_id_type=MESH,
        ).wait_recv()
        return carry

    lax.fori_loop(1, 64, drain, 0)


def exchange_all(scale, slots, meta, w):
    taps, rows, chans = w.shape
    half = rows // 2
    return pl.pallas_call(
        functools.partial(exchange_kernel, scale),
        out_shape=[
            jax.ShapeDtypeStruct(slots.shape, BF),
            jax.ShapeDtypeStruct(meta.shape, BF),
            jax.ShapeDtypeStruct(w.shape, BF),
        ],
        in_specs=[ANY, ANY, VMEM],
        out_specs=[ANY, ANY, VMEM],
        scratch_shapes=[
            pltpu.VMEM((taps, half, chans), BF),
            pltpu.VMEM((taps, half, chans), BF),
            pltpu.VMEM((3, 3, 3, 64, chans), BF),
            pltpu.VMEM((3, 3, 64, chans), BF),
            pltpu.VMEM((3, 3, 3, 16, chans), BF),
            pltpu.VMEM((3, 3, 16, chans), BF),
            pltpu.VMEM((3, 3, 3, 16, 128), BF),
            pltpu.SemaphoreType.DMA((64,)),
            pltpu.SemaphoreType.DMA((64,)),
            pltpu.SemaphoreType.DMA((64,)),
            pltpu.SemaphoreType.DMA((64,)),
            pltpu.SemaphoreType.DMA((2,)),
            pltpu.SemaphoreType.DMA((2,)),
            pltpu.SemaphoreType.DMA((2,)),
            pltpu.SemaphoreType.DMA((6, 3, 3)),
            pltpu.SemaphoreType.DMA((6, 3, 3)),
        ],
        compiler_params=pltpu.CompilerParams(
            collective_id=0, has_side_effects=True, vmem_limit_bytes=32 << 20
        ),
        name="exchange_all",
    )(slots, meta, w)


def small_sum_kernel(scale, p_ref, o_ref, land, rs_send, rs_recv, ag_send, ag_recv):
    dp = lax.axis_index("dp")
    tile = lax.axis_index("tile")
    me = dp * TILES + tile
    count = 2 * TILES
    barrier = pltpu.get_barrier_semaphore()

    def target(n):
        d = (me + n) % count
        return d, (d // TILES, d % TILES)

    def greet(n, carry):
        pl.semaphore_signal(barrier, inc=1, device_id=target(n)[1], device_id_type=MESH)
        return carry

    lax.fori_loop(1, count, greet, 0)
    pl.semaphore_wait(barrier, count - 1)

    def part(ref, d):
        return ref.at[
            pl.ds(pl.multiple_of(d // 4 * 16, 16), 16),
            pl.ds(pl.multiple_of(d % 4 * 128, 128), 128),
        ]

    def scatter(n):
        d, where = target(n)
        return pltpu.make_async_remote_copy(
            src_ref=part(p_ref, d), dst_ref=land.at[me],
            send_sem=rs_send, recv_sem=rs_recv, device_id=where, device_id_type=MESH,
        )

    def spread(n):
        d, where = target(n)
        return pltpu.make_async_remote_copy(
            src_ref=part(o_ref, me), dst_ref=part(o_ref, me),
            send_sem=ag_send, recv_sem=ag_recv, device_id=where, device_id_type=MESH,
        )

    def start(make):
        def one(n, carry):
            make(n).start()
            return carry

        lax.fori_loop(1, count, one, 0)

    rows = pl.ds(pl.multiple_of(me // 4 * 16, 16), 16)
    lanes = pl.ds(pl.multiple_of(me % 4 * 128, 128), 128)
    land[me] = p_ref[rows, lanes]
    start(scatter)
    everything = land.at[pl.ds(0, count - 1)]
    pltpu.make_async_copy(everything, everything, rs_recv).wait()
    pltpu.make_async_copy(everything, everything, rs_send).wait()
    total = jnp.sum(land[...].astype(F32), axis=0)
    o_ref[rows, lanes] = (total * scale).astype(BF)
    start(spread)
    pltpu.make_async_copy(everything, everything, ag_recv).wait()
    pltpu.make_async_copy(everything, everything, ag_send).wait()


def small_sum(scale, part):
    return pl.pallas_call(
        functools.partial(small_sum_kernel, scale),
        out_shape=jax.ShapeDtypeStruct(part.shape, BF),
        in_specs=[VMEM],
        out_specs=VMEM,
        scratch_shapes=[
            pltpu.VMEM((2 * TILES, 16, 128), BF),
            pltpu.SemaphoreType.DMA,
            pltpu.SemaphoreType.DMA,
            pltpu.SemaphoreType.DMA,
            pltpu.SemaphoreType.DMA,
        ],
        compiler_params=pltpu.CompilerParams(
            collective_id=1, has_side_effects=True, vmem_limit_bytes=8 << 20
        ),
        name="small_sum",
    )(part)


def edge_rows(block):
    count = lax.axis_size("tile")
    forward = [(i, i + 1) for i in range(count - 1)]
    backward = [(target, source) for source, target in forward]
    return lax.ppermute(block[-1:], "tile", forward), lax.ppermute(block[:1], "tile", backward)


def silu_slope(value):
    sigma = jax.nn.sigmoid(value)
    return sigma * (1.0 + value * (1.0 - sigma))


def earlier_count(hits):
    size = hits.shape[-1]
    before = lax.broadcasted_iota(jnp.int32, (size, size), 0) < lax.broadcasted_iota(
        jnp.int32, (size, size), 1
    )
    return jnp.dot(hits.astype(BF), before.astype(BF), preferred_element_type=F32).astype(jnp.int32)


def body(grad_out, bev_act, conv_weight, img_in, backbone_weight, route, offsets, frac_x, frac_y):
    my_tile = lax.axis_index("tile")
    g, act, image = grad_out[0], bev_act[0], img_in[0]
    rows, cols, chans = g.shape
    g_lo, g_hi = edge_rows(g)
    a_lo, a_hi = edge_rows(act)
    blocks = rows * cols // BLK
    per_device = image.shape[0] // PIXB

    owners = (route[0] // per_device).reshape(TILES, blocks)
    local_ids = (route[0] % per_device).reshape(TILES, blocks)
    my_owners = lax.dynamic_index_in_dim(owners, my_tile, 0, keepdims=False)
    same = my_owners[:, None] == my_owners[None, :]
    before = lax.broadcasted_iota(jnp.int32, (blocks, blocks), 1) < lax.broadcasted_iota(
        jnp.int32, (blocks, blocks), 0
    )
    my_slots = my_owners * CAP + jnp.sum((same & before).astype(jnp.int32), axis=1)
    chosen = my_slots[None, :] == lax.broadcasted_iota(jnp.int32, (TILES * CAP, blocks), 0)
    idx = jnp.sum(
        jnp.where(chosen, lax.broadcasted_iota(jnp.int32, chosen.shape, 1), 0), axis=1
    )
    cells = jnp.stack([offsets[0], frac_x[0], frac_y[0]]).astype(BF).reshape(3, blocks, BLK)
    meta = jnp.einsum("sk,rkm->srm", chosen.astype(BF), cells, preferred_element_type=F32).astype(BF)
    meta = meta.reshape(TILES, CAP, 3, BLK).transpose(0, 2, 1, 3).reshape(TILES, 3, CAP * BLK)
    meta = jnp.pad(meta, ((0, 0), (0, 13), (0, 0)))

    weights = conv_weight.transpose(1, 2, 0, 3).reshape(9, chans, chans)
    slots = bev_slots(idx, g, g_lo[0], g_hi[0], weights)

    act_frame = jnp.pad(jnp.concatenate([a_lo, act, a_hi], axis=0), ((0, 0), (1, 1), (0, 0)))
    parts = []
    for row_tap in range(3):
        for col_tap in range(3):
            moved = act_frame[row_tap : row_tap + rows, col_tap : col_tap + cols]
            parts.append(jnp.einsum("rvc,rvo->co", moved, g, preferred_element_type=F32).astype(BF))
    conv_local = jnp.stack(parts)
    cell_scale = 1.0 / math.sqrt(2 * TILES * rows * cols)
    pixel_scale = 1.0 / math.sqrt(2 * TILES * image.shape[0])
    arrived, arrived_meta, conv_sum = exchange_all(
        cell_scale, slots.reshape(TILES, CAP * BLK, chans), meta, conv_local
    )
    conv_grad = conv_sum.reshape(3, 3, chans, chans).transpose(2, 0, 1, 3)

    mine = owners == my_tile
    rank = earlier_count(mine)
    rank_iota = lax.broadcasted_iota(jnp.int32, (1, 1, CAP), 2)
    picked = mine[:, :, None] & (rank[:, :, None] == rank_iota)
    held = jnp.sum(jnp.where(picked, local_ids[:, :, None] + 1, 0), axis=1) - 1
    base = jnp.where(held >= 0, held * PIXB, -4 * PIXB)
    base = jnp.broadcast_to(base[:, :, None], (TILES, CAP, BLK)).reshape(-1, 1)
    info = arrived_meta[:, :3].astype(F32)
    left = base + info[:, 0].reshape(-1, 1).astype(jnp.int32)
    right_w = info[:, 1].reshape(-1, 1) / 256.0
    lower_w = info[:, 2].reshape(-1, 1) / 256.0
    gap = lax.broadcasted_iota(jnp.int32, (1, per_device * PIXB), 1) - left
    across = jnp.where((gap == 0) | (gap == IMGW), 1.0 - right_w, 0.0) + jnp.where(
        (gap == 1) | (gap == IMGW + 1), right_w, 0.0
    )
    band = (jnp.where(gap >= IMGW, lower_w, 1.0 - lower_w) * across).astype(BF)
    feature_grad = lax.dot_general(
        band,
        arrived.reshape(-1, chans),
        (((0,), (0,)), ((), ())),
        preferred_element_type=F32,
    )
    pre_act = jnp.dot(image, backbone_weight, preferred_element_type=F32)
    scaled = (feature_grad * silu_slope(pre_act)).astype(BF)
    image_grad = lax.dot_general(
        scaled, backbone_weight, (((1,), (1,)), ((), ())), preferred_element_type=F32
    ).astype(BF)
    backbone_local = lax.dot_general(
        image, scaled, (((0,), (0,)), ((), ())), preferred_element_type=F32
    ).astype(BF)
    backbone_grad = small_sum(pixel_scale, backbone_local)
    return (image_grad[None], conv_grad, backbone_grad)


def solution(mesh):
    return jax.shard_map(
        body,
        mesh=mesh,
        in_specs=(
            P("dp", "tile", None, None),
            P("dp", "tile", None, None),
            P(),
            P("dp", "tile", None),
            P(),
            P("dp", None),
            P("dp", "tile"),
            P("dp", "tile"),
            P("dp", "tile"),
        ),
        out_specs=(P("dp", "tile", None), P(), P()),
        check_vma=False,
    )
```

```python
import functools
import math

import jax
import jax.numpy as jnp
from jax import lax
from jax.experimental import pallas as pl
from jax.experimental.pallas import tpu as pltpu
from jax.sharding import PartitionSpec as P

BLK = 64
IMGW = 64
PIXB = 2 * IMGW
TILES = 64
CAP = 2
MESH = pl.DeviceIdType.MESH
ANY = pl.BlockSpec(memory_space=pl.ANY)
VMEM = pl.BlockSpec(memory_space=pltpu.VMEM)
SMEM = pl.BlockSpec(memory_space=pltpu.SMEM)
BF = jnp.bfloat16
F32 = jnp.float32


def coords():
    t = lax.axis_index("tile")
    return t // 16, (t // 8) % 2 * 2 + lax.axis_index("dp"), (t // 2) % 4, t % 2


def device(y, x, z, core):
    return (x % 2, ((y * 2 + x // 2) * 4 + z) * 2 + core)


def along(axis, step):
    y, x, z, core = coords()
    if axis == "y":
        y = (y + step) % 4
    elif axis == "x":
        x = (x + step) % 4
    elif axis == "z":
        z = (z + step) % 4
    else:
        core = 1 - core
    return device(y, x, z, core)


def bev_kernel(idx_ref, g_ref, lo_ref, hi_ref, w_ref, sa_ref, sb_ref, frame, w, acc, bev, sems, out_sem):
    rows, cols = g_ref.shape[0], g_ref.shape[1]
    copies = [
        pltpu.make_async_copy(w_ref, w, sems.at[0]),
        pltpu.make_async_copy(g_ref, frame.at[pl.ds(1, rows)], sems.at[1]),
        pltpu.make_async_copy(lo_ref, frame.at[0], sems.at[2]),
        pltpu.make_async_copy(hi_ref, frame.at[rows + 1], sems.at[3]),
    ]
    for copy in copies:
        copy.start()
    for copy in copies:
        copy.wait()
    half = 256

    def step(s, carry):
        r, n = s // 2, s % 2
        lanes = pl.ds(pl.multiple_of(n * half, half), half)

        def tap(j):
            total = None
            for i in range(3):
                term = lax.dot_general(
                    frame[r + 2 - i],
                    w[i * 3 + j, lanes, :],
                    (((1,), (1,)), ((), ())),
                    preferred_element_type=F32,
                )
                total = term if total is None else total + term
            return total

        acc[pl.ds(8, cols), :] = tap(1)
        acc[pl.ds(7, cols), :] += tap(0)
        acc[pl.ds(9, cols), :] += tap(2)
        bev[n, pl.ds(pl.multiple_of(r * cols, cols), cols), :] = acc[pl.ds(8, cols), :].astype(BF)
        return carry

    lax.fori_loop(0, 2 * rows, step, 0)

    def send(s, carry):
        start = pl.multiple_of(idx_ref[s] * BLK, BLK)
        rows_of = pl.ds(start, BLK)
        pltpu.make_async_copy(bev.at[0, rows_of], sa_ref.at[s], out_sem.at[0]).start()
        pltpu.make_async_copy(bev.at[1, rows_of], sb_ref.at[s], out_sem.at[1]).start()
        return carry

    lax.fori_loop(0, TILES * CAP, send, 0)
    pltpu.make_async_copy(sa_ref, sa_ref, out_sem.at[0]).wait()
    pltpu.make_async_copy(sb_ref, sb_ref, out_sem.at[1]).wait()


def bev_slots(idx, g, lo, hi, w):
    rows, cols, chans = g.shape
    return pl.pallas_call(
        bev_kernel,
        out_shape=[jax.ShapeDtypeStruct((TILES * CAP, BLK, chans // 2), BF)] * 2,
        in_specs=[SMEM, ANY, ANY, ANY, ANY],
        out_specs=[ANY, ANY],
        scratch_shapes=[
            pltpu.VMEM((rows + 2, cols, chans), BF),
            pltpu.VMEM(w.shape, BF),
            pltpu.VMEM((cols + 16, 256), F32),
            pltpu.VMEM((2, rows * cols, chans // 2), BF),
            pltpu.SemaphoreType.DMA((4,)),
            pltpu.SemaphoreType.DMA((2,)),
        ],
        compiler_params=pltpu.CompilerParams(vmem_limit_bytes=40 << 20),
        cost_estimate=pl.CostEstimate(
            flops=2 * 9 * rows * cols * chans * chans, bytes_accessed=24 << 20, transcendentals=0
        ),
        name="bev_slots",
    )(idx, g, lo, hi, w)


NPIX = 4 * PIXB
CELLS = CAP * BLK
GROUP = 8


def exchange_kernel(
    scale, sa_ref, sb_ref, m_ref, w_ref, f_ref, o_ref,
    land, meta, band, dense, land2, sums, land3, recv0, acc0, recv1, acc1, recv2,
    m_send, m_recv, p1_send, p1_recv, own_sem, p2_send, p2_recv, p3_send, p3_recv,
    pair_send, pair_recv, x_send, x_recv, yz_send, yz_recv,
):
    y, x, z, core = coords()
    x_hi = x // 2

    def remote(src, dst, sends, recvs, where):
        return pltpu.make_async_remote_copy(
            src_ref=src, dst_ref=dst, send_sem=sends, recv_sem=recvs,
            device_id=where, device_id_type=MESH,
        )

    plane = [(dy, dz) for dy in range(4) for dz in range(4) if dy or dz]

    def at(dy, dz, dc):
        return device((y + dy) % 4, x, (z + dz) % 4, (core + dc) % 2)

    barrier = pltpu.get_barrier_semaphore()
    greeted = [at(0, 0, 1)] + [at(dy, dz, 0) for dy, dz in plane]
    greeted += [at(dy, dz, 1) for dy, dz in plane if not (dy and dz)]
    greeted += [along("x", d) for d in (1, 2, 3)]
    for where in greeted:
        pl.semaphore_signal(barrier, inc=1, device_id=where, device_id_type=MESH)
    pl.semaphore_wait(barrier, len(greeted))

    line = (z, y)
    here = [line[h] * 2 + core for h in range(2)]

    def slots_of(h, member):
        return sa_ref.at[:, member] if h == 0 else sb_ref.at[member // 2, :, member % 2]

    steps = [(d, dc) for d in range(4) for dc in range(2) if d or dc]

    def member_at(h, d, dc):
        return (line[h] + d) % 4 * 2 + (core + dc) % 2

    def group_copy(h, k, sign, which):
        d, dc = steps[k]
        member = member_at(h, d if sign > 0 else 4 - d, dc)
        where = at(0, d, dc) if h == 0 else at(d, 0, dc)
        place = here[h] if sign > 0 else member
        if which == "meta":
            return remote(
                mb(h, member), meta.at[h, place], m_send.at[h, k], m_recv.at[h, k], where
            )
        return remote(
            slots_of(h, member), land.at[h, place], p1_send.at[h, k], p1_recv.at[h, k], where
        )

    def mb(h, member):
        return m_ref.at[0, :, member] if h == 0 else m_ref.at[1, :, member]

    own = []
    for h in range(2):
        own.append(pltpu.make_async_copy(mb(h, here[h]), meta.at[h, here[h]], own_sem.at[h, 0]))
        own.append(
            pltpu.make_async_copy(slots_of(h, here[h]), land.at[h, here[h]], own_sem.at[h, 1])
        )
    for copy in own:
        copy.start()
    for k in range(7):
        for h in range(2):
            group_copy(h, k, 1, "meta").start()

    half = w_ref.shape[1] // 2
    mine = pl.ds(pl.multiple_of(core * half, half), half)
    other = pl.ds(pl.multiple_of((1 - core) * half, half), half)
    pair = remote(
        w_ref.at[:, other], recv0, pair_send.at[0], pair_recv.at[0], at(0, 0, 1)
    )
    pair.start()
    for k in range(7):
        for h in range(2):
            group_copy(h, k, 1, "slots").start()
    pair.wait()

    def add0(k, carry):
        acc0[k] = (w_ref[k, mine, :].astype(F32) + recv0[k].astype(F32)).astype(BF)
        return carry

    lax.fori_loop(0, w_ref.shape[0], add0, 0)

    def rows64(q):
        return pl.ds(pl.multiple_of(q * 64, 64), 64)

    along_x = [
        remote(
            acc0.at[:, rows64((x + d) % 4)], recv1.at[d - 1],
            x_send.at[0, d - 1], x_recv.at[0, d - 1], along("x", d),
        )
        for d in (1, 2, 3)
    ]
    for copy in along_x:
        copy.start()

    for k in range(7):
        for h in range(2):
            group_copy(h, k, 1, "meta").wait_send()
            group_copy(h, k, -1, "meta").wait_recv()
    own[0].wait()
    own[2].wait()

    def make_band(n, carry):
        h, owner, member = n // 64, n // 8 % 8, n % 8
        info = meta[h, member, owner].astype(F32)
        q = lax.broadcasted_iota(jnp.int32, (IMGW, CELLS), 0).astype(F32)
        left, right = q == info[0:1], q == info[0:1] + 1.0
        zero = jnp.zeros((IMGW, CELLS), F32)
        upper = jnp.where(left, info[2:3], jnp.where(right, info[3:4], zero))
        lower = jnp.where(left, info[4:5], jnp.where(right, info[5:6], zero))
        whole = jnp.concatenate([upper, lower], axis=0)
        lanes = pl.ds(pl.multiple_of(member * CELLS, CELLS), CELLS)
        for block in range(4):
            kept = jnp.where(info[1:2] == float(block), whole, 0.0)
            band[h, owner, pl.ds(block * PIXB, PIXB), lanes] = kept.astype(BF)
        return carry

    lax.fori_loop(0, 128, make_band, 0)

    for copy in along_x:
        copy.wait()

    def add1(k, carry):
        total = acc0[k, rows64(x), :].astype(F32)
        for d in range(3):
            total = total + recv1[d, k].astype(F32)
        acc1[k] = total.astype(BF)
        return carry

    lax.fori_loop(0, w_ref.shape[0], add1, 0)

    def rows16(ref, base, q_y, q_z):
        return ref.at[
            :,
            pl.ds(pl.multiple_of(base + q_y * 16, 16), 16),
            pl.ds(pl.multiple_of(q_z * 128, 128), 128),
        ]

    to_plane = [
        remote(
            rows16(acc1, 0, (y + dy) % 4, (z + dz) % 4), recv2.at[k],
            yz_send.at[0, k], yz_recv.at[0, k], at(dy, dz, 0),
        )
        for k, (dy, dz) in enumerate(plane)
    ]
    for copy in to_plane:
        copy.start()

    def reduce_half(h):
        for k in range(7):
            group_copy(h, k, 1, "slots").wait_send()
            group_copy(h, k, -1, "slots").wait_recv()
        own[2 * h + 1].wait()

        def one(owner, carry):
            cells = land[h, :, owner].reshape(GROUP * CELLS, land.shape[-1])
            dense[h, owner] = jnp.dot(
                band[h, owner], cells, preferred_element_type=F32
            ).astype(BF)
            return carry

        lax.fori_loop(0, GROUP, one, 0)

    def dense_part(h, x_part, q):
        return dense.at[h, q * 2 + x_part] if h == 0 else dense.at[h, x_part * 4 + q]

    cross = (y, z)

    def second(h):
        return [
            remote(
                dense_part(h, x_part, (cross[h] + d) % 4), land2.at[h, x_part, d - 1],
                p2_send.at[h, x_part, d - 1], p2_recv.at[h, x_part, d - 1],
                at(d, 0, 0) if h == 0 else at(0, d, 0),
            )
            for x_part in range(2)
            for d in (1, 2, 3)
        ]

    reduce_half(0)
    for copy in to_plane:
        copy.wait()

    def add2(k, carry):
        total = acc1[
            k, pl.ds(pl.multiple_of(y * 16, 16), 16), pl.ds(pl.multiple_of(z * 128, 128), 128)
        ].astype(F32)
        for p in range(15):
            total = total + recv2[p, k].astype(F32)
        o_ref[
            k,
            pl.ds(pl.multiple_of(core * half + x * 64 + y * 16, 16), 16),
            pl.ds(pl.multiple_of(z * 128, 128), 128),
        ] = (total * scale).astype(BF)
        return carry

    lax.fori_loop(0, w_ref.shape[0], add2, 0)
    base = core * half + x * 64

    def spread(k, sign):
        dy, dz = plane[k]
        part = rows16(o_ref, base, (y + sign * dy + 4) % 4, (z + sign * dz + 4) % 4)
        if sign == 0:
            part = rows16(o_ref, base, y, z)
        return remote(part, part, yz_send.at[1, k], yz_recv.at[1, k], at(dy, dz, 0))

    for k in range(15):
        spread(k, 0).start()
    second0 = second(0)
    for copy in second0:
        copy.start()
    reduce_half(1)
    second1 = second(1)
    for copy in second1:
        copy.start()
    for k in range(15):
        spread(k, 0).wait_send()
        spread(k, -1).wait_recv()

    def strip(d, sign):
        part = o_ref.at[:, rows64(core * 4 + (x + sign * d + 4) % 4)]
        return remote(part, part, x_send.at[1, d - 1], x_recv.at[1, d - 1], along("x", d))

    for d in (1, 2, 3):
        strip(d, 0).start()

    for copy in second0 + second1:
        copy.wait()

    def add3(h, x_part):
        start = dense[h, cross[h] * 2 + x_part] if h == 0 else dense[h, x_part * 4 + cross[h]]
        total = start.astype(F32)
        for d in range(3):
            total = total + land2[h, x_part, d].astype(F32)
        return total

    third = []
    for h in range(2):
        sums[h] = add3(h, 1 - x_hi).astype(BF)
        third.append(
            remote(sums.at[h], land3.at[h], p3_send.at[h], p3_recv.at[h], along("x", 2))
        )
        third[h].start()
    lanes_of = (pl.ds(0, 256), pl.ds(256, 256))
    for h in range(2):
        f_ref[:, lanes_of[h]] = add3(h, x_hi)

    for d in (1, 2, 3):
        strip(d, 0).wait_send()
        strip(d, -1).wait_recv()
    back = remote(
        o_ref.at[:, mine], o_ref.at[:, mine], pair_send.at[1], pair_recv.at[1], at(0, 0, 1)
    )
    back.start()
    for h in range(2):
        third[h].wait()
        f_ref[:, lanes_of[h]] += land3[h].astype(F32)
    back.wait_send()
    remote(
        o_ref.at[:, other], o_ref.at[:, other], pair_send.at[1], pair_recv.at[1], at(0, 0, 1)
    ).wait_recv()


def exchange_all(scale, slots, meta, w):
    taps, rows, chans = w.shape
    half = rows // 2
    wide = chans // 2
    dma = pltpu.SemaphoreType.DMA
    return pl.pallas_call(
        functools.partial(exchange_kernel, scale),
        out_shape=[
            jax.ShapeDtypeStruct((NPIX, chans), F32),
            jax.ShapeDtypeStruct(w.shape, BF),
        ],
        in_specs=[ANY, ANY, ANY, VMEM],
        out_specs=[VMEM, VMEM],
        scratch_shapes=[
            pltpu.VMEM((2, GROUP, GROUP, CELLS, wide), BF),
            pltpu.VMEM((2, GROUP, GROUP, 16, CELLS), BF),
            pltpu.VMEM((2, GROUP, NPIX, GROUP * CELLS), BF),
            pltpu.VMEM((2, GROUP, NPIX, wide), BF),
            pltpu.VMEM((2, 2, 3, NPIX, wide), BF),
            pltpu.VMEM((2, NPIX, wide), BF),
            pltpu.VMEM((2, NPIX, wide), BF),
            pltpu.VMEM((taps, half, chans), BF),
            pltpu.VMEM((taps, half, chans), BF),
            pltpu.VMEM((3, taps, 64, chans), BF),
            pltpu.VMEM((taps, 64, chans), BF),
            pltpu.VMEM((15, taps, 16, 128), BF),
            dma((2, 7)), dma((2, 7)), dma((2, 7)), dma((2, 7)), dma((2, 2)),
            dma((2, 2, 3)), dma((2, 2, 3)), dma((2,)), dma((2,)),
            dma((2,)), dma((2,)), dma((2, 3)), dma((2, 3)), dma((2, 15)), dma((2, 15)),
        ],
        compiler_params=pltpu.CompilerParams(
            collective_id=0, has_side_effects=True, vmem_limit_bytes=60 << 20
        ),
        name="exchange_all",
    )(*slots, meta, w)


def small_sum_kernel(scale, p_ref, o_ref, land, rs_send, rs_recv, ag_send, ag_recv):
    dp = lax.axis_index("dp")
    tile = lax.axis_index("tile")
    me = dp * TILES + tile
    count = 2 * TILES
    barrier = pltpu.get_barrier_semaphore()

    def target(n):
        d = (me + n) % count
        return d, (d // TILES, d % TILES)

    def greet(n, carry):
        pl.semaphore_signal(barrier, inc=1, device_id=target(n)[1], device_id_type=MESH)
        return carry

    lax.fori_loop(1, count, greet, 0)
    pl.semaphore_wait(barrier, count - 1)

    def part(ref, d):
        return ref.at[
            pl.ds(pl.multiple_of(d // 4 * 16, 16), 16),
            pl.ds(pl.multiple_of(d % 4 * 128, 128), 128),
        ]

    def scatter(n):
        d, where = target(n)
        return pltpu.make_async_remote_copy(
            src_ref=part(p_ref, d), dst_ref=land.at[me],
            send_sem=rs_send, recv_sem=rs_recv, device_id=where, device_id_type=MESH,
        )

    def spread(n):
        d, where = target(n)
        return pltpu.make_async_remote_copy(
            src_ref=part(o_ref, me), dst_ref=part(o_ref, me),
            send_sem=ag_send, recv_sem=ag_recv, device_id=where, device_id_type=MESH,
        )

    def start(make):
        def one(n, carry):
            make(n).start()
            return carry

        lax.fori_loop(1, count, one, 0)

    rows = pl.ds(pl.multiple_of(me // 4 * 16, 16), 16)
    lanes = pl.ds(pl.multiple_of(me % 4 * 128, 128), 128)
    land[me] = p_ref[rows, lanes]
    start(scatter)
    everything = land.at[pl.ds(0, count - 1)]
    pltpu.make_async_copy(everything, everything, rs_recv).wait()
    pltpu.make_async_copy(everything, everything, rs_send).wait()
    total = jnp.sum(land[...].astype(F32), axis=0)
    o_ref[rows, lanes] = (total * scale).astype(BF)
    start(spread)
    pltpu.make_async_copy(everything, everything, ag_recv).wait()
    pltpu.make_async_copy(everything, everything, ag_send).wait()


def small_sum(scale, part):
    return pl.pallas_call(
        functools.partial(small_sum_kernel, scale),
        out_shape=jax.ShapeDtypeStruct(part.shape, BF),
        in_specs=[VMEM],
        out_specs=VMEM,
        scratch_shapes=[
            pltpu.VMEM((2 * TILES, 16, 128), BF),
            pltpu.SemaphoreType.DMA,
            pltpu.SemaphoreType.DMA,
            pltpu.SemaphoreType.DMA,
            pltpu.SemaphoreType.DMA,
        ],
        compiler_params=pltpu.CompilerParams(
            collective_id=1, has_side_effects=True, vmem_limit_bytes=8 << 20
        ),
        name="small_sum",
    )(part)


def edge_rows(block):
    count = lax.axis_size("tile")
    forward = [(i, i + 1) for i in range(count - 1)]
    backward = [(target, source) for source, target in forward]
    return lax.ppermute(block[-1:], "tile", forward), lax.ppermute(block[:1], "tile", backward)


def silu_slope(value):
    sigma = jax.nn.sigmoid(value)
    return sigma * (1.0 + value * (1.0 - sigma))


def body(grad_out, bev_act, conv_weight, img_in, backbone_weight, route, offsets, frac_x, frac_y):
    my_tile = lax.axis_index("tile")
    g, act, image = grad_out[0], bev_act[0], img_in[0]
    rows, cols, chans = g.shape
    g_lo, g_hi = edge_rows(g)
    a_lo, a_hi = edge_rows(act)
    blocks = rows * cols // BLK
    per_device = image.shape[0] // PIXB

    owners = (route[0] // per_device).reshape(TILES, blocks)
    local_ids = (route[0] % per_device).reshape(TILES, blocks)
    my_owners = lax.dynamic_index_in_dim(owners, my_tile, 0, keepdims=False)
    same = my_owners[:, None] == my_owners[None, :]
    before = lax.broadcasted_iota(jnp.int32, (blocks, blocks), 1) < lax.broadcasted_iota(
        jnp.int32, (blocks, blocks), 0
    )
    my_slots = my_owners * CAP + jnp.sum((same & before).astype(jnp.int32), axis=1)
    chosen = my_slots[None, :] == lax.broadcasted_iota(jnp.int32, (TILES * CAP, blocks), 0)
    idx = jnp.sum(
        jnp.where(chosen, lax.broadcasted_iota(jnp.int32, chosen.shape, 1), 0), axis=1
    )
    right_w = frac_x[0].astype(F32) / 256.0
    lower_w = frac_y[0].astype(F32) / 256.0
    cells = jnp.stack(
        [
            offsets[0].astype(F32),
            (1.0 - lower_w) * (1.0 - right_w),
            (1.0 - lower_w) * right_w,
            lower_w * (1.0 - right_w),
            lower_w * right_w,
        ]
    )
    cells = cells.astype(BF).reshape(5, blocks, BLK)
    info = jnp.einsum("sk,rkm->srm", chosen.astype(BF), cells, preferred_element_type=F32)
    my_local = lax.dynamic_index_in_dim(local_ids, my_tile, 0, keepdims=False)
    held = jnp.sum(jnp.where(chosen, my_local[None, :] + 1, 0), axis=1) - 1
    held = jnp.broadcast_to(held.astype(F32)[:, None, None], (TILES * CAP, 1, BLK))
    info = jnp.concatenate([info[:, :1], held, info[:, 1:]], axis=1).astype(BF)
    info = info.reshape(TILES, CAP, 6, BLK).transpose(0, 2, 1, 3).reshape(TILES, 6, CELLS)
    info = jnp.pad(info, ((0, 0), (0, 10), (0, 0)))
    by_z = info.reshape(8, 8, 16, CELLS)
    by_y = info.reshape(4, 8, 2, 16, CELLS).transpose(1, 0, 2, 3, 4).reshape(8, 8, 16, CELLS)
    meta = jnp.stack([by_z, by_y])

    weights = conv_weight.transpose(1, 2, 0, 3).reshape(9, chans, chans)
    slot_z, slot_y = bev_slots(idx, g, g_lo[0], g_hi[0], weights)
    slot_z = slot_z.reshape(8, 8, CELLS, chans // 2)
    slot_y = slot_y.reshape(4, 8, 2, CELLS, chans // 2)

    act_frame = jnp.pad(jnp.concatenate([a_lo, act, a_hi], axis=0), ((0, 0), (1, 1), (0, 0)))
    parts = []
    for row_tap in range(3):
        for col_tap in range(3):
            moved = act_frame[row_tap : row_tap + rows, col_tap : col_tap + cols]
            parts.append(jnp.einsum("rvc,rvo->co", moved, g, preferred_element_type=F32).astype(BF))
    conv_local = jnp.stack(parts)
    cell_scale = 1.0 / math.sqrt(2 * TILES * rows * cols)
    pixel_scale = 1.0 / math.sqrt(2 * TILES * image.shape[0])
    feature_grad, conv_sum = exchange_all(cell_scale, (slot_z, slot_y), meta, conv_local)
    conv_grad = conv_sum.reshape(3, 3, chans, chans).transpose(2, 0, 1, 3)

    pre_act = jnp.dot(image, backbone_weight, preferred_element_type=F32)
    scaled = (feature_grad * silu_slope(pre_act)).astype(BF)
    image_grad = lax.dot_general(
        scaled, backbone_weight, (((1,), (1,)), ((), ())), preferred_element_type=F32
    ).astype(BF)
    backbone_local = lax.dot_general(
        image, scaled, (((0,), (0,)), ((), ())), preferred_element_type=F32
    ).astype(BF)
    backbone_grad = small_sum(pixel_scale, backbone_local)
    return (image_grad[None], conv_grad, backbone_grad)


def solution(mesh):
    return jax.shard_map(
        body,
        mesh=mesh,
        in_specs=(
            P("dp", "tile", None, None),
            P("dp", "tile", None, None),
            P(),
            P("dp", "tile", None),
            P(),
            P("dp", None),
            P("dp", "tile"),
            P("dp", "tile"),
            P("dp", "tile"),
        ),
        out_specs=(P("dp", "tile", None), P(), P()),
        check_vma=False,
    )
```

```python
import functools
import math

import jax
import jax.numpy as jnp
from jax import lax
from jax.experimental import pallas as pl
from jax.experimental.pallas import tpu as pltpu
from jax.sharding import PartitionSpec as P

BLK = 64
IMGW = 64
PIXB = 2 * IMGW
TILES = 64
CAP = 2
MESH = pl.DeviceIdType.MESH
ANY = pl.BlockSpec(memory_space=pl.ANY)
VMEM = pl.BlockSpec(memory_space=pltpu.VMEM)
SMEM = pl.BlockSpec(memory_space=pltpu.SMEM)
HBM = pl.BlockSpec(memory_space=pltpu.HBM)
BF = jnp.bfloat16
F32 = jnp.float32


def coords():
    t = lax.axis_index("tile")
    return t // 16, (t // 8) % 2 * 2 + lax.axis_index("dp"), (t // 2) % 4, t % 2


def device(y, x, z, core):
    return (x % 2, ((y * 2 + x // 2) * 4 + z) * 2 + core)


def along(axis, step):
    y, x, z, core = coords()
    if axis == "y":
        y = (y + step) % 4
    elif axis == "x":
        x = (x + step) % 4
    elif axis == "z":
        z = (z + step) % 4
    else:
        core = 1 - core
    return device(y, x, z, core)


def bev_kernel(idx_ref, g_ref, lo_ref, hi_ref, w_ref, sa_ref, sb_ref, frame, w, acc, bev, sems, out_sem):
    rows, cols = g_ref.shape[0], g_ref.shape[1]
    copies = [
        pltpu.make_async_copy(w_ref, w, sems.at[0]),
        pltpu.make_async_copy(g_ref, frame.at[pl.ds(1, rows)], sems.at[1]),
        pltpu.make_async_copy(lo_ref, frame.at[0], sems.at[2]),
        pltpu.make_async_copy(hi_ref, frame.at[rows + 1], sems.at[3]),
    ]
    for copy in copies:
        copy.start()
    for copy in copies:
        copy.wait()
    half = 256

    def step(s, carry):
        r, n = s // 2, s % 2
        lanes = pl.ds(pl.multiple_of(n * half, half), half)

        def tap(j):
            total = None
            for i in range(3):
                term = lax.dot_general(
                    frame[r + 2 - i],
                    w[i * 3 + j, lanes, :],
                    (((1,), (1,)), ((), ())),
                    preferred_element_type=F32,
                )
                total = term if total is None else total + term
            return total

        acc[pl.ds(8, cols), :] = tap(1)
        acc[pl.ds(7, cols), :] += tap(0)
        acc[pl.ds(9, cols), :] += tap(2)
        bev[n, pl.ds(pl.multiple_of(r * cols, cols), cols), :] = acc[pl.ds(8, cols), :].astype(BF)
        return carry

    lax.fori_loop(0, 2 * rows, step, 0)

    def send(s, carry):
        start = pl.multiple_of(idx_ref[s] * BLK, BLK)
        rows_of = pl.ds(start, BLK)
        pltpu.make_async_copy(bev.at[0, rows_of], sa_ref.at[s], out_sem.at[0]).start()
        pltpu.make_async_copy(bev.at[1, rows_of], sb_ref.at[s], out_sem.at[1]).start()
        return carry

    lax.fori_loop(0, TILES * CAP, send, 0)
    pltpu.make_async_copy(sa_ref, sa_ref, out_sem.at[0]).wait()
    pltpu.make_async_copy(sb_ref, sb_ref, out_sem.at[1]).wait()


def bev_slots(idx, g, lo, hi, w):
    rows, cols, chans = g.shape
    return pl.pallas_call(
        bev_kernel,
        out_shape=[jax.ShapeDtypeStruct((TILES * CAP, BLK, chans // 2), BF)] * 2,
        in_specs=[SMEM, ANY, ANY, ANY, ANY],
        out_specs=[HBM, HBM],
        scratch_shapes=[
            pltpu.VMEM((rows + 2, cols, chans), BF),
            pltpu.VMEM(w.shape, BF),
            pltpu.VMEM((cols + 16, 256), F32),
            pltpu.VMEM((2, rows * cols, chans // 2), BF),
            pltpu.SemaphoreType.DMA((4,)),
            pltpu.SemaphoreType.DMA((2,)),
        ],
        compiler_params=pltpu.CompilerParams(vmem_limit_bytes=40 << 20),
        cost_estimate=pl.CostEstimate(
            flops=2 * 9 * rows * cols * chans * chans, bytes_accessed=24 << 20, transcendentals=0
        ),
        name="bev_slots",
    )(idx, g, lo, hi, w)


NPIX = 4 * PIXB
CELLS = CAP * BLK
GROUP = 8


def silu_slope(value):
    sigma = jax.nn.sigmoid(value)
    return sigma * (1.0 + value * (1.0 - sigma))


def exchange_kernel(
    cell_scale, pixel_scale,
    sa_ref, sb_ref, m_ref, g_ref, a_ref, alo_ref, ahi_ref, img_ref, bw_ref,
    ig_ref, o_ref, bb_ref,
    land, meta, band, dense, land2, sums, land3, w_ref, recv0, acc0, recv1, acc1, recv2,
    shift, feature, slope, img_t, bb, bb0, bb0_acc, bb1, bb1_acc, bb2,
    in_sem, m_send, m_recv, p1_send, p1_recv, own_sem, p2_send, p2_recv, p3_send, p3_recv,
    pair_send, pair_recv, x_send, x_recv, yz_send, yz_recv, ag_send, ag_recv, far_send, far_recv,
    by_send, by_recv, bx_send, bx_recv,
):
    y, x, z, core = coords()
    x_hi = x // 2
    taps, chans = w_ref.shape[0], w_ref.shape[1]
    rows, cols = a_ref.shape[0] // alo_ref.shape[0], alo_ref.shape[0] * 64

    def remote(src, dst, sends, recvs, where):
        return pltpu.make_async_remote_copy(
            src_ref=src, dst_ref=dst, send_sem=sends, recv_sem=recvs,
            device_id=where, device_id_type=MESH,
        )

    plane = [(p, q) for p in range(4) for q in range(4) if p or q]
    corner = [(p, q) for p, q in plane if p and q]

    def at(dy, dz, dc, dx=0):
        return device((y + dy) % 4, (x + dx) % 4, (z + dz) % 4, (core + dc) % 2)

    barrier = pltpu.get_barrier_semaphore()
    greeted = [at(0, 0, 1)] + [at(dy, dz, 0) for dy, dz in plane]
    greeted += [at(dy, dz, 1) for dy, dz in plane if not (dy and dz)]
    greeted += [at(0, 0, 0, d) for d in (1, 2, 3)]
    greeted += [at(p, 0, 0, q) for p, q in corner] + [at(0, p, 0, q) for p, q in corner]
    for where in greeted:
        pl.semaphore_signal(barrier, inc=1, device_id=where, device_id_type=MESH)

    loads = [
        pltpu.make_async_copy(g_ref.at[pl.ds(p * 512, 512)], w_ref.at[p], in_sem.at[p])
        for p in range(5)
    ]
    loads += [
        pltpu.make_async_copy(
            a_ref.at[pl.ds(4 * u, 4)], o_ref.at[u // 2, u % 2], in_sem.at[5 + u]
        )
        for u in range(10)
    ]
    for k, ref in enumerate((alo_ref, ahi_ref)):
        for u in range(3):
            size = 4 if u < 2 else 2
            loads.append(
                pltpu.make_async_copy(
                    ref.at[pl.ds(4 * u, size)],
                    o_ref.at[5 + 2 * k + u // 2, u % 2, pl.ds(0, size)],
                    in_sem.at[15 + 3 * k + u],
                )
            )
    for copy in loads:
        copy.start()
    pl.semaphore_wait(barrier, len(greeted))

    line = (z, y)
    here = [line[h] * 2 + core for h in range(2)]

    def slots_of(h, member):
        return sa_ref.at[:, member] if h == 0 else sb_ref.at[member // 2, :, member % 2]

    def info_of(h, member):
        return m_ref.at[h, :, member]

    steps = [(d, dc) for d in range(4) for dc in range(2) if d or dc]

    def group_copy(h, k, sign, which):
        d, dc = steps[k]
        member = (line[h] + (d if sign > 0 else 4 - d)) % 4 * 2 + (core + dc) % 2
        where = at(0, d, dc) if h == 0 else at(d, 0, dc)
        place = here[h] if sign > 0 else member
        if which == "meta":
            return remote(
                info_of(h, member), meta.at[h, place], m_send.at[h, k], m_recv.at[h, k], where
            )
        return remote(
            slots_of(h, member), land.at[h, place], p1_send.at[h, k], p1_recv.at[h, k], where
        )

    own = []
    for h in range(2):
        own.append(
            pltpu.make_async_copy(info_of(h, here[h]), meta.at[h, here[h]], own_sem.at[h, 0])
        )
        own.append(
            pltpu.make_async_copy(slots_of(h, here[h]), land.at[h, here[h]], own_sem.at[h, 1])
        )
    for copy in own:
        copy.start()
    for which in ("meta", "slots"):
        for k in range(7):
            for h in range(2):
                group_copy(h, k, 1, which).start()

    for copy in loads:
        copy.wait()

    def turn(r, piece, start, column):
        block = o_ref[piece, start // 256, pl.ds(start // 64 % 4, 2)]
        band[r, :, column] = block.reshape(128, chans).T

    def turn_inner(n, carry):
        column = pl.ds(pl.multiple_of(n % 5 * 128, 128), 128)
        turn(n // 5 + 1, n // 4, n % 4 * 128, column)
        return carry

    lax.fori_loop(0, 20, turn_inner, 0)
    for k, r in ((0, 0), (1, rows + 1)):
        for n in range(5):
            turn(r, 5 + 2 * k + n // 4, n % 4 * 128, pl.ds(n * 128, 128))

    def store_moved(j, n, value):
        p = j * 5 + n // 4
        band[
            6 + p // 2,
            pl.ds(pl.multiple_of(n % 4 * 128, 128), 128),
            pl.ds(pl.multiple_of(p % 2 * 512, 512), 512),
        ] = value.astype(BF)

    edge = jnp.zeros((8, chans), F32)
    shift[pl.ds(0, 8), :] = edge
    shift[pl.ds(cols + 8, 8), :] = edge

    def move(r, carry):
        for n in range(5):
            b = r * 5 + n
            block = w_ref[b // 4, pl.ds(pl.multiple_of(b % 4 * 128, 128), 128), :]
            store_moved(1, b, block)
            shift[pl.ds(8 + n * 128, 128), :] = block.astype(F32)
        for n in range(5):
            store_moved(0, r * 5 + n, shift[pl.ds(9 + n * 128, 128), :])
            store_moved(2, r * 5 + n, shift[pl.ds(7 + n * 128, 128), :])
        return carry

    lax.fori_loop(0, rows, move, 0)

    def tap(n, carry):
        i, j = n // 3, n % 3
        left = jnp.concatenate([band[r + i, :, 0:cols] for r in range(rows)], axis=1)
        parts = []
        for k in range(5):
            p = j * 5 + k
            parts.append(
                band[6 + p // 2, :, pl.ds(pl.multiple_of(p % 2 * 512, 512), 512)]
            )
        right = jnp.concatenate(parts, axis=0)
        w_ref[n] = jnp.dot(left, right, preferred_element_type=F32).astype(BF)
        return carry

    lax.fori_loop(0, taps, tap, 0)

    half = chans // 2
    mine = pl.ds(pl.multiple_of(core * half, half), half)
    other = pl.ds(pl.multiple_of((1 - core) * half, half), half)
    pair = remote(w_ref.at[:, other], recv0, pair_send.at[0], pair_recv.at[0], at(0, 0, 1))
    pair.start()

    image = img_ref[...]
    slope[...] = silu_slope(jnp.dot(image, bw_ref[...], preferred_element_type=F32))
    img_t[...] = image.T
    pair.wait()

    def add0(k, carry):
        acc0[k] = (w_ref[k, mine, :].astype(F32) + recv0[k].astype(F32)).astype(BF)
        return carry

    lax.fori_loop(0, taps, add0, 0)

    def rows64(q):
        return pl.ds(pl.multiple_of(q * 64, 64), 64)

    along_x = [
        remote(
            acc0.at[:, rows64((x + d) % 4)], recv1.at[d - 1],
            x_send.at[d - 1], x_recv.at[d - 1], at(0, 0, 0, d),
        )
        for d in (1, 2, 3)
    ]
    for copy in along_x:
        copy.start()

    for k in range(7):
        for h in range(2):
            group_copy(h, k, 1, "meta").wait_send()
            group_copy(h, k, -1, "meta").wait_recv()
    own[0].wait()
    own[2].wait()

    def make_band(n, carry):
        h, owner, member = n // 64, n // 8 % 8, n % 8
        info = meta[h, member, owner].astype(F32)
        q = lax.broadcasted_iota(jnp.int32, (IMGW, CELLS), 0).astype(F32)
        left, right = q == info[0:1], q == info[0:1] + 1.0
        zero = jnp.zeros((IMGW, CELLS), F32)
        upper = jnp.where(left, info[2:3], jnp.where(right, info[3:4], zero))
        lower = jnp.where(left, info[4:5], jnp.where(right, info[5:6], zero))
        whole = jnp.concatenate([upper, lower], axis=0)
        lanes = pl.ds(pl.multiple_of(member * CELLS, CELLS), CELLS)
        for block in range(4):
            kept = jnp.where(info[1:2] == float(block), whole, 0.0)
            band[h * 8 + owner, pl.ds(block * PIXB, PIXB), lanes] = kept.astype(BF)
        return carry

    lax.fori_loop(0, 128, make_band, 0)
    for k in range(7):
        for h in range(2):
            group_copy(h, k, 1, "slots").wait_send()
            group_copy(h, k, -1, "slots").wait_recv()
    own[1].wait()
    own[3].wait()

    def owner_of(h, x_part, d):
        q = (y + h * (z - y) + d) % 4
        return (1 - h) * (q * 2 + x_part) + h * (x_part * 4 + q)

    def second(h, x_part, d):
        far = (x_part + x_hi) % 2
        return remote(
            dense.at[h, owner_of(h, x_part, d)], land2.at[h, far, d - 1],
            p2_send.at[h, far, d - 1], p2_recv.at[h, far, d - 1],
            at((1 - h) * d, h * d, 0),
        )

    def form(x_part):
        def one(n, carry):
            h, d = n % 2, n // 2 + 1
            owner = owner_of(h, x_part, d)
            cells = land[h, :, owner].reshape(GROUP * CELLS, half)
            dense[h, owner] = jnp.dot(
                band[h * 8 + owner], cells, preferred_element_type=F32
            ).astype(BF)

            @pl.when(d < 4)
            def _():
                second(h, x_part, d).start()

            return carry

        lax.fori_loop(0, 8, one, 0)

    form(1 - x_hi)

    for copy in along_x:
        copy.wait()

    def add1(k, carry):
        total = acc0[k, rows64(x), :].astype(F32)
        for d in range(3):
            total = total + recv1[d, k].astype(F32)
        acc1[k] = total.astype(BF)
        return carry

    lax.fori_loop(0, taps, add1, 0)

    def lanes128(q):
        return pl.ds(pl.multiple_of(q * 128, 128), 128)

    def rows16(q):
        return pl.ds(pl.multiple_of(q * 16, 16), 16)

    to_plane = [
        remote(
            acc1.at[:, rows16((y + dy) % 4), lanes128((z + dz) % 4)], recv2.at[k],
            yz_send.at[k], yz_recv.at[k], at(dy, dz, 0),
        )
        for k, (dy, dz) in enumerate(plane)
    ]
    for copy in to_plane:
        copy.start()
    form(x_hi)

    def settle(far):
        for h in range(2):
            for d in (1, 2, 3):
                second(h, (far + x_hi) % 2, d).wait()

    def gathered(h, x_part, far):
        total = dense[h, owner_of(h, x_part, 0)].astype(F32)
        for d in range(3):
            total = total + land2[h, far, d].astype(F32)
        return total

    settle(1)
    third = []
    for h in range(2):
        sums[h] = gathered(h, 1 - x_hi, 1).astype(BF)
        third.append(
            remote(sums.at[h], land3.at[h], p3_send.at[h], p3_recv.at[h], at(0, 0, 0, 2))
        )
        third[h].start()

    for copy in to_plane:
        copy.wait()

    def add2(k, carry):
        total = acc1[k, rows16(y), lanes128(z)].astype(F32)
        for p in range(15):
            total = total + recv2[p, k].astype(F32)
        o_ref[k, core, x, y, :, lanes128(z)] = (total * cell_scale).astype(BF)
        return carry

    lax.fori_loop(0, taps, add2, 0)

    def spread(s, k, sign):
        p, q = plane[k]
        dy, dx, dz = ((p, 0, q), (0, p, q), (p, q, 0))[s]
        part = o_ref.at[
            pl.ds(3 * s, 3), core, (x + sign * dx + 4) % 4, (y + sign * dy + 4) % 4, :,
            lanes128((z + sign * dz + 4) % 4),
        ]
        return remote(part, part, ag_send.at[s, k], ag_recv.at[s, k], at(dy, dz, 0, dx))

    def strip(s, d, sign):
        t = pl.ds(3 * s, 3)
        if s == 0:
            part, where = o_ref.at[t, core, (x + sign * d + 4) % 4], at(0, 0, 0, d)
        elif s == 1:
            part, where = o_ref.at[t, core, :, (y + sign * d + 4) % 4], at(d, 0, 0)
        else:
            part = o_ref.at[t, core, :, :, :, lanes128((z + sign * d + 4) % 4)]
            where = at(0, d, 0)
        return remote(part, part, far_send.at[s, d - 1], far_recv.at[s, d - 1], where)

    for k in range(15):
        for s in range(3):
            spread(s, k, 0).start()

    settle(0)
    lanes_of = (pl.ds(0, 256), pl.ds(256, 256))
    for h in range(2):
        feature[:, lanes_of[h]] = gathered(h, x_hi, 0)
    for k in range(15):
        for s in range(3):
            spread(s, k, 0).wait_send()
            spread(s, k, -1).wait_recv()
    for d in (1, 2, 3):
        for s in range(3):
            strip(s, d, 0).start()

    for h in range(2):
        third[h].wait()
        feature[:, lanes_of[h]] += land3[h].astype(F32)
    scaled = (feature[...] * slope[...]).astype(BF)
    bb[...] = jnp.dot(img_t[...], scaled, preferred_element_type=F32).astype(BF)
    bb_pair = remote(bb.at[other], bb0, pair_send.at[1], pair_recv.at[1], at(0, 0, 1))
    bb_pair.start()
    ig_ref[...] = lax.dot_general(
        scaled, bw_ref[...], (((1,), (1,)), ((), ())), preferred_element_type=F32
    ).astype(BF)
    bb_pair.wait()
    bb0_acc[...] = (bb[mine, :].astype(F32) + bb0[...].astype(F32)).astype(BF)

    def place(dy, dz):
        return (y + dy + 4) % 4 * 4 + (z + dz + 4) % 4

    bb_plane = [
        remote(
            bb0_acc.at[rows16(place(dy, dz))], bb1.at[k],
            by_send.at[0, k], by_recv.at[0, k], at(dy, dz, 0),
        )
        for k, (dy, dz) in enumerate(plane)
    ]
    for copy in bb_plane:
        copy.start()
    for copy in bb_plane:
        copy.wait()
    total = bb0_acc[rows16(place(0, 0)), :].astype(F32)
    for k in range(15):
        total = total + bb1[k].astype(F32)
    bb1_acc[...] = total.astype(BF)
    bb_line = [
        remote(
            bb1_acc.at[:, lanes128((x + d) % 4)], bb2.at[d - 1],
            bx_send.at[0, d - 1], bx_recv.at[0, d - 1], at(0, 0, 0, d),
        )
        for d in (1, 2, 3)
    ]
    for copy in bb_line:
        copy.start()

    for d in (1, 2, 3):
        for s in range(3):
            strip(s, d, 0).wait_send()
            strip(s, d, -1).wait_recv()

    def back(c):
        return remote(
            o_ref.at[:, c], o_ref.at[:, c], pair_send.at[2], pair_recv.at[2], at(0, 0, 1)
        )

    back(core).start()
    for copy in bb_line:
        copy.wait()
    total = bb1_acc[:, lanes128(x)].astype(F32)
    for d in range(3):
        total = total + bb2[d].astype(F32)

    def bb_rows(dy, dz):
        return pl.ds(pl.multiple_of(core * half + place(dy, dz) * 16, 16), 16)

    bb_ref[bb_rows(0, 0), lanes128(x)] = (total * pixel_scale).astype(BF)

    def bb_strip(d, sign):
        part = bb_ref.at[bb_rows(0, 0), lanes128((x + sign * d + 4) % 4)]
        return remote(part, part, bx_send.at[1, d - 1], bx_recv.at[1, d - 1], at(0, 0, 0, d))

    def bb_spread(k, sign):
        dy, dz = plane[k]
        part = bb_ref.at[bb_rows(sign * dy, sign * dz)]
        return remote(part, part, by_send.at[1, k], by_recv.at[1, k], at(dy, dz, 0))

    def bb_back(which):
        part = bb_ref.at[which]
        return remote(part, part, pair_send.at[3], pair_recv.at[3], at(0, 0, 1))

    for d in (1, 2, 3):
        bb_strip(d, 0).start()
    for d in (1, 2, 3):
        bb_strip(d, 0).wait_send()
        bb_strip(d, -1).wait_recv()
    for k in range(15):
        bb_spread(k, 0).start()
    for k in range(15):
        bb_spread(k, 0).wait_send()
        bb_spread(k, -1).wait_recv()
    bb_back(mine).start()
    back(core).wait_send()
    back(1 - core).wait_recv()
    bb_back(mine).wait_send()
    bb_back(other).wait_recv()


def exchange_all(cell_scale, pixel_scale, slots, meta, g, act, a_lo, a_hi, image, weight):
    chans = image.shape[1]
    half = chans // 2
    wide = chans // 2
    taps = 9
    dma = pltpu.SemaphoreType.DMA
    vmem = pltpu.VMEM
    pixels = image.shape[0]
    return pl.pallas_call(
        functools.partial(exchange_kernel, cell_scale, pixel_scale),
        out_shape=[
            jax.ShapeDtypeStruct((pixels, chans), BF),
            jax.ShapeDtypeStruct((taps, 2, 4, 4, 16, chans), BF),
            jax.ShapeDtypeStruct((chans, chans), BF),
        ],
        in_specs=[HBM] * 7 + [VMEM, VMEM],
        out_specs=[VMEM, VMEM, VMEM],
        scratch_shapes=[
            vmem((2, GROUP, GROUP, CELLS, wide), BF),
            vmem((2, GROUP, GROUP, 16, CELLS), BF),
            vmem((2 * GROUP, NPIX, GROUP * CELLS), BF),
            vmem((2, GROUP, NPIX, wide), BF),
            vmem((2, 2, 3, NPIX, wide), BF),
            vmem((2, NPIX, wide), BF),
            vmem((2, NPIX, wide), BF),
            vmem((taps, chans, chans), BF),
            vmem((taps, half, chans), BF),
            vmem((taps, half, chans), BF),
            vmem((3, taps, 64, chans), BF),
            vmem((taps, 64, chans), BF),
            vmem((15, taps, 16, 128), BF),
            vmem((a_lo.shape[0] * 64 + 16, chans), F32),
            vmem((pixels, chans), F32),
            vmem((pixels, chans), F32),
            vmem((chans, pixels), BF),
            vmem((chans, chans), BF),
            vmem((half, chans), BF),
            vmem((half, chans), BF),
            vmem((15, 16, chans), BF),
            vmem((16, chans), BF),
            vmem((3, 16, 128), BF),
            dma((21,)), dma((2, 7)), dma((2, 7)), dma((2, 7)), dma((2, 7)), dma((2, 2)),
            dma((2, 2, 3)), dma((2, 2, 3)), dma((2,)), dma((2,)),
            dma((4,)), dma((4,)), dma((3,)), dma((3,)), dma((15,)), dma((15,)),
            dma((3, 15)), dma((3, 15)), dma((3, 3)), dma((3, 3)),
            dma((2, 15)), dma((2, 15)), dma((2, 3)), dma((2, 3)),
        ],
        compiler_params=pltpu.CompilerParams(
            collective_id=0, has_side_effects=True, vmem_limit_bytes=63 << 20
        ),
        name="exchange_all",
    )(*slots, meta, g, act, a_lo, a_hi, image, weight)


def edge_rows(block):
    count = lax.axis_size("tile")
    forward = [(i, i + 1) for i in range(count - 1)]
    backward = [(target, source) for source, target in forward]
    return lax.ppermute(block[-1:], "tile", forward), lax.ppermute(block[:1], "tile", backward)


def body(grad_out, bev_act, conv_weight, img_in, backbone_weight, route, offsets, frac_x, frac_y):
    my_tile = lax.axis_index("tile")
    g, act, image = grad_out[0], bev_act[0], img_in[0]
    rows, cols, chans = g.shape
    g_lo, g_hi = edge_rows(g)
    a_lo, a_hi = edge_rows(act)
    blocks = rows * cols // BLK
    per_device = image.shape[0] // PIXB

    owners = (route[0] // per_device).reshape(TILES, blocks)
    local_ids = (route[0] % per_device).reshape(TILES, blocks)
    my_owners = lax.dynamic_index_in_dim(owners, my_tile, 0, keepdims=False)
    same = my_owners[:, None] == my_owners[None, :]
    before = lax.broadcasted_iota(jnp.int32, (blocks, blocks), 1) < lax.broadcasted_iota(
        jnp.int32, (blocks, blocks), 0
    )
    my_slots = my_owners * CAP + jnp.sum((same & before).astype(jnp.int32), axis=1)
    chosen = my_slots[None, :] == lax.broadcasted_iota(jnp.int32, (TILES * CAP, blocks), 0)
    idx = jnp.sum(
        jnp.where(chosen, lax.broadcasted_iota(jnp.int32, chosen.shape, 1), 0), axis=1
    )
    right_w = frac_x[0].astype(F32) / 256.0
    lower_w = frac_y[0].astype(F32) / 256.0
    cells = jnp.stack(
        [
            offsets[0].astype(F32),
            (1.0 - lower_w) * (1.0 - right_w),
            (1.0 - lower_w) * right_w,
            lower_w * (1.0 - right_w),
            lower_w * right_w,
        ]
    )
    cells = cells.astype(BF).reshape(5, blocks, BLK)
    info = jnp.einsum("sk,rkm->srm", chosen.astype(BF), cells, preferred_element_type=F32)
    my_local = lax.dynamic_index_in_dim(local_ids, my_tile, 0, keepdims=False)
    held = jnp.sum(jnp.where(chosen, my_local[None, :] + 1, 0), axis=1) - 1
    held = jnp.broadcast_to(held.astype(F32)[:, None, None], (TILES * CAP, 1, BLK))
    info = jnp.concatenate([info[:, :1], held, info[:, 1:]], axis=1).astype(BF)
    info = info.reshape(TILES, CAP, 6, BLK).transpose(0, 2, 1, 3).reshape(TILES, 6, CELLS)
    info = jnp.pad(info, ((0, 0), (0, 10), (0, 0)))
    by_z = info.reshape(8, 8, 16, CELLS)
    by_y = info.reshape(4, 8, 2, 16, CELLS).transpose(1, 0, 2, 3, 4).reshape(8, 8, 16, CELLS)
    meta = jnp.stack([by_z, by_y])

    weights = conv_weight.transpose(1, 2, 0, 3).reshape(9, chans, chans)
    slot_z, slot_y = bev_slots(idx, g, g_lo[0], g_hi[0], weights)
    slot_z = slot_z.reshape(8, 8, CELLS, chans // 2)
    slot_y = slot_y.reshape(4, 8, 2, CELLS, chans // 2)

    cell_scale = 1.0 / math.sqrt(2 * TILES * rows * cols)
    pixel_scale = 1.0 / math.sqrt(2 * TILES * image.shape[0])
    image_grad, conv_sum, backbone_grad = exchange_all(
        cell_scale,
        pixel_scale,
        (slot_z, slot_y),
        meta,
        g.reshape(rows * cols, chans),
        act.reshape(-1, 4, 16, chans),
        a_lo.reshape(-1, 4, 16, chans),
        a_hi.reshape(-1, 4, 16, chans),
        image,
        backbone_weight,
    )
    conv_grad = conv_sum.reshape(3, 3, chans, chans).transpose(2, 0, 1, 3)
    return (image_grad[None], conv_grad, backbone_grad)


def solution(mesh):
    return jax.shard_map(
        body,
        mesh=mesh,
        in_specs=(
            P("dp", "tile", None, None),
            P("dp", "tile", None, None),
            P(),
            P("dp", "tile", None),
            P(),
            P("dp", None),
            P("dp", "tile"),
            P("dp", "tile"),
            P("dp", "tile"),
        ),
        out_specs=(P("dp", "tile", None), P(), P()),
        check_vma=False,
    )
```

```python
import functools
import math

import jax
import jax.numpy as jnp
from jax import lax
from jax.experimental import pallas as pl
from jax.experimental.pallas import tpu as pltpu
from jax.sharding import PartitionSpec as P

BLK = 64
IMGW = 64
PIXB = 2 * IMGW
TILES = 64
CAP = 2
MESH = pl.DeviceIdType.MESH
ANY = pl.BlockSpec(memory_space=pl.ANY)
VMEM = pl.BlockSpec(memory_space=pltpu.VMEM)
SMEM = pl.BlockSpec(memory_space=pltpu.SMEM)
HBM = pl.BlockSpec(memory_space=pltpu.HBM)
BF = jnp.bfloat16
F32 = jnp.float32


def coords():
    t = lax.axis_index("tile")
    return t // 16, (t // 8) % 2 * 2 + lax.axis_index("dp"), (t // 2) % 4, t % 2


def device(y, x, z, core):
    return (x % 2, ((y * 2 + x // 2) * 4 + z) * 2 + core)


def along(axis, step):
    y, x, z, core = coords()
    if axis == "y":
        y = (y + step) % 4
    elif axis == "x":
        x = (x + step) % 4
    elif axis == "z":
        z = (z + step) % 4
    else:
        core = 1 - core
    return device(y, x, z, core)


NPIX = 4 * PIXB
CELLS = CAP * BLK
GROUP = 8


def silu_slope(value):
    sigma = jax.nn.sigmoid(value)
    return sigma * (1.0 + value * (1.0 - sigma))


def exchange_kernel(
    cell_scale, pixel_scale,
    idx_ref, m_ref, g_ref, a_ref, cw_ref, img_ref, bw_ref,
    ig_ref, o_ref, bb_ref,
    land, meta, band, dense, slots1, land2, sums, land3, w_ref, recv0, recv1, acc1, recv2,
    edges, shift, slope, img_t, bb0, bb1, bb1_acc, bb2,
    in_sem, e_send, e_recv, m_send, m_recv, p1_send, p1_recv, own_sem, p2_send, p2_recv, p3_send, p3_recv,
    pair_send, pair_recv, x_send, x_recv, yz_send, yz_recv, ag_send, ag_recv, far_send, far_recv,
    by_send, by_recv, bx_send, bx_recv,
):
    y, x, z, core = coords()
    x_hi = x // 2
    taps, chans = w_ref.shape[0], w_ref.shape[3]
    cols = edges.shape[1]
    rows = g_ref.shape[0] // cols
    half = chans // 2
    dp, tile = lax.axis_index("dp"), lax.axis_index("tile")

    def remote(src, dst, sends, recvs, where):
        return pltpu.make_async_remote_copy(
            src_ref=src, dst_ref=dst, send_sem=sends, recv_sem=recvs,
            device_id=where, device_id_type=MESH,
        )

    plane = [(p, q) for p in range(4) for q in range(4) if p or q]
    corner = [(p, q) for p, q in plane if p and q]

    def at(dy, dz, dc, dx=0):
        return device((y + dy) % 4, (x + dx) % 4, (z + dz) % 4, (core + dc) % 2)

    barrier = pltpu.get_barrier_semaphore()
    greeted = [at(0, 0, 1)] + [at(dy, dz, 0) for dy, dz in plane]
    greeted += [at(dy, dz, 1) for dy, dz in plane if not (dy and dz)]
    greeted += [at(0, 0, 0, d) for d in (1, 2, 3)]
    greeted += [at(p, 0, 0, q) for p, q in corner] + [at(0, p, 0, q) for p, q in corner]
    below, above = (dp, (tile + TILES - 1) % TILES), (dp, (tile + 1) % TILES)
    has_below, has_above = tile > 0, tile < TILES - 1
    greeted += [below, above]
    for where in greeted:
        pl.semaphore_signal(barrier, inc=1, device_id=where, device_id_type=MESH)

    def unit(n):
        return n // 2, pl.ds(pl.multiple_of(n % 2 * 512, 512), 512)

    def moved(j, r, n):
        b = j * 5 * (rows + 2) + r * 5 + n
        slot, lanes = unit(b // 4)
        return slot, pl.ds(pl.multiple_of(b % 4 * 128, 128), 128), lanes

    first_weight = 23

    loads = []
    for k in range(taps):
        slot, lanes = unit(first_weight + k)
        loads.append(pltpu.make_async_copy(cw_ref.at[k], band.at[slot, :, lanes], in_sem.at[k]))
    loads += [
        pltpu.make_async_copy(
            a_ref.at[pl.ds(4 * u, 4)], o_ref.at[u // 2, u % 2], in_sem.at[taps + u]
        )
        for u in range(10)
    ]

    def load_gradient(b, carry):
        pltpu.make_async_copy(
            g_ref.at[pl.ds(pl.multiple_of(b * 128, 128), 128)],
            band.at[moved(1, 1 + b // 5, b % 5)], in_sem.at[19],
        ).start()
        return carry

    lax.fori_loop(0, 5 * rows, load_gradient, 0)
    for copy in loads:
        copy.start()

    pl.semaphore_wait(barrier, len(greeted))

    def edge_copies(up, where):
        side = 0 if up else 1
        row = pl.ds((rows - 1) * cols if up else 0, cols)
        copies = [
            remote(g_ref.at[row], edges.at[side], e_send.at[side, 0], e_recv.at[side, 0], where)
        ]
        for u in range(3):
            size = 4 if u < 2 else 2
            copies.append(
                remote(
                    a_ref.at[pl.ds((10 * (rows - 1) if up else 0) + 4 * u, size)],
                    o_ref.at[5 + 2 * side + u // 2, u % 2, pl.ds(0, size)],
                    e_send.at[side, 1 + u], e_recv.at[side, 1 + u], where,
                )
            )
        return copies

    @pl.when(has_above)
    def _():
        for copy in edge_copies(True, above):
            copy.start()

    @pl.when(has_below)
    def _():
        for copy in edge_copies(False, below):
            copy.start()

    edge = jnp.zeros((8, half), F32)
    shift[pl.ds(0, 8), :] = edge
    shift[pl.ds(cols + 8, 8), :] = edge

    def move(r, carry):
        for part in (slice(0, half), slice(half, chans)):

            def block(j, n):
                slot, places, lanes = moved(j, r, n)
                start = pl.multiple_of(lanes.start + part.start, half)
                return slot, places, pl.ds(start, half)

            for n in range(5):
                shift[pl.ds(8 + n * 128, 128), :] = band[block(1, n)].astype(F32)
            for n in range(5):
                band[block(0, n)] = shift[pl.ds(9 + n * 128, 128), :].astype(BF)
                band[block(2, n)] = shift[pl.ds(7 + n * 128, 128), :].astype(BF)
        return carry

    pltpu.make_async_copy(g_ref, g_ref, in_sem.at[19]).wait()
    lax.fori_loop(1, rows + 1, move, 0)

    def arrive(side, up, present):
        @pl.when(present)
        def _():
            for copy in edge_copies(up, below if up else above):
                copy.wait_recv()

        @pl.when(jnp.logical_not(present))
        def _():
            edges[side] = jnp.zeros((cols, chans), BF)
            nothing = jnp.zeros((4, 16, chans), BF)
            for u in range(10):
                o_ref[5 + 2 * side + u // 8, u // 4 % 2, u % 4] = nothing

        r = 0 if side == 0 else rows + 1
        for n in range(5):
            band[moved(1, r, n)] = edges[side, pl.ds(n * 128, 128), :]
        move(r, 0)

    arrive(0, True, has_below)
    arrive(1, False, has_above)
    for copy in loads:
        copy.wait()

    def ground(s, carry):
        r, n = s // 2, s % 2
        out = None
        for i in range(3):
            left, right = [], []
            for j in range(3):
                left.append(
                    jnp.concatenate([band[moved(j, r + 2 - i, m)] for m in range(5)], axis=0)
                )
                slot, lanes = unit(first_weight + 3 * i + j)
                right.append(band[slot, pl.ds(pl.multiple_of(n * half, half), half), lanes])
            term = lax.dot_general(
                jnp.concatenate(left, axis=1), jnp.concatenate(right, axis=1),
                (((1,), (1,)), ((), ())), preferred_element_type=F32,
            )
            out = term if out is None else out + term
        out = out.astype(BF)
        lanes = pl.ds(pl.multiple_of(n * half, half), half)
        for m in range(10):
            k = r * 10 + m
            w_ref[k // 8, k % 8, :, lanes] = out[m * BLK : (m + 1) * BLK]
        return carry

    lax.fori_loop(0, 2 * rows, ground, 0)

    def fill(s, carry):
        block = w_ref[idx_ref[0, s], idx_ref[1, s]]
        place = pl.ds(pl.multiple_of(s % CAP * BLK, BLK), BLK)
        o = s // CAP
        dense[o // 8, o % 8, place, :] = block[:, :half]
        slots1[o // 16, o // 2 % 8, o % 2, place, :] = block[:, half:]
        return carry

    lax.fori_loop(0, TILES * CAP, fill, 0)

    line = (z, y)
    here = [line[h] * 2 + core for h in range(2)]

    def slots_of(h, member):
        if h == 0:
            return dense.at[:, member]
        return slots1.at[member // 2, :, member % 2]

    def info_of(h, member):
        return m_ref.at[h, :, member]

    steps = [(d, dc) for d in range(4) for dc in range(2) if d or dc]

    def group_copy(h, k, sign, which):
        d, dc = steps[k]
        member = (line[h] + (d if sign > 0 else 4 - d)) % 4 * 2 + (core + dc) % 2
        where = at(0, d, dc) if h == 0 else at(d, 0, dc)
        place = here[h] if sign > 0 else member
        if which == "meta":
            return remote(
                info_of(h, member), meta.at[h, place], m_send.at[h, k], m_recv.at[h, k], where
            )
        return remote(
            slots_of(h, member), land.at[h, place], p1_send.at[h, k], p1_recv.at[h, k], where
        )

    own = []
    for h in range(2):
        own.append(
            pltpu.make_async_copy(info_of(h, here[h]), meta.at[h, here[h]], own_sem.at[h, 0])
        )
        own.append(
            pltpu.make_async_copy(slots_of(h, here[h]), land.at[h, here[h]], own_sem.at[h, 1])
        )
    for copy in own:
        copy.start()
    for which in ("meta", "slots"):
        for k in range(7):
            for h in range(2):
                group_copy(h, k, 1, which).start()

    def column(u):
        n = first_weight + u // 4
        return n // 2, pl.ds(pl.multiple_of(n % 2 * 512 + u % 4 * 128, 128), 128)

    def turn(u, piece, start):
        block = o_ref[piece, start // 256, pl.ds(start // 64 % 4, 2)].reshape(128, chans)
        slot, lanes = column(u)
        band[slot, :, lanes] = block.T

    def turn_inner(n, carry):
        turn(5 + n, n // 4, n % 4 * 128)
        return carry

    lax.fori_loop(0, 5 * rows, turn_inner, 0)
    for side in range(2):
        for n in range(5):
            turn(5 * (rows + 1) * side + n, 5 + 2 * side + n // 4, n % 4 * 128)

    def tap(n, carry):
        i, j = n // 3, n % 3
        left = []
        for m in range(5 * rows):
            slot, lanes = column(5 * i + m)
            left.append(band[slot, :, lanes])
        right = [band[moved(j, 1 + m // 5, m % 5)] for m in range(5 * rows)]
        w_ref[n] = jnp.dot(
            jnp.concatenate(left, axis=1), jnp.concatenate(right, axis=0),
            preferred_element_type=F32,
        ).astype(BF).reshape(w_ref.shape[1:])
        return carry

    mine, other = pl.ds(core * 4, 4), pl.ds((1 - core) * 4, 4)

    def pair(k):
        t = pl.ds(3 * k, 3)
        return remote(
            w_ref.at[t, other], recv0.at[t], pair_send.at[4 + k], pair_recv.at[4 + k], at(0, 0, 1)
        )

    def along_x(k, d):
        t = pl.ds(3 * k, 3)
        return remote(
            w_ref.at[t, core * 4 + (x + d) % 4], recv1.at[d - 1, t],
            x_send.at[k, d - 1], x_recv.at[k, d - 1], at(0, 0, 0, d),
        )

    def add0(k, carry):
        w_ref[k, mine] = (w_ref[k, mine].astype(F32) + recv0[k].astype(F32)).astype(BF)
        return carry

    def pass_on(k):
        pair(k).wait()
        lax.fori_loop(3 * k, 3 * k + 3, add0, 0)
        for d in (1, 2, 3):
            along_x(k, d).start()

    for k in range(3):
        lax.fori_loop(3 * k, 3 * k + 3, tap, 0)
        pair(k).start()
        if k > 0:
            pass_on(k - 1)

    image = img_ref[...]
    slope[...] = silu_slope(jnp.dot(image, bw_ref[...], preferred_element_type=F32))
    img_t[...] = image.T
    pass_on(2)

    for k in range(7):
        for h in range(2):
            group_copy(h, k, 1, "meta").wait_send()
            group_copy(h, k, -1, "meta").wait_recv()
    own[0].wait()
    own[2].wait()

    def make_band(n, carry):
        h, owner, member = n // 64, n // 8 % 8, n % 8
        info = meta[h, member, owner].astype(F32)
        q = lax.broadcasted_iota(jnp.int32, (IMGW, CELLS), 0).astype(F32)
        left, right = q == info[0:1], q == info[0:1] + 1.0
        zero = jnp.zeros((IMGW, CELLS), F32)
        upper = jnp.where(left, info[2:3], jnp.where(right, info[3:4], zero))
        lower = jnp.where(left, info[4:5], jnp.where(right, info[5:6], zero))
        whole = jnp.concatenate([upper, lower], axis=0)
        lanes = pl.ds(pl.multiple_of(member * CELLS, CELLS), CELLS)
        for block in range(4):
            kept = jnp.where(info[1:2] == float(block), whole, 0.0)
            band[h * 8 + owner, pl.ds(block * PIXB, PIXB), lanes] = kept.astype(BF)
        return carry

    lax.fori_loop(0, 128, make_band, 0)

    for k in range(3):
        for d in (1, 2, 3):
            along_x(k, d).wait()

    def add1(k, carry):
        total = w_ref[k, core * 4 + x].astype(F32)
        for d in range(3):
            total = total + recv1[d, k].astype(F32)
        acc1[k] = total.astype(BF)
        return carry

    lax.fori_loop(0, taps, add1, 0)

    def lanes128(q):
        return pl.ds(pl.multiple_of(q * 128, 128), 128)

    def rows16(q):
        return pl.ds(pl.multiple_of(q * 16, 16), 16)

    to_plane = [
        remote(
            acc1.at[:, rows16((y + dy) % 4), lanes128((z + dz) % 4)], recv2.at[k],
            yz_send.at[k], yz_recv.at[k], at(dy, dz, 0),
        )
        for k, (dy, dz) in enumerate(plane)
    ]
    for copy in to_plane:
        copy.start()
    for k in range(7):
        for h in range(2):
            group_copy(h, k, 1, "slots").wait_send()
            group_copy(h, k, -1, "slots").wait_recv()
    own[1].wait()
    own[3].wait()

    def owner_of(h, x_part, d):
        q = (y + h * (z - y) + d) % 4
        return (1 - h) * (q * 2 + x_part) + h * (x_part * 4 + q)

    def owner_part(h, x_part, d):
        owner = owner_of(h, x_part, d)
        return h * 4 + owner // 2, pl.ds(owner % 2 * 4, 4)

    def second(h, x_part, d):
        far = (x_part + x_hi) % 2
        return remote(
            dense.at[owner_part(h, x_part, d)], land2.at[h, far, d - 1],
            p2_send.at[h, far, d - 1], p2_recv.at[h, far, d - 1],
            at((1 - h) * d, h * d, 0),
        )

    def form(x_part):
        def one(n, carry):
            h, d = n % 2, n // 2 + 1
            owner = owner_of(h, x_part, d)
            cells = land[h, :, owner].reshape(GROUP * CELLS, half)
            dense[owner_part(h, x_part, d)] = (
                jnp.dot(band[h * 8 + owner], cells, preferred_element_type=F32)
                .astype(BF)
                .reshape(4, PIXB, half)
            )

            @pl.when(d < 4)
            def _():
                second(h, x_part, d).start()

            return carry

        lax.fori_loop(0, 8, one, 0)

    form(1 - x_hi)

    for copy in to_plane:
        copy.wait()

    def add2(k, carry):
        total = acc1[k, rows16(y), lanes128(z)].astype(F32)
        for p in range(15):
            total = total + recv2[p, k].astype(F32)
        o_ref[k, core, x, y, :, lanes128(z)] = (total * cell_scale).astype(BF)
        return carry

    lax.fori_loop(0, taps, add2, 0)

    def spread(s, k, sign):
        p, q = plane[k]
        dy, dx, dz = ((p, 0, q), (0, p, q), (p, q, 0))[s]
        part = o_ref.at[
            pl.ds(3 * s, 3), core, (x + sign * dx + 4) % 4, (y + sign * dy + 4) % 4, :,
            lanes128((z + sign * dz + 4) % 4),
        ]
        return remote(part, part, ag_send.at[s, k], ag_recv.at[s, k], at(dy, dz, 0, dx))

    def strip(s, d, sign):
        t = pl.ds(3 * s, 3)
        if s == 0:
            part, where = o_ref.at[t, core, (x + sign * d + 4) % 4], at(0, 0, 0, d)
        elif s == 1:
            part, where = o_ref.at[t, core, :, (y + sign * d + 4) % 4], at(d, 0, 0)
        else:
            part = o_ref.at[t, core, :, :, :, lanes128((z + sign * d + 4) % 4)]
            where = at(0, d, 0)
        return remote(part, part, far_send.at[s, d - 1], far_recv.at[s, d - 1], where)

    for k in range(15):
        for s in range(3):
            spread(s, k, 0).start()

    form(x_hi)

    def settle(far):
        for h in range(2):
            for d in (1, 2, 3):
                second(h, (far + x_hi) % 2, d).wait()

    def gathered(h, x_part, far):
        total = dense[owner_part(h, x_part, 0)].astype(F32)
        for d in range(3):
            total = total + land2[h, far, d].astype(F32)
        return total.reshape(NPIX, half)

    settle(1)
    third = []
    for h in range(2):
        sums[h] = gathered(h, 1 - x_hi, 1).astype(BF)
        third.append(
            remote(sums.at[h], land3.at[h], p3_send.at[h], p3_recv.at[h], at(0, 0, 0, 2))
        )
        third[h].start()

    for k in range(15):
        for s in range(3):
            spread(s, k, 0).wait_send()
            spread(s, k, -1).wait_recv()
    for d in (1, 2, 3):
        for s in range(3):
            strip(s, d, 0).start()

    settle(0)

    scaled = []
    for h in range(2):
        third[h].wait()
        feature = gathered(h, x_hi, 0) + land3[h].astype(F32)
        scaled.append((feature * slope[:, h * half : (h + 1) * half]).astype(BF))
    scaled = jnp.concatenate(scaled, axis=1)
    part = jnp.dot(img_t[...], scaled, preferred_element_type=F32).astype(BF)
    w_ref[0] = part.reshape(w_ref.shape[1:])
    bb_pair = remote(w_ref.at[0, other], bb0, pair_send.at[1], pair_recv.at[1], at(0, 0, 1))
    bb_pair.start()
    ig_ref[...] = lax.dot_general(
        scaled, bw_ref[...], (((1,), (1,)), ((), ())), preferred_element_type=F32
    ).astype(BF)
    bb_pair.wait()
    w_ref[1, pl.ds(0, 4)] = (w_ref[0, mine].astype(F32) + bb0[...].astype(F32)).astype(BF)

    def place(dy, dz):
        return (y + dy + 4) % 4 * 4 + (z + dz + 4) % 4

    bb_plane = [
        remote(
            w_ref.at[1, place(dy, dz) // 4, rows16(place(dy, dz) % 4)], bb1.at[k],
            by_send.at[0, k], by_recv.at[0, k], at(dy, dz, 0),
        )
        for k, (dy, dz) in enumerate(plane)
    ]
    for copy in bb_plane:
        copy.start()
    for copy in bb_plane:
        copy.wait()
    total = w_ref[1, y, rows16(z), :].astype(F32)
    for k in range(15):
        total = total + bb1[k].astype(F32)
    bb1_acc[...] = total.astype(BF)
    bb_line = [
        remote(
            bb1_acc.at[:, lanes128((x + d) % 4)], bb2.at[d - 1],
            bx_send.at[0, d - 1], bx_recv.at[0, d - 1], at(0, 0, 0, d),
        )
        for d in (1, 2, 3)
    ]
    for copy in bb_line:
        copy.start()

    for d in (1, 2, 3):
        for s in range(3):
            strip(s, d, 0).wait_send()
            strip(s, d, -1).wait_recv()

    def back(c):
        return remote(
            o_ref.at[:, c], o_ref.at[:, c], pair_send.at[2], pair_recv.at[2], at(0, 0, 1)
        )

    back(core).start()
    for copy in bb_line:
        copy.wait()
    total = bb1_acc[:, lanes128(x)].astype(F32)
    for d in range(3):
        total = total + bb2[d].astype(F32)

    def bb_rows(dy, dz):
        return pl.ds(pl.multiple_of(core * half + place(dy, dz) * 16, 16), 16)

    bb_ref[bb_rows(0, 0), lanes128(x)] = (total * pixel_scale).astype(BF)

    def bb_strip(d, sign):
        part = bb_ref.at[bb_rows(0, 0), lanes128((x + sign * d + 4) % 4)]
        return remote(part, part, bx_send.at[1, d - 1], bx_recv.at[1, d - 1], at(0, 0, 0, d))

    def bb_spread(k, sign):
        dy, dz = plane[k]
        part = bb_ref.at[bb_rows(sign * dy, sign * dz)]
        return remote(part, part, by_send.at[1, k], by_recv.at[1, k], at(dy, dz, 0))

    def bb_half(c):
        return pl.ds(pl.multiple_of(c * half, half), half)

    def bb_back(which):
        part = bb_ref.at[which]
        return remote(part, part, pair_send.at[3], pair_recv.at[3], at(0, 0, 1))

    for d in (1, 2, 3):
        bb_strip(d, 0).start()
    for d in (1, 2, 3):
        bb_strip(d, 0).wait_send()
        bb_strip(d, -1).wait_recv()
    for k in range(15):
        bb_spread(k, 0).start()
    for k in range(15):
        bb_spread(k, 0).wait_send()
        bb_spread(k, -1).wait_recv()
    bb_back(bb_half(core)).start()
    back(core).wait_send()
    back(1 - core).wait_recv()
    bb_back(bb_half(core)).wait_send()
    bb_back(bb_half(1 - core)).wait_recv()

    @pl.when(has_above)
    def _():
        for copy in edge_copies(True, above):
            copy.wait_send()

    @pl.when(has_below)
    def _():
        for copy in edge_copies(False, below):
            copy.wait_send()


def exchange_all(cell_scale, pixel_scale, idx, meta, g, act, kernel, image, weight):
    chans = image.shape[1]
    half = chans // 2
    taps = kernel.shape[0]
    cols = 640
    dma = pltpu.SemaphoreType.DMA
    vmem = pltpu.VMEM
    pixels = image.shape[0]
    return pl.pallas_call(
        functools.partial(exchange_kernel, cell_scale, pixel_scale),
        out_shape=[
            jax.ShapeDtypeStruct((pixels, chans), BF),
            jax.ShapeDtypeStruct((taps, 2, 4, 4, 16, chans), BF),
            jax.ShapeDtypeStruct((chans, chans), BF),
        ],
        in_specs=[SMEM] + [HBM] * 4 + [VMEM, VMEM],
        out_specs=[VMEM, VMEM, VMEM],
        scratch_shapes=[
            vmem((2, GROUP, GROUP, CELLS, half), BF),
            vmem((2, GROUP, GROUP, 16, CELLS), BF),
            vmem((2 * GROUP, NPIX, GROUP * CELLS), BF),
            vmem((8, 8, CELLS, half), BF),
            vmem((4, 8, 2, CELLS, half), BF),
            vmem((2, 2, 3, 4, PIXB, half), BF),
            vmem((2, NPIX, half), BF),
            vmem((2, NPIX, half), BF),
            vmem((taps, 8, BLK, chans), BF),
            vmem((taps, 4, BLK, chans), BF),
            vmem((3, taps, 64, chans), BF),
            vmem((taps, 64, chans), BF),
            vmem((15, taps, 16, 128), BF),
            vmem((2, cols, chans), BF),
            vmem((cols + 16, half), F32),
            vmem((pixels, chans), F32),
            vmem((chans, pixels), BF),
            vmem((4, BLK, chans), BF),
            vmem((15, 16, chans), BF),
            vmem((16, chans), BF),
            vmem((3, 16, 128), BF),
            dma((20,)), dma((2, 4)), dma((2, 4)),
            dma((2, 7)), dma((2, 7)), dma((2, 7)), dma((2, 7)), dma((2, 2)),
            dma((2, 2, 3)), dma((2, 2, 3)), dma((2,)), dma((2,)),
            dma((7,)), dma((7,)), dma((3, 3)), dma((3, 3)), dma((15,)), dma((15,)),
            dma((3, 15)), dma((3, 15)), dma((3, 3)), dma((3, 3)),
            dma((2, 15)), dma((2, 15)), dma((2, 3)), dma((2, 3)),
        ],
        compiler_params=pltpu.CompilerParams(
            collective_id=0, has_side_effects=True, vmem_limit_bytes=67043328
        ),
        name="exchange_all",
    )(idx, meta, g, act, kernel, image, weight)


def body(grad_out, bev_act, conv_weight, img_in, backbone_weight, route, offsets, frac_x, frac_y):
    my_tile = lax.axis_index("tile")
    g, act, image = grad_out[0], bev_act[0], img_in[0]
    rows, cols, chans = g.shape
    blocks = rows * cols // BLK
    per_device = image.shape[0] // PIXB

    owners = (route[0] // per_device).reshape(TILES, blocks)
    local_ids = (route[0] % per_device).reshape(TILES, blocks)
    my_owners = lax.dynamic_index_in_dim(owners, my_tile, 0, keepdims=False)
    same = my_owners[:, None] == my_owners[None, :]
    before = lax.broadcasted_iota(jnp.int32, (blocks, blocks), 1) < lax.broadcasted_iota(
        jnp.int32, (blocks, blocks), 0
    )
    my_slots = my_owners * CAP + jnp.sum((same & before).astype(jnp.int32), axis=1)
    chosen = my_slots[None, :] == lax.broadcasted_iota(jnp.int32, (TILES * CAP, blocks), 0)
    idx = jnp.sum(
        jnp.where(chosen, lax.broadcasted_iota(jnp.int32, chosen.shape, 1), 0), axis=1
    )
    right_w = frac_x[0].astype(F32) / 256.0
    lower_w = frac_y[0].astype(F32) / 256.0
    cells = jnp.stack(
        [
            offsets[0].astype(F32),
            (1.0 - lower_w) * (1.0 - right_w),
            (1.0 - lower_w) * right_w,
            lower_w * (1.0 - right_w),
            lower_w * right_w,
        ]
    )
    cells = cells.astype(BF).reshape(5, blocks, BLK)
    info = jnp.einsum("sk,rkm->srm", chosen.astype(BF), cells, preferred_element_type=F32)
    my_local = lax.dynamic_index_in_dim(local_ids, my_tile, 0, keepdims=False)
    held = jnp.sum(jnp.where(chosen, my_local[None, :] + 1, 0), axis=1) - 1
    held = jnp.broadcast_to(held.astype(F32)[:, None, None], (TILES * CAP, 1, BLK))
    info = jnp.concatenate([info[:, :1], held, info[:, 1:]], axis=1).astype(BF)
    info = info.reshape(TILES, CAP, 6, BLK).transpose(0, 2, 1, 3).reshape(TILES, 6, CELLS)
    info = jnp.pad(info, ((0, 0), (0, 10), (0, 0)))
    by_z = info.reshape(8, 8, 16, CELLS)
    by_y = info.reshape(4, 8, 2, 16, CELLS).transpose(1, 0, 2, 3, 4).reshape(8, 8, 16, CELLS)
    meta = jnp.stack([by_z, by_y])

    weights = conv_weight.transpose(1, 2, 0, 3).reshape(9, chans, chans)
    cell_scale = 1.0 / math.sqrt(2 * TILES * rows * cols)
    pixel_scale = 1.0 / math.sqrt(2 * TILES * image.shape[0])
    image_grad, conv_sum, backbone_grad = exchange_all(
        cell_scale,
        pixel_scale,
        jnp.stack([idx // 8, idx % 8]),
        meta,
        g.reshape(rows * cols, chans),
        act.reshape(-1, 4, 16, chans),
        weights,
        image,
        backbone_weight,
    )
    conv_grad = conv_sum.reshape(3, 3, chans, chans).transpose(2, 0, 1, 3)
    return (image_grad[None], conv_grad, backbone_grad)


def solution(mesh):
    return jax.shard_map(
        body,
        mesh=mesh,
        in_specs=(
            P("dp", "tile", None, None),
            P("dp", "tile", None, None),
            P(),
            P("dp", "tile", None),
            P(),
            P("dp", None),
            P("dp", "tile"),
            P("dp", "tile"),
            P("dp", "tile"),
        ),
        out_specs=(P("dp", "tile", None), P(), P()),
        check_vma=False,
    )
```

```python
import functools
import math

import jax
import jax.numpy as jnp
from jax import lax
from jax.experimental import pallas as pl
from jax.experimental.pallas import tpu as pltpu
from jax.sharding import PartitionSpec as P

BLK = 64
IMGW = 64
PIXB = 2 * IMGW
TILES = 64
CAP = 2
UP = 256.0
MESH = pl.DeviceIdType.MESH
ANY = pl.BlockSpec(memory_space=pl.ANY)
VMEM = pl.BlockSpec(memory_space=pltpu.VMEM)
SMEM = pl.BlockSpec(memory_space=pltpu.SMEM)
HBM = pl.BlockSpec(memory_space=pltpu.HBM)
BF = jnp.bfloat16
F32 = jnp.float32


def coords():
    t = lax.axis_index("tile")
    return t // 16, (t // 8) % 2 * 2 + lax.axis_index("dp"), (t // 2) % 4, t % 2


def device(y, x, z, core):
    return (x % 2, ((y * 2 + x // 2) * 4 + z) * 2 + core)


def along(axis, step):
    y, x, z, core = coords()
    if axis == "y":
        y = (y + step) % 4
    elif axis == "x":
        x = (x + step) % 4
    elif axis == "z":
        z = (z + step) % 4
    else:
        core = 1 - core
    return device(y, x, z, core)


NPIX = 4 * PIXB
CELLS = CAP * BLK
GROUP = 8


def silu_slope(value):
    sigma = jax.nn.sigmoid(value)
    return sigma * (1.0 + value * (1.0 - sigma))


def exchange_kernel(
    cell_scale, pixel_scale,
    idx_ref, m_ref, g_ref, a_ref, cw_ref, img_ref, bw_ref,
    ig_ref, o_ref, bb_ref,
    land, meta, band, dense, slots1, land2, sums, land3, w_ref, recv0, recv1, acc1, recv2,
    edges, shift, slope, img_t, bb0, bb1, bb1_acc, bb2,
    in_sem, e_send, e_recv, m_send, m_recv, p1_send, p1_recv, own_sem, p2_send, p2_recv, p3_send, p3_recv,
    pair_send, pair_recv, x_send, x_recv, yz_send, yz_recv, ag_send, ag_recv, far_send, far_recv,
    by_send, by_recv, bx_send, bx_recv,
):
    y, x, z, core = coords()
    x_hi = x // 2
    taps, chans = w_ref.shape[0], w_ref.shape[3]
    cols = edges.shape[1]
    rows = g_ref.shape[0] // cols
    half = chans // 2
    dp, tile = lax.axis_index("dp"), lax.axis_index("tile")

    def remote(src, dst, sends, recvs, where):
        return pltpu.make_async_remote_copy(
            src_ref=src, dst_ref=dst, send_sem=sends, recv_sem=recvs,
            device_id=where, device_id_type=MESH,
        )

    plane = [(p, q) for p in range(4) for q in range(4) if p or q]
    corner = [(p, q) for p, q in plane if p and q]

    def at(dy, dz, dc, dx=0):
        return device((y + dy) % 4, (x + dx) % 4, (z + dz) % 4, (core + dc) % 2)

    barrier = pltpu.get_barrier_semaphore()
    greeted = [at(0, 0, 1)] + [at(dy, dz, 0) for dy, dz in plane]
    greeted += [at(dy, dz, 1) for dy, dz in plane if not (dy and dz)]
    greeted += [at(0, 0, 0, d) for d in (1, 2, 3)]
    greeted += [at(p, 0, 0, q) for p, q in corner] + [at(0, p, 0, q) for p, q in corner]
    below, above = (dp, (tile + TILES - 1) % TILES), (dp, (tile + 1) % TILES)
    has_below, has_above = tile > 0, tile < TILES - 1
    greeted += [below, above]
    for where in greeted:
        pl.semaphore_signal(barrier, inc=1, device_id=where, device_id_type=MESH)

    def unit(n):
        return n // 2, pl.ds(pl.multiple_of(n % 2 * 512, 512), 512)

    def moved(j, r, n):
        b = j * 5 * (rows + 2) + r * 5 + n
        slot, lanes = unit(b // 4)
        return slot, pl.ds(pl.multiple_of(b % 4 * 128, 128), 128), lanes

    first_weight = 23

    loads = []
    for k in range(taps):
        slot, lanes = unit(first_weight + k)
        loads.append(pltpu.make_async_copy(cw_ref.at[k], band.at[slot, :, lanes], in_sem.at[k]))
    loads += [
        pltpu.make_async_copy(
            a_ref.at[pl.ds(4 * u, 4)], o_ref.at[u // 2, u % 2], in_sem.at[taps + u]
        )
        for u in range(10)
    ]

    def load_gradient(b, carry):
        pltpu.make_async_copy(
            g_ref.at[pl.ds(pl.multiple_of(b * 128, 128), 128)],
            band.at[moved(1, 1 + b // 5, b % 5)], in_sem.at[19],
        ).start()
        return carry

    lax.fori_loop(0, 5 * rows, load_gradient, 0)
    for copy in loads:
        copy.start()

    pl.semaphore_wait(barrier, len(greeted))

    def edge_gradient(up, where):
        side = 0 if up else 1
        row = pl.ds((rows - 1) * cols if up else 0, cols)
        return [
            remote(g_ref.at[row], edges.at[side], e_send.at[side, 0], e_recv.at[side, 0], where)
        ]

    def edge_features(up, where):
        side = 0 if up else 1
        copies = []
        for u in range(3):
            size = 4 if u < 2 else 2
            copies.append(
                remote(
                    a_ref.at[pl.ds((10 * (rows - 1) if up else 0) + 4 * u, size)],
                    o_ref.at[5 + 2 * side + u // 2, u % 2, pl.ds(0, size)],
                    e_send.at[side, 1 + u], e_recv.at[side, 1 + u], where,
                )
            )
        return copies

    for edge_copies in (edge_gradient, edge_features):

        @pl.when(has_above)
        def _():
            for copy in edge_copies(True, above):
                copy.start()

        @pl.when(has_below)
        def _():
            for copy in edge_copies(False, below):
                copy.start()

    edge = jnp.zeros((8, half), F32)
    shift[pl.ds(0, 8), :] = edge
    shift[pl.ds(cols + 8, 8), :] = edge

    def move(r, carry):
        for part in (slice(0, half), slice(half, chans)):

            def block(j, n):
                slot, places, lanes = moved(j, r, n)
                start = pl.multiple_of(lanes.start + part.start, half)
                return slot, places, pl.ds(start, half)

            for n in range(5):
                shift[pl.ds(8 + n * 128, 128), :] = band[block(1, n)].astype(F32)
            for n in range(5):
                band[block(0, n)] = shift[pl.ds(9 + n * 128, 128), :].astype(BF)
                band[block(2, n)] = shift[pl.ds(7 + n * 128, 128), :].astype(BF)
        return carry

    pltpu.make_async_copy(g_ref, g_ref, in_sem.at[19]).wait()
    lax.fori_loop(1, rows + 1, move, 0)

    def arrive(side, edge_copies, clear):
        up, present = side == 0, has_below if side == 0 else has_above

        @pl.when(present)
        def _():
            for copy in edge_copies(up, below if up else above):
                copy.wait_recv()

        @pl.when(jnp.logical_not(present))
        def _():
            clear()

    def arrive_gradient():
        for side in range(2):

            def clear():
                edges[side] = jnp.zeros((cols, chans), BF)

            arrive(side, edge_gradient, clear)
            r = 0 if side == 0 else rows + 1
            for n in range(5):
                band[moved(1, r, n)] = edges[side, pl.ds(n * 128, 128), :]
            move(r, 0)

    def arrive_features():
        for side in range(2):

            def clear():
                nothing = jnp.zeros((4, 16, chans), BF)
                for u in range(10):
                    o_ref[5 + 2 * side + u // 8, u // 4 % 2, u % 4] = nothing

            arrive(side, edge_features, clear)

    for copy in loads:
        copy.wait()

    def ground(s, carry):
        r, n = (s // 2 + 1) % 3 + s // 6 * 2, s % 2

        @pl.when(s == 4)
        def _():
            arrive_gradient()

        out = None
        for i in range(3):
            left, right = [], []
            for j in range(3):
                left.append(
                    jnp.concatenate([band[moved(j, r + 2 - i, m)] for m in range(5)], axis=0)
                )
                slot, lanes = unit(first_weight + 3 * i + j)
                right.append(band[slot, pl.ds(pl.multiple_of(n * half, half), half), lanes])
            term = lax.dot_general(
                jnp.concatenate(left, axis=1), jnp.concatenate(right, axis=1),
                (((1,), (1,)), ((), ())), preferred_element_type=F32,
            )
            out = term if out is None else out + term
        out = out.astype(BF)
        lanes = pl.ds(pl.multiple_of(n * half, half), half)
        for m in range(10):
            k = r * 10 + m
            w_ref[k // 8, k % 8, :, lanes] = out[m * BLK : (m + 1) * BLK]
        return carry

    lax.fori_loop(0, 2 * rows, ground, 0)

    def fill(h):
        def one(s, carry):
            o = s // CAP
            place = pl.ds(pl.multiple_of(s % CAP * BLK, BLK), BLK)
            block = w_ref[idx_ref[0, s], idx_ref[1, s]]
            if h == 0:
                dense[o // 8, o % 8, place, :] = block[:, :half]
            else:
                slots1[o // 16, o // 2 % 8, o % 2, place, :] = block[:, half:]
            return carry

        lax.fori_loop(0, TILES * CAP, one, 0, unroll=4)

    line = (z, y)
    here = [line[h] * 2 + core for h in range(2)]

    def slots_of(h, member):
        if h == 0:
            return dense.at[:, member]
        return slots1.at[member // 2, :, member % 2]

    def info_of(h, member):
        return m_ref.at[h, :, member]

    steps = [(d, dc) for d in range(4) for dc in range(2) if d or dc]

    def group_copy(h, k, sign, which):
        d, dc = steps[k]
        member = (line[h] + (d if sign > 0 else 4 - d)) % 4 * 2 + (core + dc) % 2
        where = at(0, d, dc) if h == 0 else at(d, 0, dc)
        place = here[h] if sign > 0 else member
        if which == "meta":
            return remote(
                info_of(h, member), meta.at[h, place], m_send.at[h, k], m_recv.at[h, k], where
            )
        return remote(
            slots_of(h, member), land.at[h, place], p1_send.at[h, k], p1_recv.at[h, k], where
        )

    own = [
        pltpu.make_async_copy(src, dst.at[h, here[h]], own_sem.at[h, k])
        for h in range(2)
        for k, (src, dst) in enumerate(
            ((info_of(h, here[h]), meta), (slots_of(h, here[h]), land))
        )
    ]
    for h in range(2):
        fill(h)
        for copy in own[2 * h : 2 * h + 2]:
            copy.start()
        for which in ("meta", "slots"):
            for k in range(7):
                group_copy(h, k, 1, which).start()

    def column(u):
        n = first_weight + u // 4
        return n // 2, pl.ds(pl.multiple_of(n % 2 * 512 + u % 4 * 128, 128), 128)

    def turn(u, piece, start):
        block = o_ref[piece, start // 256, pl.ds(start // 64 % 4, 2)].reshape(128, chans)
        slot, lanes = column(u)
        band[slot, :, lanes] = block.T

    def turn_inner(n, carry):
        turn(5 + n, n // 4, n % 4 * 128)
        return carry

    lax.fori_loop(0, 5 * rows, turn_inner, 0)
    arrive_features()
    for side in range(2):
        for n in range(5):
            turn(5 * (rows + 1) * side + n, 5 + 2 * side + n // 4, n % 4 * 128)

    def tap(n, carry):
        i, j = n // 3, n % 3
        left = []
        for m in range(5 * rows):
            slot, lanes = column(5 * i + m)
            left.append(band[slot, :, lanes])
        right = [band[moved(j, 1 + m // 5, m % 5)] for m in range(5 * rows)]
        w_ref[n] = jnp.dot(
            jnp.concatenate(left, axis=1), jnp.concatenate(right, axis=0),
            preferred_element_type=F32,
        ).astype(BF).reshape(w_ref.shape[1:])
        return carry

    mine, other = pl.ds(core * 4, 4), pl.ds((1 - core) * 4, 4)

    def pair(k):
        t = pl.ds(3 * k, 3)
        return remote(
            w_ref.at[t, other], recv0.at[t], pair_send.at[4 + k], pair_recv.at[4 + k], at(0, 0, 1)
        )

    def along_x(k, d):
        t = pl.ds(3 * k, 3)
        return remote(
            w_ref.at[t, core * 4 + (x + d) % 4], recv1.at[d - 1, t],
            x_send.at[k, d - 1], x_recv.at[k, d - 1], at(0, 0, 0, d),
        )

    def add0(k, carry):
        w_ref[k, mine] = (w_ref[k, mine].astype(F32) + recv0[k].astype(F32)).astype(BF)
        return carry

    def pass_on(k):
        pair(k).wait()
        lax.fori_loop(3 * k, 3 * k + 3, add0, 0)
        for d in (1, 2, 3):
            along_x(k, d).start()

    for k in range(3):
        lax.fori_loop(3 * k, 3 * k + 3, tap, 0)
        pair(k).start()
        if k > 0:
            pass_on(k - 1)

    image = img_ref[...]
    slope[...] = silu_slope(jnp.dot(image, bw_ref[...], preferred_element_type=F32))
    img_t[...] = image.T
    pass_on(2)

    for k in range(7):
        for h in range(2):
            group_copy(h, k, 1, "meta").wait_send()
            group_copy(h, k, -1, "meta").wait_recv()
    own[0].wait()
    own[2].wait()

    def make_band(n, carry):
        h, owner, member = n // 64, n // 8 % 8, n % 8
        info = meta[h, member, owner].astype(F32)
        q = lax.broadcasted_iota(jnp.int32, (IMGW, CELLS), 0).astype(F32)
        left, right = q == info[0:1], q == info[0:1] + 1.0
        zero = jnp.zeros((IMGW, CELLS), F32)
        upper = jnp.where(left, info[2:3], jnp.where(right, info[3:4], zero))
        lower = jnp.where(left, info[4:5], jnp.where(right, info[5:6], zero))
        whole = jnp.concatenate([upper, lower], axis=0)
        lanes = pl.ds(pl.multiple_of(member * CELLS, CELLS), CELLS)
        for block in range(4):
            kept = jnp.where(info[1:2] == float(block), whole, 0.0)
            band[h * 8 + owner, pl.ds(block * PIXB, PIXB), lanes] = kept.astype(BF)
        return carry

    lax.fori_loop(0, 128, make_band, 0)

    for k in range(3):
        for d in (1, 2, 3):
            along_x(k, d).wait()

    def add1(k, carry):
        total = w_ref[k, core * 4 + x].astype(F32)
        for d in range(3):
            total = total + recv1[d, k].astype(F32)
        acc1[k] = total.astype(BF)
        return carry

    lax.fori_loop(0, taps, add1, 0)

    def lanes128(q):
        return pl.ds(pl.multiple_of(q * 128, 128), 128)

    def rows16(q):
        return pl.ds(pl.multiple_of(q * 16, 16), 16)

    to_plane = [
        remote(
            acc1.at[:, rows16((y + dy) % 4), lanes128((z + dz) % 4)], recv2.at[k],
            yz_send.at[k], yz_recv.at[k], at(dy, dz, 0),
        )
        for k, (dy, dz) in enumerate(plane)
    ]
    for copy in to_plane:
        copy.start()
    for k in range(7):
        for h in range(2):
            group_copy(h, k, 1, "slots").wait_send()
            group_copy(h, k, -1, "slots").wait_recv()
    own[1].wait()
    own[3].wait()

    def owner_of(h, x_part, d):
        q = (y + h * (z - y) + d) % 4
        return (1 - h) * (q * 2 + x_part) + h * (x_part * 4 + q)

    def owner_part(h, x_part, d):
        owner = owner_of(h, x_part, d)
        return h * 4 + owner // 2, pl.ds(owner % 2 * 4, 4)

    def second(h, x_part, d):
        far = (x_part + x_hi) % 2
        return remote(
            dense.at[owner_part(h, x_part, d)], land2.at[h, far, d - 1],
            p2_send.at[h, far, d - 1], p2_recv.at[h, far, d - 1],
            at((1 - h) * d, h * d, 0),
        )

    def form(x_part):
        def one(n, carry):
            h, d = n % 2, n // 2 + 1
            owner = owner_of(h, x_part, d)
            cells = land[h, :, owner].reshape(GROUP * CELLS, half)
            dense[owner_part(h, x_part, d)] = (
                jnp.dot(band[h * 8 + owner], cells, preferred_element_type=F32)
                .astype(BF)
                .reshape(4, PIXB, half)
            )

            @pl.when(d < 4)
            def _():
                second(h, x_part, d).start()

            return carry

        lax.fori_loop(0, 8, one, 0)

    form(1 - x_hi)

    for copy in to_plane:
        copy.wait()

    def add2(k, carry):
        total = acc1[k, rows16(y), lanes128(z)].astype(F32)
        for p in range(15):
            total = total + recv2[p, k].astype(F32)
        o_ref[k, core, x, y, :, lanes128(z)] = (total * (cell_scale * UP)).astype(BF)
        return carry

    lax.fori_loop(0, taps, add2, 0)

    def spread(s, k, sign):
        p, q = plane[k]
        dy, dx, dz = ((p, 0, q), (0, p, q), (p, q, 0))[s]
        part = o_ref.at[
            pl.ds(3 * s, 3), core, (x + sign * dx + 4) % 4, (y + sign * dy + 4) % 4, :,
            lanes128((z + sign * dz + 4) % 4),
        ]
        return remote(part, part, ag_send.at[s, k], ag_recv.at[s, k], at(dy, dz, 0, dx))

    def strip(s, d, sign):
        t = pl.ds(3 * s, 3)
        if s == 0:
            part, where = o_ref.at[t, core, (x + sign * d + 4) % 4], at(0, 0, 0, d)
        elif s == 1:
            part, where = o_ref.at[t, core, :, (y + sign * d + 4) % 4], at(d, 0, 0)
        else:
            part = o_ref.at[t, core, :, :, :, lanes128((z + sign * d + 4) % 4)]
            where = at(0, d, 0)
        return remote(part, part, far_send.at[s, d - 1], far_recv.at[s, d - 1], where)

    for k in range(15):
        for s in range(3):
            spread(s, k, 0).start()

    form(x_hi)

    def settle(far):
        for h in range(2):
            for d in (1, 2, 3):
                second(h, (far + x_hi) % 2, d).wait()

    def gathered(h, x_part, far):
        total = dense[owner_part(h, x_part, 0)].astype(F32)
        for d in range(3):
            total = total + land2[h, far, d].astype(F32)
        return total.reshape(NPIX, half)

    settle(1)
    third = []
    for h in range(2):
        sums[h] = gathered(h, 1 - x_hi, 1).astype(BF)
        third.append(
            remote(sums.at[h], land3.at[h], p3_send.at[h], p3_recv.at[h], at(0, 0, 0, 2))
        )
        third[h].start()

    for k in range(15):
        for s in range(3):
            spread(s, k, 0).wait_send()
            spread(s, k, -1).wait_recv()
    for d in (1, 2, 3):
        for s in range(3):
            strip(s, d, 0).start()

    settle(0)

    scaled = []
    for h in range(2):
        third[h].wait()
        feature = gathered(h, x_hi, 0) + land3[h].astype(F32)
        scaled.append((feature * slope[:, h * half : (h + 1) * half]).astype(BF))
    scaled = jnp.concatenate(scaled, axis=1)
    part = jnp.dot(img_t[...], scaled, preferred_element_type=F32).astype(BF)
    w_ref[0] = part.reshape(w_ref.shape[1:])
    bb_pair = remote(w_ref.at[0, other], bb0, pair_send.at[1], pair_recv.at[1], at(0, 0, 1))
    bb_pair.start()
    image_grad = lax.dot_general(
        scaled, bw_ref[...], (((1,), (1,)), ((), ())), preferred_element_type=F32
    )
    ig_ref[...] = (image_grad * UP).astype(BF)
    bb_pair.wait()
    w_ref[1, pl.ds(0, 4)] = (w_ref[0, mine].astype(F32) + bb0[...].astype(F32)).astype(BF)

    def place(dy, dz):
        return (y + dy + 4) % 4 * 4 + (z + dz + 4) % 4

    bb_plane = [
        remote(
            w_ref.at[1, place(dy, dz) // 4, rows16(place(dy, dz) % 4)], bb1.at[k],
            by_send.at[0, k], by_recv.at[0, k], at(dy, dz, 0),
        )
        for k, (dy, dz) in enumerate(plane)
    ]
    for copy in bb_plane:
        copy.start()
    for copy in bb_plane:
        copy.wait()
    total = w_ref[1, y, rows16(z), :].astype(F32)
    for k in range(15):
        total = total + bb1[k].astype(F32)
    bb1_acc[...] = total.astype(BF)
    bb_line = [
        remote(
            bb1_acc.at[:, lanes128((x + d) % 4)], bb2.at[d - 1],
            bx_send.at[0, d - 1], bx_recv.at[0, d - 1], at(0, 0, 0, d),
        )
        for d in (1, 2, 3)
    ]
    for copy in bb_line:
        copy.start()

    for d in (1, 2, 3):
        for s in range(3):
            strip(s, d, 0).wait_send()
            strip(s, d, -1).wait_recv()

    def back(c):
        return remote(
            o_ref.at[:, c], o_ref.at[:, c], pair_send.at[2], pair_recv.at[2], at(0, 0, 1)
        )

    back(core).start()
    for copy in bb_line:
        copy.wait()
    total = bb1_acc[:, lanes128(x)].astype(F32)
    for d in range(3):
        total = total + bb2[d].astype(F32)

    def bb_rows(dy, dz):
        return pl.ds(pl.multiple_of(core * half + place(dy, dz) * 16, 16), 16)

    bb_ref[bb_rows(0, 0), lanes128(x)] = (total * (pixel_scale * UP)).astype(BF)

    def bb_strip(d, sign):
        part = bb_ref.at[bb_rows(0, 0), lanes128((x + sign * d + 4) % 4)]
        return remote(part, part, bx_send.at[1, d - 1], bx_recv.at[1, d - 1], at(0, 0, 0, d))

    def bb_spread(k, sign):
        dy, dz = plane[k]
        part = bb_ref.at[bb_rows(sign * dy, sign * dz)]
        return remote(part, part, by_send.at[1, k], by_recv.at[1, k], at(dy, dz, 0))

    def bb_half(c):
        return pl.ds(pl.multiple_of(c * half, half), half)

    def bb_back(which):
        part = bb_ref.at[which]
        return remote(part, part, pair_send.at[3], pair_recv.at[3], at(0, 0, 1))

    for d in (1, 2, 3):
        bb_strip(d, 0).start()
    for d in (1, 2, 3):
        bb_strip(d, 0).wait_send()
        bb_strip(d, -1).wait_recv()
    for k in range(15):
        bb_spread(k, 0).start()
    for k in range(15):
        bb_spread(k, 0).wait_send()
        bb_spread(k, -1).wait_recv()
    bb_back(bb_half(core)).start()
    back(core).wait_send()
    back(1 - core).wait_recv()
    bb_back(bb_half(core)).wait_send()
    bb_back(bb_half(1 - core)).wait_recv()

    @pl.when(has_above)
    def _():
        for copy in edge_gradient(True, above) + edge_features(True, above):
            copy.wait_send()

    @pl.when(has_below)
    def _():
        for copy in edge_gradient(False, below) + edge_features(False, below):
            copy.wait_send()


def exchange_all(cell_scale, pixel_scale, idx, meta, g, act, kernel, image, weight):
    chans = image.shape[1]
    half = chans // 2
    taps = kernel.shape[0]
    cols = 640
    dma = pltpu.SemaphoreType.DMA
    vmem = pltpu.VMEM
    pixels = image.shape[0]
    return pl.pallas_call(
        functools.partial(exchange_kernel, cell_scale, pixel_scale),
        out_shape=[
            jax.ShapeDtypeStruct((pixels, chans), BF),
            jax.ShapeDtypeStruct((taps, 2, 4, 4, 16, chans), BF),
            jax.ShapeDtypeStruct((chans, chans), BF),
        ],
        in_specs=[SMEM] + [HBM] * 4 + [VMEM, VMEM],
        out_specs=[VMEM, VMEM, VMEM],
        scratch_shapes=[
            vmem((2, GROUP, GROUP, CELLS, half), BF),
            vmem((2, GROUP, GROUP, 16, CELLS), BF),
            vmem((2 * GROUP, NPIX, GROUP * CELLS), BF),
            vmem((8, 8, CELLS, half), BF),
            vmem((4, 8, 2, CELLS, half), BF),
            vmem((2, 2, 3, 4, PIXB, half), BF),
            vmem((2, NPIX, half), BF),
            vmem((2, NPIX, half), BF),
            vmem((taps, 8, BLK, chans), BF),
            vmem((taps, 4, BLK, chans), BF),
            vmem((3, taps, 64, chans), BF),
            vmem((taps, 64, chans), BF),
            vmem((15, taps, 16, 128), BF),
            vmem((2, cols, chans), BF),
            vmem((cols + 16, half), F32),
            vmem((pixels, chans), F32),
            vmem((chans, pixels), BF),
            vmem((4, BLK, chans), BF),
            vmem((15, 16, chans), BF),
            vmem((16, chans), BF),
            vmem((3, 16, 128), BF),
            dma((20,)), dma((2, 4)), dma((2, 4)),
            dma((2, 7)), dma((2, 7)), dma((2, 7)), dma((2, 7)), dma((2, 2)),
            dma((2, 2, 3)), dma((2, 2, 3)), dma((2,)), dma((2,)),
            dma((7,)), dma((7,)), dma((3, 3)), dma((3, 3)), dma((15,)), dma((15,)),
            dma((3, 15)), dma((3, 15)), dma((3, 3)), dma((3, 3)),
            dma((2, 15)), dma((2, 15)), dma((2, 3)), dma((2, 3)),
        ],
        compiler_params=pltpu.CompilerParams(
            collective_id=0, has_side_effects=True, vmem_limit_bytes=67043328
        ),
        name="exchange_all",
    )(idx, meta, g, act, kernel, image, weight)


def body(grad_out, bev_act, conv_weight, img_in, backbone_weight, route, offsets, frac_x, frac_y):
    my_tile = lax.axis_index("tile")
    g, act, image = grad_out[0], bev_act[0], img_in[0]
    rows, cols, chans = g.shape
    blocks = rows * cols // BLK
    per_device = image.shape[0] // PIXB

    owners = (route[0] // per_device).reshape(TILES, blocks)
    local_ids = (route[0] % per_device).reshape(TILES, blocks)
    my_owners = lax.dynamic_index_in_dim(owners, my_tile, 0, keepdims=False)
    same = my_owners[:, None] == my_owners[None, :]
    before = lax.broadcasted_iota(jnp.int32, (blocks, blocks), 1) < lax.broadcasted_iota(
        jnp.int32, (blocks, blocks), 0
    )
    my_slots = my_owners * CAP + jnp.sum((same & before).astype(jnp.int32), axis=1)
    chosen = my_slots[None, :] == lax.broadcasted_iota(jnp.int32, (TILES * CAP, blocks), 0)
    idx = jnp.sum(
        jnp.where(chosen, lax.broadcasted_iota(jnp.int32, chosen.shape, 1), 0), axis=1
    )
    right_w = frac_x[0].astype(F32) / 256.0
    lower_w = frac_y[0].astype(F32) / 256.0
    cells = jnp.stack(
        [
            offsets[0].astype(F32),
            (1.0 - lower_w) * (1.0 - right_w),
            (1.0 - lower_w) * right_w,
            lower_w * (1.0 - right_w),
            lower_w * right_w,
        ]
    )
    cells = cells.astype(BF).reshape(5, blocks, BLK)
    info = jnp.einsum("sk,rkm->srm", chosen.astype(BF), cells, preferred_element_type=F32)
    my_local = lax.dynamic_index_in_dim(local_ids, my_tile, 0, keepdims=False)
    held = jnp.sum(jnp.where(chosen, my_local[None, :] + 1, 0), axis=1) - 1
    held = jnp.broadcast_to(held.astype(F32)[:, None, None], (TILES * CAP, 1, BLK))
    info = jnp.concatenate([info[:, :1], held, info[:, 1:]], axis=1).astype(BF)
    info = info.reshape(TILES, CAP, 6, BLK).transpose(0, 2, 1, 3).reshape(TILES, 6, CELLS)
    info = jnp.pad(info, ((0, 0), (0, 10), (0, 0)))
    by_z = info.reshape(8, 8, 16, CELLS)
    by_y = info.reshape(4, 8, 2, 16, CELLS).transpose(1, 0, 2, 3, 4).reshape(8, 8, 16, CELLS)
    meta = jnp.stack([by_z, by_y])

    weights = conv_weight.transpose(1, 2, 0, 3).reshape(9, chans, chans)
    cell_scale = 1.0 / math.sqrt(2 * TILES * rows * cols)
    pixel_scale = 1.0 / math.sqrt(2 * TILES * image.shape[0])
    image_grad, conv_sum, backbone_grad = exchange_all(
        cell_scale,
        pixel_scale,
        jnp.stack([idx // 8, idx % 8]),
        meta,
        g.reshape(rows * cols, chans),
        act.reshape(-1, 4, 16, chans),
        weights,
        image,
        backbone_weight,
    )
    image_grad, conv_sum, backbone_grad = (
        (part * jnp.asarray(1.0 / UP, BF)) for part in (image_grad, conv_sum, backbone_grad)
    )
    conv_grad = conv_sum.reshape(3, 3, chans, chans).transpose(2, 0, 1, 3)
    return (image_grad[None], conv_grad, backbone_grad)


def solution(mesh):
    return jax.shard_map(
        body,
        mesh=mesh,
        in_specs=(
            P("dp", "tile", None, None),
            P("dp", "tile", None, None),
            P(),
            P("dp", "tile", None),
            P(),
            P("dp", None),
            P("dp", "tile"),
            P("dp", "tile"),
            P("dp", "tile"),
        ),
        out_specs=(P("dp", "tile", None), P(), P()),
        check_vma=False,
    )
```

```python
import functools
import math

import jax
import jax.numpy as jnp
from jax import lax
from jax.experimental import pallas as pl
from jax.experimental.pallas import tpu as pltpu
from jax.sharding import PartitionSpec as P

BLK = 64
IMGW = 64
PIXB = 2 * IMGW
TILES = 64
CAP = 2
MESH = pl.DeviceIdType.MESH
ANY = pl.BlockSpec(memory_space=pl.ANY)
VMEM = pl.BlockSpec(memory_space=pltpu.VMEM)
SMEM = pl.BlockSpec(memory_space=pltpu.SMEM)
HBM = pl.BlockSpec(memory_space=pltpu.HBM)
BF = jnp.bfloat16
F32 = jnp.float32


def coords():
    t = lax.axis_index("tile")
    return t // 16, (t // 8) % 2 * 2 + lax.axis_index("dp"), (t // 2) % 4, t % 2


def device(y, x, z, core):
    return (x % 2, ((y * 2 + x // 2) * 4 + z) * 2 + core)


def along(axis, step):
    y, x, z, core = coords()
    if axis == "y":
        y = (y + step) % 4
    elif axis == "x":
        x = (x + step) % 4
    elif axis == "z":
        z = (z + step) % 4
    else:
        core = 1 - core
    return device(y, x, z, core)


NPIX = 4 * PIXB
CELLS = CAP * BLK
GROUP = 8


def silu_slope(value):
    sigma = jax.nn.sigmoid(value)
    return sigma * (1.0 + value * (1.0 - sigma))


def exchange_kernel(
    cell_scale, pixel_scale,
    idx_ref, m_ref, g_ref, a_ref, cw_ref, img_ref, bw_ref,
    ig_ref, o_ref, bb_ref,
    land, meta, band, dense, slots1, land2, sums, land3, w_ref, recv0, recv1, acc1, recv2,
    edges, shift, slope, img_t, bb0, bb1, bb1_acc, bb2,
    in_sem, e_send, e_recv, m_send, m_recv, p1_send, p1_recv, own_sem, p2_send, p2_recv, p3_send, p3_recv,
    pair_send, pair_recv, x_send, x_recv, yz_send, yz_recv, ag_send, ag_recv, far_send, far_recv,
    by_send, by_recv, bx_send, bx_recv,
):
    y, x, z, core = coords()
    x_hi = x // 2
    taps, chans = w_ref.shape[0], w_ref.shape[3]
    cols = edges.shape[1]
    rows = g_ref.shape[0] // cols
    half = chans // 2
    dp, tile = lax.axis_index("dp"), lax.axis_index("tile")

    def remote(src, dst, sends, recvs, where):
        return pltpu.make_async_remote_copy(
            src_ref=src, dst_ref=dst, send_sem=sends, recv_sem=recvs,
            device_id=where, device_id_type=MESH,
        )

    plane = [(p, q) for p in range(4) for q in range(4) if p or q]
    corner = [(p, q) for p, q in plane if p and q]

    def at(dy, dz, dc, dx=0):
        return device((y + dy) % 4, (x + dx) % 4, (z + dz) % 4, (core + dc) % 2)

    barrier = pltpu.get_barrier_semaphore()
    greeted = [at(0, 0, 1)] + [at(dy, dz, 0) for dy, dz in plane]
    greeted += [at(dy, dz, 1) for dy, dz in plane if not (dy and dz)]
    greeted += [at(0, 0, 0, d) for d in (1, 2, 3)]
    greeted += [at(p, 0, 0, q) for p, q in corner] + [at(0, p, 0, q) for p, q in corner]
    below, above = (dp, (tile + TILES - 1) % TILES), (dp, (tile + 1) % TILES)
    has_below, has_above = tile > 0, tile < TILES - 1
    greeted += [below, above]
    for where in greeted:
        pl.semaphore_signal(barrier, inc=1, device_id=where, device_id_type=MESH)

    def unit(n):
        return n // 2, pl.ds(pl.multiple_of(n % 2 * 512, 512), 512)

    def moved(j, r, n):
        b = j * 5 * (rows + 2) + r * 5 + n
        slot, lanes = unit(b // 4)
        return slot, pl.ds(pl.multiple_of(b % 4 * 128, 128), 128), lanes

    first_weight = 23

    loads = []
    for k in range(taps):
        slot, lanes = unit(first_weight + k)
        loads.append(pltpu.make_async_copy(cw_ref.at[k], band.at[slot, :, lanes], in_sem.at[k]))
    loads += [
        pltpu.make_async_copy(
            a_ref.at[pl.ds(4 * u, 4)], o_ref.at[u // 2, u % 2], in_sem.at[taps + u]
        )
        for u in range(10)
    ]

    def load_gradient(b, carry):
        pltpu.make_async_copy(
            g_ref.at[pl.ds(pl.multiple_of(b * 128, 128), 128)],
            band.at[moved(1, 1 + b // 5, b % 5)], in_sem.at[19],
        ).start()
        return carry

    lax.fori_loop(0, 5 * rows, load_gradient, 0)
    for copy in loads:
        copy.start()

    pl.semaphore_wait(barrier, len(greeted))

    def edge_gradient(up, where):
        side = 0 if up else 1
        row = pl.ds((rows - 1) * cols if up else 0, cols)
        return [
            remote(g_ref.at[row], edges.at[side], e_send.at[side, 0], e_recv.at[side, 0], where)
        ]

    def edge_features(up, where):
        side = 0 if up else 1
        copies = []
        for u in range(3):
            size = 4 if u < 2 else 2
            copies.append(
                remote(
                    a_ref.at[pl.ds((10 * (rows - 1) if up else 0) + 4 * u, size)],
                    o_ref.at[5 + 2 * side + u // 2, u % 2, pl.ds(0, size)],
                    e_send.at[side, 1 + u], e_recv.at[side, 1 + u], where,
                )
            )
        return copies

    for edge_copies in (edge_gradient, edge_features):

        @pl.when(has_above)
        def _():
            for copy in edge_copies(True, above):
                copy.start()

        @pl.when(has_below)
        def _():
            for copy in edge_copies(False, below):
                copy.start()

    edge = jnp.zeros((8, half), F32)
    shift[pl.ds(0, 8), :] = edge
    shift[pl.ds(cols + 8, 8), :] = edge

    def move(r, carry):
        for part in (slice(0, half), slice(half, chans)):

            def block(j, n):
                slot, places, lanes = moved(j, r, n)
                start = pl.multiple_of(lanes.start + part.start, half)
                return slot, places, pl.ds(start, half)

            for n in range(5):
                shift[pl.ds(8 + n * 128, 128), :] = band[block(1, n)].astype(F32)
            for n in range(5):
                band[block(0, n)] = shift[pl.ds(9 + n * 128, 128), :].astype(BF)
                band[block(2, n)] = shift[pl.ds(7 + n * 128, 128), :].astype(BF)
        return carry

    pltpu.make_async_copy(g_ref, g_ref, in_sem.at[19]).wait()
    lax.fori_loop(1, rows + 1, move, 0)

    def arrive(side, edge_copies, clear):
        up, present = side == 0, has_below if side == 0 else has_above

        @pl.when(present)
        def _():
            for copy in edge_copies(up, below if up else above):
                copy.wait_recv()

        @pl.when(jnp.logical_not(present))
        def _():
            clear()

    def arrive_gradient():
        for side in range(2):

            def clear():
                edges[side] = jnp.zeros((cols, chans), BF)

            arrive(side, edge_gradient, clear)
            r = 0 if side == 0 else rows + 1
            for n in range(5):
                band[moved(1, r, n)] = edges[side, pl.ds(n * 128, 128), :]
            move(r, 0)

    def arrive_features():
        for side in range(2):

            def clear():
                nothing = jnp.zeros((4, 16, chans), BF)
                for u in range(10):
                    o_ref[5 + 2 * side + u // 8, u // 4 % 2, u % 4] = nothing

            arrive(side, edge_features, clear)

    for copy in loads:
        copy.wait()

    def ground(s, carry):
        r, n = (s // 2 + 1) % 3 + s // 6 * 2, s % 2

        @pl.when(s == 4)
        def _():
            arrive_gradient()

        out = None
        for i in range(3):
            left, right = [], []
            for j in range(3):
                left.append(
                    jnp.concatenate([band[moved(j, r + 2 - i, m)] for m in range(5)], axis=0)
                )
                slot, lanes = unit(first_weight + 3 * i + j)
                right.append(band[slot, pl.ds(pl.multiple_of(n * half, half), half), lanes])
            term = lax.dot_general(
                jnp.concatenate(left, axis=1), jnp.concatenate(right, axis=1),
                (((1,), (1,)), ((), ())), preferred_element_type=F32,
            )
            out = term if out is None else out + term
        out = out.astype(BF)
        lanes = pl.ds(pl.multiple_of(n * half, half), half)
        for m in range(10):
            k = r * 10 + m
            w_ref[k // 8, k % 8, :, lanes] = out[m * BLK : (m + 1) * BLK]
        return carry

    lax.fori_loop(0, 2 * rows, ground, 0)

    def fill(s, carry):
        o = s // CAP
        place = pl.ds(pl.multiple_of(s % CAP * BLK, BLK), BLK)
        block = w_ref[idx_ref[0, s], idx_ref[1, s]]
        dense[o // 8, o % 8, place, :] = block[:, :half]
        slots1[o // 16, o // 2 % 8, o % 2, place, :] = block[:, half:]
        return carry

    lax.fori_loop(0, TILES * CAP, fill, 0)

    line = (z, y)
    here = [line[h] * 2 + core for h in range(2)]

    def slots_of(h, member):
        if h == 0:
            return dense.at[:, member]
        return slots1.at[member // 2, :, member % 2]

    def info_of(h, member):
        return m_ref.at[h, :, member]

    steps = [(d, dc) for d in range(4) for dc in range(2) if d or dc]

    def group_copy(h, k, sign, which):
        d, dc = steps[k]
        member = (line[h] + (d if sign > 0 else 4 - d)) % 4 * 2 + (core + dc) % 2
        where = at(0, d, dc) if h == 0 else at(d, 0, dc)
        place = here[h] if sign > 0 else member
        if which == "meta":
            return remote(
                info_of(h, member), meta.at[h, place], m_send.at[h, k], m_recv.at[h, k], where
            )
        return remote(
            slots_of(h, member), land.at[h, place], p1_send.at[h, k], p1_recv.at[h, k], where
        )

    own = [
        pltpu.make_async_copy(src, dst.at[h, here[h]], own_sem.at[h, k])
        for h in range(2)
        for k, (src, dst) in enumerate(
            ((info_of(h, here[h]), meta), (slots_of(h, here[h]), land))
        )
    ]
    for copy in own:
        copy.start()
    for which in ("meta", "slots"):
        for k in range(7):
            for h in range(2):
                group_copy(h, k, 1, which).start()

    def column(u):
        n = first_weight + u // 4
        return n // 2, pl.ds(pl.multiple_of(n % 2 * 512 + u % 4 * 128, 128), 128)

    def turn(u, piece, start):
        block = o_ref[piece, start // 256, pl.ds(start // 64 % 4, 2)].reshape(128, chans)
        slot, lanes = column(u)
        band[slot, :, lanes] = block.T

    def turn_inner(n, carry):
        turn(5 + n, n // 4, n % 4 * 128)
        return carry

    lax.fori_loop(0, 5 * rows, turn_inner, 0)
    arrive_features()
    for side in range(2):
        for n in range(5):
            turn(5 * (rows + 1) * side + n, 5 + 2 * side + n // 4, n % 4 * 128)

    def tap(n, carry):
        i, j = n // 3, n % 3
        left = []
        for m in range(5 * rows):
            slot, lanes = column(5 * i + m)
            left.append(band[slot, :, lanes])
        right = [band[moved(j, 1 + m // 5, m % 5)] for m in range(5 * rows)]
        w_ref[n] = jnp.dot(
            jnp.concatenate(left, axis=1), jnp.concatenate(right, axis=0),
            preferred_element_type=F32,
        ).astype(BF).reshape(w_ref.shape[1:])
        return carry

    mine, other = pl.ds(core * 4, 4), pl.ds((1 - core) * 4, 4)

    def pair(k):
        t = pl.ds(3 * k, 3)
        return remote(
            w_ref.at[t, other], recv0.at[t], pair_send.at[4 + k], pair_recv.at[4 + k], at(0, 0, 1)
        )

    def along_x(k, d):
        t = pl.ds(3 * k, 3)
        return remote(
            w_ref.at[t, core * 4 + (x + d) % 4], recv1.at[d - 1, t],
            x_send.at[k, d - 1], x_recv.at[k, d - 1], at(0, 0, 0, d),
        )

    def add0(k, carry):
        w_ref[k, mine] = (w_ref[k, mine].astype(F32) + recv0[k].astype(F32)).astype(BF)
        return carry

    def pass_on(k):
        pair(k).wait()
        lax.fori_loop(3 * k, 3 * k + 3, add0, 0)
        for d in (1, 2, 3):
            along_x(k, d).start()

    for k in range(3):
        lax.fori_loop(3 * k, 3 * k + 3, tap, 0)
        pair(k).start()
        if k > 0:
            pass_on(k - 1)

    image = img_ref[...]
    slope[...] = silu_slope(jnp.dot(image, bw_ref[...], preferred_element_type=F32))
    img_t[...] = image.T
    pass_on(2)

    for k in range(7):
        for h in range(2):
            group_copy(h, k, 1, "meta").wait_send()
            group_copy(h, k, -1, "meta").wait_recv()
    own[0].wait()
    own[2].wait()

    def make_band(n, carry):
        h, owner, member = n // 64, n // 8 % 8, n % 8
        info = meta[h, member, owner].astype(F32)
        q = lax.broadcasted_iota(jnp.int32, (IMGW, CELLS), 0).astype(F32)
        left, right = q == info[0:1], q == info[0:1] + 1.0
        zero = jnp.zeros((IMGW, CELLS), F32)
        upper = jnp.where(left, info[2:3], jnp.where(right, info[3:4], zero))
        lower = jnp.where(left, info[4:5], jnp.where(right, info[5:6], zero))
        whole = jnp.concatenate([upper, lower], axis=0)
        lanes = pl.ds(pl.multiple_of(member * CELLS, CELLS), CELLS)
        for block in range(4):
            kept = jnp.where(info[1:2] == float(block), whole, 0.0)
            band[h * 8 + owner, pl.ds(block * PIXB, PIXB), lanes] = kept.astype(BF)
        return carry

    lax.fori_loop(0, 128, make_band, 0)

    for k in range(3):
        for d in (1, 2, 3):
            along_x(k, d).wait()

    def add1(k, carry):
        total = w_ref[k, core * 4 + x].astype(F32)
        for d in range(3):
            total = total + recv1[d, k].astype(F32)
        acc1[k] = total.astype(BF)
        return carry

    lax.fori_loop(0, taps, add1, 0)

    def lanes128(q):
        return pl.ds(pl.multiple_of(q * 128, 128), 128)

    def rows16(q):
        return pl.ds(pl.multiple_of(q * 16, 16), 16)

    to_plane = [
        remote(
            acc1.at[:, rows16((y + dy) % 4), lanes128((z + dz) % 4)], recv2.at[k],
            yz_send.at[k], yz_recv.at[k], at(dy, dz, 0),
        )
        for k, (dy, dz) in enumerate(plane)
    ]
    for copy in to_plane:
        copy.start()
    for k in range(7):
        for h in range(2):
            group_copy(h, k, 1, "slots").wait_send()
            group_copy(h, k, -1, "slots").wait_recv()
    own[1].wait()
    own[3].wait()

    def owner_of(h, x_part, d):
        q = (y + h * (z - y) + d) % 4
        return (1 - h) * (q * 2 + x_part) + h * (x_part * 4 + q)

    def owner_part(h, x_part, d):
        owner = owner_of(h, x_part, d)
        return h * 4 + owner // 2, pl.ds(owner % 2 * 4, 4)

    def second(h, x_part, d):
        far = (x_part + x_hi) % 2
        return remote(
            dense.at[owner_part(h, x_part, d)], land2.at[h, far, d - 1],
            p2_send.at[h, far, d - 1], p2_recv.at[h, far, d - 1],
            at((1 - h) * d, h * d, 0),
        )

    def form(x_part):
        def one(n, carry):
            h, d = n % 2, n // 2 + 1
            owner = owner_of(h, x_part, d)
            cells = land[h, :, owner].reshape(GROUP * CELLS, half)
            dense[owner_part(h, x_part, d)] = (
                jnp.dot(band[h * 8 + owner], cells, preferred_element_type=F32)
                .astype(BF)
                .reshape(4, PIXB, half)
            )

            @pl.when(d < 4)
            def _():
                second(h, x_part, d).start()

            return carry

        lax.fori_loop(0, 8, one, 0)

    form(1 - x_hi)

    for copy in to_plane:
        copy.wait()

    def add2(k, carry):
        total = acc1[k, rows16(y), lanes128(z)].astype(F32)
        for p in range(15):
            total = total + recv2[p, k].astype(F32)
        o_ref[k, core, x, y, :, lanes128(z)] = (total * cell_scale).astype(BF)
        return carry

    lax.fori_loop(0, taps, add2, 0)

    sets = (("x", 0, 3), ("y", 3, 2), ("z", 5, 2), ("x", 7, 2))

    def spread(s, k, sign):
        axis, first, count = sets[s]
        p, q = plane[k]
        dy, dx, dz = {"x": (p, 0, q), "y": (0, p, q), "z": (p, q, 0)}[axis]
        part = o_ref.at[
            pl.ds(first, count), core, (x + sign * dx + 4) % 4, (y + sign * dy + 4) % 4, :,
            lanes128((z + sign * dz + 4) % 4),
        ]
        return remote(part, part, ag_send.at[s, k], ag_recv.at[s, k], at(dy, dz, 0, dx))

    def strip(s, d, sign):
        axis, first, count = sets[s]
        t = pl.ds(first, count)
        if axis == "x":
            part, where = o_ref.at[t, core, (x + sign * d + 4) % 4], at(0, 0, 0, d)
        elif axis == "y":
            part, where = o_ref.at[t, core, :, (y + sign * d + 4) % 4], at(d, 0, 0)
        else:
            part = o_ref.at[t, core, :, :, :, lanes128((z + sign * d + 4) % 4)]
            where = at(0, d, 0)
        return remote(part, part, far_send.at[s, d - 1], far_recv.at[s, d - 1], where)

    def strips(s):
        for d in (1, 2, 3):
            strip(s, d, 0).start()

    for k in range(15):
        for s in range(4):
            spread(s, k, 0).start()

    form(x_hi)

    def settle(far):
        for h in range(2):
            for d in (1, 2, 3):
                second(h, (far + x_hi) % 2, d).wait()

    def gathered(h, x_part, far):
        total = dense[owner_part(h, x_part, 0)].astype(F32)
        for d in range(3):
            total = total + land2[h, far, d].astype(F32)
        return total.reshape(NPIX, half)

    settle(1)
    third = []
    for h in range(2):
        sums[h] = gathered(h, 1 - x_hi, 1).astype(BF)
        third.append(
            remote(sums.at[h], land3.at[h], p3_send.at[h], p3_recv.at[h], at(0, 0, 0, 2))
        )
        third[h].start()

    for k in range(15):
        for s in range(4):
            spread(s, k, 0).wait_send()
            spread(s, k, -1).wait_recv()
    strips(0)
    strips(3)
    settle(0)

    scaled = []
    for h in range(2):
        third[h].wait()
        feature = gathered(h, x_hi, 0) + land3[h].astype(F32)
        scaled.append((feature * slope[:, h * half : (h + 1) * half]).astype(BF))
    scaled = jnp.concatenate(scaled, axis=1)
    part = jnp.dot(img_t[...], scaled, preferred_element_type=F32).astype(BF)
    w_ref[0] = part.reshape(w_ref.shape[1:])
    bb_pair = remote(w_ref.at[0, other], bb0, pair_send.at[1], pair_recv.at[1], at(0, 0, 1))
    bb_pair.start()
    image_grad = lax.dot_general(
        scaled, bw_ref[...], (((1,), (1,)), ((), ())), preferred_element_type=F32
    )
    ig_ref[...] = image_grad.astype(BF)
    bb_pair.wait()
    w_ref[1, pl.ds(0, 4)] = (w_ref[0, mine].astype(F32) + bb0[...].astype(F32)).astype(BF)

    def place(dy, dz):
        return (y + dy + 4) % 4 * 4 + (z + dz + 4) % 4

    bb_plane = [
        remote(
            w_ref.at[1, place(dy, dz) // 4, rows16(place(dy, dz) % 4)], bb1.at[k],
            by_send.at[0, k], by_recv.at[0, k], at(dy, dz, 0),
        )
        for k, (dy, dz) in enumerate(plane)
    ]
    for copy in bb_plane:
        copy.start()
    strips(1)
    strips(2)
    for copy in bb_plane:
        copy.wait()
    total = w_ref[1, y, rows16(z), :].astype(F32)
    for k in range(15):
        total = total + bb1[k].astype(F32)
    bb1_acc[...] = total.astype(BF)
    bb_line = [
        remote(
            bb1_acc.at[:, lanes128((x + d) % 4)], bb2.at[d - 1],
            bx_send.at[0, d - 1], bx_recv.at[0, d - 1], at(0, 0, 0, d),
        )
        for d in (1, 2, 3)
    ]
    for copy in bb_line:
        copy.start()

    def back(c):
        return remote(
            o_ref.at[:, c], o_ref.at[:, c], pair_send.at[2], pair_recv.at[2], at(0, 0, 1)
        )

    for copy in bb_line:
        copy.wait()
    total = bb1_acc[:, lanes128(x)].astype(F32)
    for d in range(3):
        total = total + bb2[d].astype(F32)

    def bb_rows(dy, dz):
        return pl.ds(pl.multiple_of(core * half + place(dy, dz) * 16, 16), 16)

    bb_ref[bb_rows(0, 0), lanes128(x)] = (total * pixel_scale).astype(BF)

    def bb_strip(d, sign):
        part = bb_ref.at[bb_rows(0, 0), lanes128((x + sign * d + 4) % 4)]
        return remote(part, part, bx_send.at[1, d - 1], bx_recv.at[1, d - 1], at(0, 0, 0, d))

    def bb_spread(k, sign):
        dy, dz = plane[k]
        part = bb_ref.at[bb_rows(sign * dy, sign * dz)]
        return remote(part, part, by_send.at[1, k], by_recv.at[1, k], at(dy, dz, 0))

    def bb_half(c):
        return pl.ds(pl.multiple_of(c * half, half), half)

    def bb_back(which):
        part = bb_ref.at[which]
        return remote(part, part, pair_send.at[3], pair_recv.at[3], at(0, 0, 1))

    for d in (1, 2, 3):
        bb_strip(d, 0).start()

    for s in (0, 3, 1, 2):
        for d in (1, 2, 3):
            strip(s, d, 0).wait_send()
            strip(s, d, -1).wait_recv()
    back(core).start()
    for d in (1, 2, 3):
        bb_strip(d, 0).wait_send()
        bb_strip(d, -1).wait_recv()
    for k in range(15):
        bb_spread(k, 0).start()
    for k in range(15):
        bb_spread(k, 0).wait_send()
        bb_spread(k, -1).wait_recv()
    bb_back(bb_half(core)).start()
    back(core).wait_send()
    back(1 - core).wait_recv()
    bb_back(bb_half(core)).wait_send()
    bb_back(bb_half(1 - core)).wait_recv()

    @pl.when(has_above)
    def _():
        for copy in edge_gradient(True, above) + edge_features(True, above):
            copy.wait_send()

    @pl.when(has_below)
    def _():
        for copy in edge_gradient(False, below) + edge_features(False, below):
            copy.wait_send()


def exchange_all(cell_scale, pixel_scale, idx, meta, g, act, kernel, image, weight):
    chans = image.shape[1]
    half = chans // 2
    taps = kernel.shape[0]
    cols = 640
    dma = pltpu.SemaphoreType.DMA
    vmem = pltpu.VMEM
    pixels = image.shape[0]
    return pl.pallas_call(
        functools.partial(exchange_kernel, cell_scale, pixel_scale),
        out_shape=[
            jax.ShapeDtypeStruct((pixels, chans), BF),
            jax.ShapeDtypeStruct((taps, 2, 4, 4, 16, chans), BF),
            jax.ShapeDtypeStruct((chans, chans), BF),
        ],
        in_specs=[SMEM] + [HBM] * 4 + [VMEM, VMEM],
        out_specs=[VMEM, VMEM, VMEM],
        scratch_shapes=[
            vmem((2, GROUP, GROUP, CELLS, half), BF),
            vmem((2, GROUP, GROUP, 16, CELLS), BF),
            vmem((2 * GROUP, NPIX, GROUP * CELLS), BF),
            vmem((8, 8, CELLS, half), BF),
            vmem((4, 8, 2, CELLS, half), BF),
            vmem((2, 2, 3, 4, PIXB, half), BF),
            vmem((2, NPIX, half), BF),
            vmem((2, NPIX, half), BF),
            vmem((taps, 8, BLK, chans), BF),
            vmem((taps, 4, BLK, chans), BF),
            vmem((3, taps, 64, chans), BF),
            vmem((taps, 64, chans), BF),
            vmem((15, taps, 16, 128), BF),
            vmem((2, cols, chans), BF),
            vmem((cols + 16, half), F32),
            vmem((pixels, chans), F32),
            vmem((chans, pixels), BF),
            vmem((4, BLK, chans), BF),
            vmem((15, 16, chans), BF),
            vmem((16, chans), BF),
            vmem((3, 16, 128), BF),
            dma((20,)), dma((2, 4)), dma((2, 4)),
            dma((2, 7)), dma((2, 7)), dma((2, 7)), dma((2, 7)), dma((2, 2)),
            dma((2, 2, 3)), dma((2, 2, 3)), dma((2,)), dma((2,)),
            dma((7,)), dma((7,)), dma((3, 3)), dma((3, 3)), dma((15,)), dma((15,)),
            dma((4, 15)), dma((4, 15)), dma((4, 3)), dma((4, 3)),
            dma((2, 15)), dma((2, 15)), dma((2, 3)), dma((2, 3)),
        ],
        compiler_params=pltpu.CompilerParams(
            collective_id=0, has_side_effects=True, vmem_limit_bytes=67043328
        ),
        name="exchange_all",
    )(idx, meta, g, act, kernel, image, weight)


def hand_out_kernel(ig_in, o_in, bb_in, ig_out, o_out, bb_out, ig, o, bb, sem_in, sem_out):
    pieces = [(o_in.at[k], o.at[k], o_out.at[k]) for k in range(o.shape[0])]
    pieces += [(ig_in, ig, ig_out), (bb_in, bb, bb_out)]
    into = [
        pltpu.make_async_copy(src, held, sem_in.at[k]) for k, (src, held, _) in enumerate(pieces)
    ]
    out = [
        pltpu.make_async_copy(held, dst, sem_out.at[k]) for k, (_, held, dst) in enumerate(pieces)
    ]
    for copy in into:
        copy.start()
    for first, second in zip(into, out):
        first.wait()
        second.start()
    for copy in out:
        copy.wait()


def hand_out(*arrays):
    count = arrays[1].shape[0] + 2
    return pl.pallas_call(
        hand_out_kernel,
        out_shape=[jax.ShapeDtypeStruct(a.shape, a.dtype) for a in arrays],
        in_specs=[HBM] * 3,
        out_specs=[HBM] * 3,
        scratch_shapes=[pltpu.VMEM(a.shape, a.dtype) for a in arrays]
        + [pltpu.SemaphoreType.DMA((count,))] * 2,
        name="hand_out",
    )(*arrays)


def body(grad_out, bev_act, conv_weight, img_in, backbone_weight, route, offsets, frac_x, frac_y):
    my_tile = lax.axis_index("tile")
    g, act, image = grad_out[0], bev_act[0], img_in[0]
    rows, cols, chans = g.shape
    blocks = rows * cols // BLK
    per_device = image.shape[0] // PIXB

    owners = (route[0] // per_device).reshape(TILES, blocks)
    local_ids = (route[0] % per_device).reshape(TILES, blocks)
    my_owners = lax.dynamic_index_in_dim(owners, my_tile, 0, keepdims=False)
    same = my_owners[:, None] == my_owners[None, :]
    before = lax.broadcasted_iota(jnp.int32, (blocks, blocks), 1) < lax.broadcasted_iota(
        jnp.int32, (blocks, blocks), 0
    )
    my_slots = my_owners * CAP + jnp.sum((same & before).astype(jnp.int32), axis=1)
    chosen = my_slots[None, :] == lax.broadcasted_iota(jnp.int32, (TILES * CAP, blocks), 0)
    idx = jnp.sum(
        jnp.where(chosen, lax.broadcasted_iota(jnp.int32, chosen.shape, 1), 0), axis=1
    )
    right_w = frac_x[0].astype(F32) / 256.0
    lower_w = frac_y[0].astype(F32) / 256.0
    cells = jnp.stack(
        [
            offsets[0].astype(F32),
            (1.0 - lower_w) * (1.0 - right_w),
            (1.0 - lower_w) * right_w,
            lower_w * (1.0 - right_w),
            lower_w * right_w,
        ]
    )
    cells = cells.astype(BF).reshape(5, blocks, BLK)
    info = jnp.einsum("sk,rkm->srm", chosen.astype(BF), cells, preferred_element_type=F32)
    my_local = lax.dynamic_index_in_dim(local_ids, my_tile, 0, keepdims=False)
    held = jnp.sum(jnp.where(chosen, my_local[None, :] + 1, 0), axis=1) - 1
    held = jnp.broadcast_to(held.astype(F32)[:, None, None], (TILES * CAP, 1, BLK))
    info = jnp.concatenate([info[:, :1], held, info[:, 1:]], axis=1).astype(BF)
    info = info.reshape(TILES, CAP, 6, BLK).transpose(0, 2, 1, 3).reshape(TILES, 6, CELLS)
    info = jnp.pad(info, ((0, 0), (0, 10), (0, 0)))
    by_z = info.reshape(8, 8, 16, CELLS)
    by_y = info.reshape(4, 8, 2, 16, CELLS).transpose(1, 0, 2, 3, 4).reshape(8, 8, 16, CELLS)
    meta = jnp.stack([by_z, by_y])

    weights = conv_weight.transpose(1, 2, 0, 3).reshape(9, chans, chans)
    cell_scale = 1.0 / math.sqrt(2 * TILES * rows * cols)
    pixel_scale = 1.0 / math.sqrt(2 * TILES * image.shape[0])
    image_grad, conv_sum, backbone_grad = exchange_all(
        cell_scale,
        pixel_scale,
        jnp.stack([idx // 8, idx % 8]),
        meta,
        g.reshape(rows * cols, chans),
        act.reshape(-1, 4, 16, chans),
        weights,
        image,
        backbone_weight,
    )
    image_grad, conv_sum, backbone_grad = hand_out(image_grad, conv_sum, backbone_grad)
    conv_grad = conv_sum.reshape(3, 3, chans, chans).transpose(2, 0, 1, 3)
    return (image_grad[None], conv_grad, backbone_grad)


def solution(mesh):
    return jax.shard_map(
        body,
        mesh=mesh,
        in_specs=(
            P("dp", "tile", None, None),
            P("dp", "tile", None, None),
            P(),
            P("dp", "tile", None),
            P(),
            P("dp", None),
            P("dp", "tile"),
            P("dp", "tile"),
            P("dp", "tile"),
        ),
        out_specs=(P("dp", "tile", None), P(), P()),
        check_vma=False,
    )
```

```python
import functools
import math

import jax
import jax.numpy as jnp
from jax import lax
from jax.experimental import pallas as pl
from jax.experimental.pallas import tpu as pltpu
from jax.sharding import PartitionSpec as P

BLK = 64
IMGW = 64
PIXB = 2 * IMGW
TILES = 64
CAP = 2
MESH = pl.DeviceIdType.MESH
ANY = pl.BlockSpec(memory_space=pl.ANY)
VMEM = pl.BlockSpec(memory_space=pltpu.VMEM)
SMEM = pl.BlockSpec(memory_space=pltpu.SMEM)
HBM = pl.BlockSpec(memory_space=pltpu.HBM)
BF = jnp.bfloat16
F32 = jnp.float32


def coords():
    t = lax.axis_index("tile")
    return t // 16, (t // 8) % 2 * 2 + lax.axis_index("dp"), (t // 2) % 4, t % 2


def device(y, x, z, core):
    return (x % 2, ((y * 2 + x // 2) * 4 + z) * 2 + core)


def along(axis, step):
    y, x, z, core = coords()
    if axis == "y":
        y = (y + step) % 4
    elif axis == "x":
        x = (x + step) % 4
    elif axis == "z":
        z = (z + step) % 4
    else:
        core = 1 - core
    return device(y, x, z, core)


NPIX = 4 * PIXB
CELLS = CAP * BLK
GROUP = 8


def silu_slope(value):
    sigma = jax.nn.sigmoid(value)
    return sigma * (1.0 + value * (1.0 - sigma))


def exchange_kernel(
    cell_scale, pixel_scale,
    idx_ref, m_ref, g_ref, a_ref, cw_ref, img_ref, bw_ref,
    ig_ref, o_ref, bb_ref,
    land, meta, band, dense, slots1, land2, sums, land3, w_ref, recv0, recv1, acc1, recv2,
    edges, shift, slope, img_t, bb0, bb1, bb1_acc, bb2,
    in_sem, e_send, e_recv, m_send, m_recv, p1_send, p1_recv, own_sem, p2_send, p2_recv, p3_send, p3_recv,
    pair_send, pair_recv, x_send, x_recv, yz_send, yz_recv, ag_send, ag_recv, far_send, far_recv,
    by_send, by_recv, bx_send, bx_recv,
):
    y, x, z, core = coords()
    x_hi = x // 2
    taps, chans = w_ref.shape[0], w_ref.shape[3]
    cols = edges.shape[1]
    rows = g_ref.shape[0] // cols
    half = chans // 2
    dp, tile = lax.axis_index("dp"), lax.axis_index("tile")

    def remote(src, dst, sends, recvs, where):
        return pltpu.make_async_remote_copy(
            src_ref=src, dst_ref=dst, send_sem=sends, recv_sem=recvs,
            device_id=where, device_id_type=MESH,
        )

    plane = [(p, q) for p in range(4) for q in range(4) if p or q]
    corner = [(p, q) for p, q in plane if p and q]

    def at(dy, dz, dc, dx=0):
        return device((y + dy) % 4, (x + dx) % 4, (z + dz) % 4, (core + dc) % 2)

    barrier = pltpu.get_barrier_semaphore()
    greeted = [at(0, 0, 1)] + [at(dy, dz, 0) for dy, dz in plane]
    greeted += [at(dy, dz, 1) for dy, dz in plane if not (dy and dz)]
    greeted += [at(0, 0, 0, d) for d in (1, 2, 3)]
    greeted += [at(p, 0, 0, q) for p, q in corner] + [at(0, p, 0, q) for p, q in corner]
    below, above = (dp, (tile + TILES - 1) % TILES), (dp, (tile + 1) % TILES)
    has_below, has_above = tile > 0, tile < TILES - 1
    greeted += [below, above]
    for where in greeted:
        pl.semaphore_signal(barrier, inc=1, device_id=where, device_id_type=MESH)

    def unit(n):
        return n // 2, pl.ds(pl.multiple_of(n % 2 * 512, 512), 512)

    def moved(j, r, n):
        b = j * 5 * (rows + 2) + r * 5 + n
        slot, lanes = unit(b // 4)
        return slot, pl.ds(pl.multiple_of(b % 4 * 128, 128), 128), lanes

    first_weight = 23

    loads = []
    for k in range(taps):
        slot, lanes = unit(first_weight + k)
        loads.append(pltpu.make_async_copy(cw_ref.at[k], band.at[slot, :, lanes], in_sem.at[k]))
    loads += [
        pltpu.make_async_copy(
            a_ref.at[pl.ds(4 * u, 4)], o_ref.at[u // 2, u % 2], in_sem.at[taps + u]
        )
        for u in range(10)
    ]

    def load_gradient(b, carry):
        pltpu.make_async_copy(
            g_ref.at[pl.ds(pl.multiple_of(b * 128, 128), 128)],
            band.at[moved(1, 1 + b // 5, b % 5)], in_sem.at[19],
        ).start()
        return carry

    lax.fori_loop(0, 5 * rows, load_gradient, 0)
    for copy in loads:
        copy.start()

    pl.semaphore_wait(barrier, len(greeted))

    def edge_gradient(up, where):
        side = 0 if up else 1
        row = pl.ds((rows - 1) * cols if up else 0, cols)
        return [
            remote(g_ref.at[row], edges.at[side], e_send.at[side, 0], e_recv.at[side, 0], where)
        ]

    def edge_features(up, where):
        side = 0 if up else 1
        copies = []
        for u in range(3):
            size = 4 if u < 2 else 2
            copies.append(
                remote(
                    a_ref.at[pl.ds((10 * (rows - 1) if up else 0) + 4 * u, size)],
                    o_ref.at[5 + 2 * side + u // 2, u % 2, pl.ds(0, size)],
                    e_send.at[side, 1 + u], e_recv.at[side, 1 + u], where,
                )
            )
        return copies

    for edge_copies in (edge_gradient, edge_features):

        @pl.when(has_above)
        def _():
            for copy in edge_copies(True, above):
                copy.start()

        @pl.when(has_below)
        def _():
            for copy in edge_copies(False, below):
                copy.start()

    edge = jnp.zeros((8, half), F32)
    shift[pl.ds(0, 8), :] = edge
    shift[pl.ds(cols + 8, 8), :] = edge

    def move(r, carry):
        for part in (slice(0, half), slice(half, chans)):

            def block(j, n):
                slot, places, lanes = moved(j, r, n)
                start = pl.multiple_of(lanes.start + part.start, half)
                return slot, places, pl.ds(start, half)

            for n in range(5):
                shift[pl.ds(8 + n * 128, 128), :] = band[block(1, n)].astype(F32)
            for n in range(5):
                band[block(0, n)] = shift[pl.ds(9 + n * 128, 128), :].astype(BF)
                band[block(2, n)] = shift[pl.ds(7 + n * 128, 128), :].astype(BF)
        return carry

    pltpu.make_async_copy(g_ref, g_ref, in_sem.at[19]).wait()
    lax.fori_loop(1, rows + 1, move, 0)

    def arrive(side, edge_copies, clear):
        up, present = side == 0, has_below if side == 0 else has_above

        @pl.when(present)
        def _():
            for copy in edge_copies(up, below if up else above):
                copy.wait_recv()

        @pl.when(jnp.logical_not(present))
        def _():
            clear()

    def arrive_gradient():
        for side in range(2):

            def clear():
                edges[side] = jnp.zeros((cols, chans), BF)

            arrive(side, edge_gradient, clear)
            r = 0 if side == 0 else rows + 1
            for n in range(5):
                band[moved(1, r, n)] = edges[side, pl.ds(n * 128, 128), :]
            move(r, 0)

    def arrive_features():
        for side in range(2):

            def clear():
                nothing = jnp.zeros((4, 16, chans), BF)
                for u in range(10):
                    o_ref[5 + 2 * side + u // 8, u // 4 % 2, u % 4] = nothing

            arrive(side, edge_features, clear)

    for copy in loads:
        copy.wait()

    def ground(s, carry):
        r, n = (s // 2 + 1) % 3 + s // 6 * 2, s % 2

        @pl.when(s == 4)
        def _():
            arrive_gradient()

        out = None
        for i in range(3):
            left, right = [], []
            for j in range(3):
                left.append(
                    jnp.concatenate([band[moved(j, r + 2 - i, m)] for m in range(5)], axis=0)
                )
                slot, lanes = unit(first_weight + 3 * i + j)
                right.append(band[slot, pl.ds(pl.multiple_of(n * half, half), half), lanes])
            term = lax.dot_general(
                jnp.concatenate(left, axis=1), jnp.concatenate(right, axis=1),
                (((1,), (1,)), ((), ())), preferred_element_type=F32,
            )
            out = term if out is None else out + term
        out = out.astype(BF)
        lanes = pl.ds(pl.multiple_of(n * half, half), half)
        for m in range(10):
            k = r * 10 + m
            w_ref[k // 8, k % 8, :, lanes] = out[m * BLK : (m + 1) * BLK]
        return carry

    lax.fori_loop(0, 2 * rows, ground, 0)

    def fill(s, carry):
        o = s // CAP
        place = pl.ds(pl.multiple_of(s % CAP * BLK, BLK), BLK)
        block = w_ref[idx_ref[0, s], idx_ref[1, s]]
        dense[o // 8, o % 8, place, :] = block[:, :half]
        slots1[o // 16, o // 2 % 8, o % 2, place, :] = block[:, half:]
        return carry

    lax.fori_loop(0, TILES * CAP, fill, 0)

    line = (z, y)
    here = [line[h] * 2 + core for h in range(2)]

    def slots_of(h, member):
        if h == 0:
            return dense.at[:, member]
        return slots1.at[member // 2, :, member % 2]

    def info_of(h, member):
        return m_ref.at[h, :, member]

    steps = [(d, dc) for d in range(4) for dc in range(2) if d or dc]

    def group_copy(h, k, sign, which):
        d, dc = steps[k]
        member = (line[h] + (d if sign > 0 else 4 - d)) % 4 * 2 + (core + dc) % 2
        where = at(0, d, dc) if h == 0 else at(d, 0, dc)
        place = here[h] if sign > 0 else member
        if which == "meta":
            return remote(
                info_of(h, member), meta.at[h, place], m_send.at[h, k], m_recv.at[h, k], where
            )
        return remote(
            slots_of(h, member), land.at[h, place], p1_send.at[h, k], p1_recv.at[h, k], where
        )

    own = [
        pltpu.make_async_copy(src, dst.at[h, here[h]], own_sem.at[h, k])
        for h in range(2)
        for k, (src, dst) in enumerate(
            ((info_of(h, here[h]), meta), (slots_of(h, here[h]), land))
        )
    ]
    for copy in own:
        copy.start()
    for which in ("meta", "slots"):
        for k in range(7):
            for h in range(2):
                group_copy(h, k, 1, which).start()

    def column(u):
        n = first_weight + u // 4
        return n // 2, pl.ds(pl.multiple_of(n % 2 * 512 + u % 4 * 128, 128), 128)

    def turn(u, piece, start):
        block = o_ref[piece, start // 256, pl.ds(start // 64 % 4, 2)].reshape(128, chans)
        slot, lanes = column(u)
        band[slot, :, lanes] = block.T

    def turn_inner(n, carry):
        turn(5 + n, n // 4, n % 4 * 128)
        return carry

    lax.fori_loop(0, 5 * rows, turn_inner, 0)
    arrive_features()
    for side in range(2):
        for n in range(5):
            turn(5 * (rows + 1) * side + n, 5 + 2 * side + n // 4, n % 4 * 128)

    def tap(n, carry):
        i, j = n // 3, n % 3
        left = []
        for m in range(5 * rows):
            slot, lanes = column(5 * i + m)
            left.append(band[slot, :, lanes])
        right = [band[moved(j, 1 + m // 5, m % 5)] for m in range(5 * rows)]
        w_ref[n] = jnp.dot(
            jnp.concatenate(left, axis=1), jnp.concatenate(right, axis=0),
            preferred_element_type=F32,
        ).astype(BF).reshape(w_ref.shape[1:])
        return carry

    mine, other = pl.ds(core * 4, 4), pl.ds((1 - core) * 4, 4)

    def pair(k):
        t = pl.ds(3 * k, 3)
        return remote(
            w_ref.at[t, other], recv0.at[t], pair_send.at[4 + k], pair_recv.at[4 + k], at(0, 0, 1)
        )

    def along_x(k, d):
        t = pl.ds(3 * k, 3)
        return remote(
            w_ref.at[t, core * 4 + (x + d) % 4], recv1.at[d - 1, t],
            x_send.at[k, d - 1], x_recv.at[k, d - 1], at(0, 0, 0, d),
        )

    def add0(k, carry):
        w_ref[k, mine] = (w_ref[k, mine].astype(F32) + recv0[k].astype(F32)).astype(BF)
        return carry

    def pass_on(k):
        pair(k).wait()
        lax.fori_loop(3 * k, 3 * k + 3, add0, 0)
        for d in (1, 2, 3):
            along_x(k, d).start()

    for k in range(3):
        lax.fori_loop(3 * k, 3 * k + 3, tap, 0)
        pair(k).start()
        if k > 0:
            pass_on(k - 1)

    image = img_ref[...]
    slope[...] = silu_slope(jnp.dot(image, bw_ref[...], preferred_element_type=F32))
    img_t[...] = image.T
    pass_on(2)

    for k in range(7):
        for h in range(2):
            group_copy(h, k, 1, "meta").wait_send()
            group_copy(h, k, -1, "meta").wait_recv()
    own[0].wait()
    own[2].wait()

    def make_band(n, carry):
        h, owner, member = n // 64, n // 8 % 8, n % 8
        info = meta[h, member, owner].astype(F32)
        q = lax.broadcasted_iota(jnp.int32, (IMGW, CELLS), 0).astype(F32)
        left, right = q == info[0:1], q == info[0:1] + 1.0
        zero = jnp.zeros((IMGW, CELLS), F32)
        upper = jnp.where(left, info[2:3], jnp.where(right, info[3:4], zero))
        lower = jnp.where(left, info[4:5], jnp.where(right, info[5:6], zero))
        whole = jnp.concatenate([upper, lower], axis=0)
        lanes = pl.ds(pl.multiple_of(member * CELLS, CELLS), CELLS)
        for block in range(4):
            kept = jnp.where(info[1:2] == float(block), whole, 0.0)
            band[h * 8 + owner, pl.ds(block * PIXB, PIXB), lanes] = kept.astype(BF)
        return carry

    lax.fori_loop(0, 128, make_band, 0)

    for k in range(3):
        for d in (1, 2, 3):
            along_x(k, d).wait()

    def add1(k, carry):
        total = w_ref[k, core * 4 + x].astype(F32)
        for d in range(3):
            total = total + recv1[d, k].astype(F32)
        acc1[k] = total.astype(BF)
        return carry

    lax.fori_loop(0, taps, add1, 0)

    def lanes128(q):
        return pl.ds(pl.multiple_of(q * 128, 128), 128)

    def rows16(q):
        return pl.ds(pl.multiple_of(q * 16, 16), 16)

    to_plane = [
        remote(
            acc1.at[:, rows16((y + dy) % 4), lanes128((z + dz) % 4)], recv2.at[k],
            yz_send.at[k], yz_recv.at[k], at(dy, dz, 0),
        )
        for k, (dy, dz) in enumerate(plane)
    ]
    for copy in to_plane:
        copy.start()
    for k in range(7):
        for h in range(2):
            group_copy(h, k, 1, "slots").wait_send()
            group_copy(h, k, -1, "slots").wait_recv()
    own[1].wait()
    own[3].wait()

    def owner_of(h, x_part, d):
        q = (y + h * (z - y) + d) % 4
        return (1 - h) * (q * 2 + x_part) + h * (x_part * 4 + q)

    def owner_part(h, x_part, d):
        owner = owner_of(h, x_part, d)
        return h * 4 + owner // 2, pl.ds(owner % 2 * 4, 4)

    def second(h, x_part, d):
        far = (x_part + x_hi) % 2
        return remote(
            dense.at[owner_part(h, x_part, d)], land2.at[h, far, d - 1],
            p2_send.at[h, far, d - 1], p2_recv.at[h, far, d - 1],
            at((1 - h) * d, h * d, 0),
        )

    def form(x_part):
        def one(n, carry):
            h, d = n % 2, n // 2 + 1
            owner = owner_of(h, x_part, d)
            cells = land[h, :, owner].reshape(GROUP * CELLS, half)
            dense[owner_part(h, x_part, d)] = (
                jnp.dot(band[h * 8 + owner], cells, preferred_element_type=F32)
                .astype(BF)
                .reshape(4, PIXB, half)
            )

            @pl.when(d < 4)
            def _():
                second(h, x_part, d).start()

            return carry

        lax.fori_loop(0, 8, one, 0)

    form(1 - x_hi)

    for copy in to_plane:
        copy.wait()

    def add2(k, carry):
        total = acc1[k, rows16(y), lanes128(z)].astype(F32)
        for p in range(15):
            total = total + recv2[p, k].astype(F32)
        o_ref[k, core, x, y, :, lanes128(z)] = (total * cell_scale).astype(BF)
        return carry

    lax.fori_loop(0, taps, add2, 0)

    sets = (("x", 0, 3), ("y", 3, 2), ("z", 5, 2), ("x", 7, 2))

    def spread(s, k, sign):
        axis, first, count = sets[s]
        p, q = plane[k]
        dy, dx, dz = {"x": (p, 0, q), "y": (0, p, q), "z": (p, q, 0)}[axis]
        part = o_ref.at[
            pl.ds(first, count), core, (x + sign * dx + 4) % 4, (y + sign * dy + 4) % 4, :,
            lanes128((z + sign * dz + 4) % 4),
        ]
        return remote(part, part, ag_send.at[s, k], ag_recv.at[s, k], at(dy, dz, 0, dx))

    def strip(s, d, sign):
        axis, first, count = sets[s]
        t = pl.ds(first, count)
        if axis == "x":
            part, where = o_ref.at[t, core, (x + sign * d + 4) % 4], at(0, 0, 0, d)
        elif axis == "y":
            part, where = o_ref.at[t, core, :, (y + sign * d + 4) % 4], at(d, 0, 0)
        else:
            part = o_ref.at[t, core, :, :, :, lanes128((z + sign * d + 4) % 4)]
            where = at(0, d, 0)
        return remote(part, part, far_send.at[s, d - 1], far_recv.at[s, d - 1], where)

    def strips(s):
        for d in (1, 2, 3):
            strip(s, d, 0).start()

    for k in range(15):
        for s in range(4):
            spread(s, k, 0).start()

    form(x_hi)

    def settle(far):
        for h in range(2):
            for d in (1, 2, 3):
                second(h, (far + x_hi) % 2, d).wait()

    def gathered(h, x_part, far):
        total = dense[owner_part(h, x_part, 0)].astype(F32)
        for d in range(3):
            total = total + land2[h, far, d].astype(F32)
        return total.reshape(NPIX, half)

    settle(1)
    third = []
    for h in range(2):
        sums[h] = gathered(h, 1 - x_hi, 1).astype(BF)
        third.append(
            remote(sums.at[h], land3.at[h], p3_send.at[h], p3_recv.at[h], at(0, 0, 0, 2))
        )
        third[h].start()

    for k in range(15):
        for s in range(4):
            spread(s, k, 0).wait_send()
            spread(s, k, -1).wait_recv()
    strips(0)
    strips(3)
    settle(0)

    scaled = []
    for h in range(2):
        third[h].wait()
        feature = gathered(h, x_hi, 0) + land3[h].astype(F32)
        scaled.append((feature * slope[:, h * half : (h + 1) * half]).astype(BF))
    scaled = jnp.concatenate(scaled, axis=1)
    part = jnp.dot(img_t[...], scaled, preferred_element_type=F32).astype(BF)
    w_ref[0] = part.reshape(w_ref.shape[1:])
    bb_pair = remote(w_ref.at[0, other], bb0, pair_send.at[1], pair_recv.at[1], at(0, 0, 1))
    bb_pair.start()
    image_grad = lax.dot_general(
        scaled, bw_ref[...], (((1,), (1,)), ((), ())), preferred_element_type=F32
    )
    ig_ref[...] = image_grad.astype(BF)
    bb_pair.wait()
    w_ref[1, pl.ds(0, 4)] = (w_ref[0, mine].astype(F32) + bb0[...].astype(F32)).astype(BF)

    def place(dy, dz):
        return (y + dy + 4) % 4 * 4 + (z + dz + 4) % 4

    bb_plane = [
        remote(
            w_ref.at[1, place(dy, dz) // 4, rows16(place(dy, dz) % 4)], bb1.at[k],
            by_send.at[0, k], by_recv.at[0, k], at(dy, dz, 0),
        )
        for k, (dy, dz) in enumerate(plane)
    ]
    for copy in bb_plane:
        copy.start()
    for copy in bb_plane:
        copy.wait()
    total = w_ref[1, y, rows16(z), :].astype(F32)
    for k in range(15):
        total = total + bb1[k].astype(F32)
    bb1_acc[...] = total.astype(BF)
    bb_line = [
        remote(
            bb1_acc.at[:, lanes128((x + d) % 4)], bb2.at[d - 1],
            bx_send.at[0, d - 1], bx_recv.at[0, d - 1], at(0, 0, 0, d),
        )
        for d in (1, 2, 3)
    ]
    for copy in bb_line:
        copy.start()
    strips(1)
    strips(2)

    def back(c):
        return remote(
            o_ref.at[:, c], o_ref.at[:, c], pair_send.at[2], pair_recv.at[2], at(0, 0, 1)
        )

    for copy in bb_line:
        copy.wait()
    total = bb1_acc[:, lanes128(x)].astype(F32)
    for d in range(3):
        total = total + bb2[d].astype(F32)

    def bb_rows(dy, dz):
        return pl.ds(pl.multiple_of(core * half + place(dy, dz) * 16, 16), 16)

    bb_ref[bb_rows(0, 0), lanes128(x)] = (total * pixel_scale).astype(BF)

    def bb_strip(d, sign):
        part = bb_ref.at[bb_rows(0, 0), lanes128((x + sign * d + 4) % 4)]
        return remote(part, part, bx_send.at[1, d - 1], bx_recv.at[1, d - 1], at(0, 0, 0, d))

    def bb_spread(k, sign):
        dy, dz = plane[k]
        part = bb_ref.at[bb_rows(sign * dy, sign * dz)]
        return remote(part, part, by_send.at[1, k], by_recv.at[1, k], at(dy, dz, 0))

    def bb_half(c):
        return pl.ds(pl.multiple_of(c * half, half), half)

    def bb_back(which):
        part = bb_ref.at[which]
        return remote(part, part, pair_send.at[3], pair_recv.at[3], at(0, 0, 1))

    for d in (1, 2, 3):
        bb_strip(d, 0).start()

    for s in (0, 3, 1, 2):
        for d in (1, 2, 3):
            strip(s, d, 0).wait_send()
            strip(s, d, -1).wait_recv()
    back(core).start()
    for d in (1, 2, 3):
        bb_strip(d, 0).wait_send()
        bb_strip(d, -1).wait_recv()
    for k in range(15):
        bb_spread(k, 0).start()
    for k in range(15):
        bb_spread(k, 0).wait_send()
        bb_spread(k, -1).wait_recv()
    bb_back(bb_half(core)).start()
    back(core).wait_send()
    back(1 - core).wait_recv()
    bb_back(bb_half(core)).wait_send()
    bb_back(bb_half(1 - core)).wait_recv()

    @pl.when(has_above)
    def _():
        for copy in edge_gradient(True, above) + edge_features(True, above):
            copy.wait_send()

    @pl.when(has_below)
    def _():
        for copy in edge_gradient(False, below) + edge_features(False, below):
            copy.wait_send()


def exchange_all(cell_scale, pixel_scale, idx, meta, g, act, kernel, image, weight):
    chans = image.shape[1]
    half = chans // 2
    taps = kernel.shape[0]
    cols = 640
    dma = pltpu.SemaphoreType.DMA
    vmem = pltpu.VMEM
    pixels = image.shape[0]
    return pl.pallas_call(
        functools.partial(exchange_kernel, cell_scale, pixel_scale),
        out_shape=[
            jax.ShapeDtypeStruct((pixels, chans), BF),
            jax.ShapeDtypeStruct((taps, 2, 4, 4, 16, chans), BF),
            jax.ShapeDtypeStruct((chans, chans), BF),
        ],
        in_specs=[SMEM] + [HBM] * 4 + [VMEM, VMEM],
        out_specs=[VMEM, VMEM, VMEM],
        scratch_shapes=[
            vmem((2, GROUP, GROUP, CELLS, half), BF),
            vmem((2, GROUP, GROUP, 16, CELLS), BF),
            vmem((2 * GROUP, NPIX, GROUP * CELLS), BF),
            vmem((8, 8, CELLS, half), BF),
            vmem((4, 8, 2, CELLS, half), BF),
            vmem((2, 2, 3, 4, PIXB, half), BF),
            vmem((2, NPIX, half), BF),
            vmem((2, NPIX, half), BF),
            vmem((taps, 8, BLK, chans), BF),
            vmem((taps, 4, BLK, chans), BF),
            vmem((3, taps, 64, chans), BF),
            vmem((taps, 64, chans), BF),
            vmem((15, taps, 16, 128), BF),
            vmem((2, cols, chans), BF),
            vmem((cols + 16, half), F32),
            vmem((pixels, chans), F32),
            vmem((chans, pixels), BF),
            vmem((4, BLK, chans), BF),
            vmem((15, 16, chans), BF),
            vmem((16, chans), BF),
            vmem((3, 16, 128), BF),
            dma((20,)), dma((2, 4)), dma((2, 4)),
            dma((2, 7)), dma((2, 7)), dma((2, 7)), dma((2, 7)), dma((2, 2)),
            dma((2, 2, 3)), dma((2, 2, 3)), dma((2,)), dma((2,)),
            dma((7,)), dma((7,)), dma((3, 3)), dma((3, 3)), dma((15,)), dma((15,)),
            dma((4, 15)), dma((4, 15)), dma((4, 3)), dma((4, 3)),
            dma((2, 15)), dma((2, 15)), dma((2, 3)), dma((2, 3)),
        ],
        compiler_params=pltpu.CompilerParams(
            collective_id=0, has_side_effects=True, vmem_limit_bytes=67043328
        ),
        name="exchange_all",
    )(idx, meta, g, act, kernel, image, weight)


def hand_out_kernel(ig_in, o_in, bb_in, ig_out, o_out, bb_out, ig, o, bb, sem_in, sem_out):
    pieces = [(ig_in, ig, ig_out), (bb_in, bb, bb_out)]
    pieces += [(o_in.at[k], o.at[k], o_out.at[k]) for k in range(o.shape[0])]
    into = [
        pltpu.make_async_copy(src, held, sem_in.at[k]) for k, (src, held, _) in enumerate(pieces)
    ]
    out = [
        pltpu.make_async_copy(held, dst, sem_out.at[k]) for k, (_, held, dst) in enumerate(pieces)
    ]
    for copy in into:
        copy.start()
    for first, second in zip(into, out):
        first.wait()
        second.start()
    for copy in out:
        copy.wait()


def hand_out(*arrays):
    count = arrays[1].shape[0] + 2
    return pl.pallas_call(
        hand_out_kernel,
        out_shape=[jax.ShapeDtypeStruct(a.shape, a.dtype) for a in arrays],
        in_specs=[HBM] * 3,
        out_specs=[HBM] * 3,
        scratch_shapes=[pltpu.VMEM(a.shape, a.dtype) for a in arrays]
        + [pltpu.SemaphoreType.DMA((count,))] * 2,
        name="hand_out",
    )(*arrays)


def body(grad_out, bev_act, conv_weight, img_in, backbone_weight, route, offsets, frac_x, frac_y):
    my_tile = lax.axis_index("tile")
    g, act, image = grad_out[0], bev_act[0], img_in[0]
    rows, cols, chans = g.shape
    blocks = rows * cols // BLK
    per_device = image.shape[0] // PIXB

    owners = (route[0] // per_device).reshape(TILES, blocks)
    local_ids = (route[0] % per_device).reshape(TILES, blocks)
    my_owners = lax.dynamic_index_in_dim(owners, my_tile, 0, keepdims=False)
    same = my_owners[:, None] == my_owners[None, :]
    before = lax.broadcasted_iota(jnp.int32, (blocks, blocks), 1) < lax.broadcasted_iota(
        jnp.int32, (blocks, blocks), 0
    )
    my_slots = my_owners * CAP + jnp.sum((same & before).astype(jnp.int32), axis=1)
    chosen = my_slots[None, :] == lax.broadcasted_iota(jnp.int32, (TILES * CAP, blocks), 0)
    idx = jnp.sum(
        jnp.where(chosen, lax.broadcasted_iota(jnp.int32, chosen.shape, 1), 0), axis=1
    )
    right_w = frac_x[0].astype(F32) / 256.0
    lower_w = frac_y[0].astype(F32) / 256.0
    cells = jnp.stack(
        [
            offsets[0].astype(F32),
            (1.0 - lower_w) * (1.0 - right_w),
            (1.0 - lower_w) * right_w,
            lower_w * (1.0 - right_w),
            lower_w * right_w,
        ]
    )
    cells = cells.astype(BF).reshape(5, blocks, BLK)
    info = jnp.einsum("sk,rkm->srm", chosen.astype(BF), cells, preferred_element_type=F32)
    my_local = lax.dynamic_index_in_dim(local_ids, my_tile, 0, keepdims=False)
    held = jnp.sum(jnp.where(chosen, my_local[None, :] + 1, 0), axis=1) - 1
    held = jnp.broadcast_to(held.astype(F32)[:, None, None], (TILES * CAP, 1, BLK))
    info = jnp.concatenate([info[:, :1], held, info[:, 1:]], axis=1).astype(BF)
    info = info.reshape(TILES, CAP, 6, BLK).transpose(0, 2, 1, 3).reshape(TILES, 6, CELLS)
    info = jnp.pad(info, ((0, 0), (0, 10), (0, 0)))
    by_z = info.reshape(8, 8, 16, CELLS)
    by_y = info.reshape(4, 8, 2, 16, CELLS).transpose(1, 0, 2, 3, 4).reshape(8, 8, 16, CELLS)
    meta = jnp.stack([by_z, by_y])

    weights = conv_weight.transpose(1, 2, 0, 3).reshape(9, chans, chans)
    cell_scale = 1.0 / math.sqrt(2 * TILES * rows * cols)
    pixel_scale = 1.0 / math.sqrt(2 * TILES * image.shape[0])
    image_grad, conv_sum, backbone_grad = exchange_all(
        cell_scale,
        pixel_scale,
        jnp.stack([idx // 8, idx % 8]),
        meta,
        g.reshape(rows * cols, chans),
        act.reshape(-1, 4, 16, chans),
        weights,
        image,
        backbone_weight,
    )
    image_grad, conv_sum, backbone_grad = hand_out(image_grad, conv_sum, backbone_grad)
    conv_grad = conv_sum.reshape(3, 3, chans, chans).transpose(2, 0, 1, 3)
    return (image_grad[None], conv_grad, backbone_grad)


def solution(mesh):
    return jax.shard_map(
        body,
        mesh=mesh,
        in_specs=(
            P("dp", "tile", None, None),
            P("dp", "tile", None, None),
            P(),
            P("dp", "tile", None),
            P(),
            P("dp", None),
            P("dp", "tile"),
            P("dp", "tile"),
            P("dp", "tile"),
        ),
        out_specs=(P("dp", "tile", None), P(), P()),
        check_vma=False,
    )
```
